32 devices in a mesh: fsdp: 8 (over y, x, core), seq: 4 (over z).
Axes of the slice: x: 2, y: 2, z: 4, core: 2. Of those that a mesh axis runs over, the one named last changes fastest.
Arguments:
- latents_in: bfloat16 [2, 8, 128, 768], P(None, 'fsdp'), may hold values from -6 to 6
- inputs: bfloat16 [2, 8, 6312, 768], P(None, 'fsdp', 'seq'), may hold values from -6 to 6
- clip_frames: int32 [2, 8], P(None, 'fsdp'), may hold values from 4 to 16
- text_mask: int32 [2, 8, 40], P(None, 'fsdp'), may hold values 0 or 1
- qkv_weight: bfloat16 [2, 3, 768, 768], P(None, None, 'fsdp'), may hold values from -0.21875 to 0.21875
- out_weight: bfloat16 [2, 768, 768], P(None, 'fsdp'), may hold values from -1.75 to 1.75
- mlp_in: bfloat16 [2, 768, 3072], P(None, 'fsdp'), may hold values from -0.21875 to 0.21875
- mlp_out: bfloat16 [2, 3072, 768], P(None, 'fsdp'), may hold values from -0.109375 to 0.109375
- norm_gain: bfloat16 [5, 768], P(None, 'fsdp'), may hold values from 0.5 to 1.5
- norm_bias: bfloat16 [5, 768], P(None, 'fsdp'), may hold values from -2.5 to 2.5
- bias_in: bfloat16 [2, 3072], P(None, 'fsdp'), may hold values from -2.5 to 2.5
- bias_out: bfloat16 [2, 768], P(None, 'fsdp'), may hold values from -2.5 to 2.5
- out_cotangent: bfloat16 [2, 8, 128, 768], P(None, 'fsdp'), may hold values from -6 to 6
Outputs:
- latents_out: float32 [2, 8, 128, 768], P(None, 'fsdp')
- latents_grad: float32 [2, 8, 128, 768], P(None, 'fsdp')
- inputs_grad: float32 [2, 8, 6312, 768], P(None, 'fsdp', 'seq')
- qkv_grad: float32 [2, 3, 768, 768], P(None, None, 'fsdp')
- out_weight_grad: float32 [2, 768, 768], P(None, 'fsdp')
- mlp_in_grad: float32 [2, 768, 3072], P(None, 'fsdp')
- mlp_out_grad: float32 [2, 3072, 768], P(None, 'fsdp')
- norm_gain_grad: float32 [5, 768], P(None, 'fsdp')
- norm_bias_grad: float32 [5, 768], P(None, 'fsdp')
- bias_in_grad: float32 [2, 3072], P(None, 'fsdp')
- bias_out_grad: float32 [2, 768], P(None, 'fsdp')
The draws below stay inside these ranges and needn't reach their ends.
Inputs may be any that keep to these rules, and one draw needn't show every extreme that they name: `clip_frames`: frames of each clip; its first 392 times that many patch slots hold tokens, the rest of its 16 frame slots are padding.
All inputs are finite; a program needn't handle non-finite values. No bound on the sum of `text_mask` on one device may be relied on, other than what follows from the above.
Results may differ from the reference program's by a relative error of at most 0.015.
Values may be sent and summed in bfloat16 or wider, within the bound.
No kernel may reach another device: no remote copies, remote signals or barrier semaphores. Data moves between devices by JAX's collectives and lax.ppermute only.
A program may use at most 320 MiB of HBM per device.

```python
import jax
import jax.numpy as jnp
from jax import lax

D = 768
HEADS = 12
HEAD = 64
FF = 3072
NLAT = 128
PATCHES = 392
TEXT = 40
FRAMES = 16
MB = 2
SEQLEN = 6312
CLIPS = 8


def touch_ends(values, key, low, high):
    index_at = [jax.random.randint(jax.random.fold_in(key, axis), (), 0, length) for axis, length in enumerate(values.shape)]
    widest = values.shape.index(max(values.shape))
    neighbour = index_at[:widest] + [(index_at[widest] + 1) % values.shape[widest]] + index_at[widest + 1:]
    return values.at[tuple(index_at)].set(low).at[tuple(neighbour)].set(high)


def steps_of(key, extent, split, least, largest):
    gain, own = 1.0, jax.random.fold_in(key, 6)
    for axis_at, parts in split:
        heights = jnp.exp(jax.random.uniform(jax.random.fold_in(own, axis_at), (parts,), jnp.float32, least / len(split), largest / len(split)))
        gain = gain * jnp.repeat(heights, extent[axis_at] // parts).reshape([-1 if axis == axis_at else 1 for axis in range(len(extent))])
    return gain


def centred(rng, extent, scale, most, pieces=(), held_as=jnp.bfloat16):
    entries = scale * jax.random.normal(rng, extent, jnp.float32)
    if pieces:
        entries = entries * steps_of(rng, extent, pieces, -0.22, 0.18)
    return jnp.clip(entries, -most, most).astype(held_as)


def setup_inputs(seed: int = 0) -> dict:
    keys = jax.random.split(jax.random.key(seed), 14)
    return {
        "latents_in": centred(keys[0], (MB, CLIPS, NLAT, D), 1.0, 6.0, ((1, 8),)),
        "inputs": centred(keys[1], (MB, CLIPS, SEQLEN, D), 1.0, 6.0, ((1, 8), (2, 4))),
        "clip_frames": touch_ends(jax.random.randint(keys[2], (MB, CLIPS), 4, FRAMES + 1), jax.random.fold_in(keys[2], 1), 4, FRAMES).astype(jnp.int32),
        "text_mask": touch_ends((jax.random.randint(keys[3], (MB, CLIPS, TEXT), 0, 4) < 3).astype(jnp.int32), jax.random.fold_in(keys[3], 1), 0, 1),
        "qkv_weight": centred(keys[4], (2, 3, D, D), D ** -0.5, 0.21875, ((2, 8),)),
        "out_weight": centred(keys[5], (2, D, D), (D // 64) ** -0.5, 1.75, ((1, 8),)),
        "mlp_in": centred(keys[6], (2, D, FF), D ** -0.5, 0.21875, ((1, 8),)),
        "mlp_out": centred(keys[7], (2, FF, D), FF ** -0.5, 0.109375, ((1, 8),)),
        "norm_gain": jnp.clip(1.0 + 0.1 * jax.random.normal(keys[8], (5, D), jnp.float32), 0.5, 1.5).astype(jnp.bfloat16),
        "norm_bias": centred(keys[9], (5, D), 0.3, 2.5, ((1, 8),)),
        "bias_in": centred(keys[10], (2, FF), 0.3, 2.5, ((1, 8),)),
        "bias_out": centred(keys[11], (2, D), 0.3, 2.5, ((1, 8),)),
        "out_cotangent": centred(keys[12], (MB, CLIPS, NLAT, D), 1.0, 6.0, ((1, 8),)),
    }


epsilon = 1e-06

@jax.custom_vjp
def low(v):
    return lax.optimization_barrier(v.astype(jnp.bfloat16)).astype(jnp.float32)

@jax.custom_vjp
def low_back(v):
    return v

def low_keep(v):
    return (low(v), None)

def low_pass(kept, grad):
    return (grad,)

def back_keep(v):
    return (v, None)

def back_low(kept, grad):
    return (low(grad),)
low.defvjp(low_keep, low_pass)
low_back.defvjp(back_keep, back_low)

def rounded_both(values):
    return low(low_back(values))

def matmul_hi(form, left, right):
    return jnp.einsum(form, left, right, precision=lax.Precision.HIGHEST)

def layer_norm(values, scales, offsets):
    center = values - lax.optimization_barrier(jnp.mean(values, -1, keepdims=True))
    spread = lax.optimization_barrier(jnp.mean(center * center, -1, keepdims=True))
    return center * lax.rsqrt(spread + epsilon) * scales + offsets

def feed_forward(residual, up_w, down_w, up_b, down_b, scales, offsets):
    normed = low(layer_norm(residual, scales, offsets))
    hidden = low_back(matmul_hi('nd,df->nf', normed, up_w) + up_b)
    active = low(jax.nn.gelu(hidden))
    return low_back(matmul_hi('nf,fd->nd', active, down_w) + down_b)

def layer_forward(params, residual, tokens, valid_keys):
    qkv_w, out_w, up_w, down_w, scales, offsets, up_b, down_b = params
    latent_normed = low(layer_norm(residual, scales[0], offsets[0]))
    token_normed = low(layer_norm(tokens, scales[1], offsets[1]))
    queries = rounded_both(matmul_hi('nd,de->ne', latent_normed, qkv_w[0, 0])).reshape(NLAT, HEADS, HEAD)
    key_heads = rounded_both(matmul_hi('ld,de->le', token_normed, qkv_w[0, 1])).reshape(SEQLEN, HEADS, HEAD)
    value_heads = rounded_both(matmul_hi('ld,de->le', token_normed, qkv_w[0, 2])).reshape(SEQLEN, HEADS, HEAD)
    scores = low_back(matmul_hi('qhd,khd->qhk', queries, key_heads) * 0.125)
    weights_exp = jnp.where(valid_keys[None, None, :], jnp.exp(scores), 0.0)
    totals = lax.optimization_barrier(jnp.sum(weights_exp, -1))
    numerator = low_back(matmul_hi('qhk,khd->qhd', low(weights_exp), value_heads))
    attended = rounded_both(numerator / totals[..., None]).reshape(NLAT, D)
    first = residual + low_back(matmul_hi('nd,de->ne', attended, out_w[0]))
    second = first + feed_forward(first, up_w[0], down_w[0], up_b[0], down_b[0], scales[2], offsets[2])
    self_normed = low(layer_norm(second, scales[3], offsets[3]))
    heads_qkv = rounded_both(matmul_hi('nd,jde->jne', self_normed, qkv_w[1])).reshape(3, NLAT, HEADS, HEAD)
    self_scores = low_back(matmul_hi('qhd,khd->qhk', heads_qkv[0], heads_qkv[1]) * 0.125)
    row_peak = lax.optimization_barrier(jnp.max(self_scores, -1, keepdims=True))
    self_exp = jnp.exp(self_scores - row_peak)
    softmax_w = self_exp / lax.optimization_barrier(jnp.sum(self_exp, -1, keepdims=True))
    mixed_heads = rounded_both(matmul_hi('qhk,khd->qhd', low(softmax_w), heads_qkv[2])).reshape(NLAT, D)
    third = second + low_back(matmul_hi('nd,de->ne', mixed_heads, out_w[1]))
    return third + feed_forward(third, up_w[1], down_w[1], up_b[1], down_b[1], scales[4], offsets[4])

def reference(latents_in, inputs, clip_frames, text_mask, qkv_weight, out_weight, mlp_in, mlp_out, norm_gain, norm_bias, bias_in, bias_out, out_cotangent):
    params = tuple((arr.astype(jnp.float32) for arr in (qkv_weight, out_weight, mlp_in, mlp_out, norm_gain, norm_bias, bias_in, bias_out)))
    count_all = MB * CLIPS
    latent_rows = latents_in.astype(jnp.float32).reshape(count_all, NLAT, D)
    token_rows = inputs.astype(jnp.float32).reshape(count_all, SEQLEN, D)
    frame_counts = clip_frames.reshape(count_all)
    text_rows = text_mask.reshape(count_all, TEXT)
    cotangents = out_cotangent.astype(jnp.float32).reshape(count_all, NLAT, D)
    zero_grads = jax.tree.map(jnp.zeros_like, params)

    def one_clip(grad_sum, item):
        residual, tokens, frames_now, text_now, cotangent = item
        valid_keys = jnp.concatenate([jnp.arange(FRAMES * PATCHES) < frames_now * PATCHES, text_now > 0])
        result, pullback = jax.vjp(lambda weights, lat_rows, tok_rows: layer_forward(weights, lat_rows, tok_rows, valid_keys), params, residual, tokens)
        grad_params, grad_latent, grad_tokens = pullback(cotangent)
        grad_sum = jax.tree.map(lambda left, right: left + right, grad_sum, grad_params)
        return (grad_sum, (result, grad_latent, grad_tokens))
    grads, (finals, latent_grads, token_grads) = lax.scan(one_clip, zero_grads, (latent_rows, token_rows, frame_counts, text_rows, cotangents))
    return (finals.reshape(MB, CLIPS, NLAT, D), latent_grads.reshape(MB, CLIPS, NLAT, D), token_grads.reshape(MB, CLIPS, SEQLEN, D), grads[0], grads[1], grads[2], grads[3], grads[4], grads[5], grads[6], grads[7])
```

```python
import functools

import jax
import jax.numpy as jnp
from jax import lax
from jax.experimental import pallas as pl
from jax.experimental.pallas import tpu as pltpu
from jax.sharding import PartitionSpec as P

D = 768
HEADS = 12
HEAD = 64
PAIRS = HEADS // 2
FF = 3072
NLAT = 128
PATCHES = 392
FRAMES = 16
OWNERS = 8
SHARE = D // OWNERS
CHUNKS = FF // D
HALF = D // 2
PAY = D + 128
VEC_F = 16
VEC_S = 32
VEC_K = 32
ROWS_F = CHUNKS * SHARE + CHUNKS * SHARE + VEC_F
ROWS_S = 2 * CHUNKS * SHARE + 5 * SHARE + VEC_S
ROWS_K = 3 * SHARE + VEC_K
EPS = 1e-06
F32 = jnp.float32
BF = jnp.bfloat16
GELU_C = 0.7978845608028654
GELU_A = 0.044715
VMEM_CAP = 60 * 1024 * 1024


def nn(a, b):
    return lax.dot_general(a, b, (((1,), (0,)), ((), ())), preferred_element_type=F32)


def nt(a, b):
    return lax.dot_general(a, b, (((1,), (1,)), ((), ())), preferred_element_type=F32)


def tn(a, b):
    return lax.dot_general(a, b, (((0,), (0,)), ((), ())), preferred_element_type=F32)


def ln_parts(x):
    center = x - jnp.mean(x, -1, keepdims=True)
    rstd = lax.rsqrt(jnp.mean(center * center, -1, keepdims=True) + EPS)
    return center, rstd


def ln(x, gain, bias):
    center, rstd = ln_parts(x)
    return center * rstd * gain + bias


def ln_back(x, gain, grad):
    center, rstd = ln_parts(x)
    xhat = center * rstd
    dx = grad * gain
    back = rstd * (dx - jnp.mean(dx, -1, keepdims=True) - xhat * jnp.mean(dx * xhat, -1, keepdims=True))
    return back, grad * xhat


def gelu(h):
    return h * (0.5 * (1.0 + jnp.tanh(GELU_C * (h + GELU_A * h * h * h))))


def gelu_both(h):
    square = h * h
    t = jnp.tanh(GELU_C * (h + GELU_A * h * square))
    cdf = 0.5 * (1.0 + t)
    slope = cdf + 0.5 * h * (1.0 - t * t) * (GELU_C * (1.0 + 3.0 * GELU_A * square))
    return h * cdf, slope


def low_lanes(rows):
    return lax.broadcasted_iota(jnp.int32, (rows, 128), 1) < HEAD


def block_diag(pair):
    wide = pair.astype(F32)
    low = low_lanes(pair.shape[0])
    return jnp.concatenate([jnp.where(low, wide, 0.0), jnp.where(low, 0.0, wide)], 0).astype(BF)


def diag_of(both):
    rows = both.shape[0] // 2
    return jnp.where(low_lanes(rows), both[:rows], both[rows:])


class Pack:
    def __init__(self, arrays, where):
        self.arrays, self.where = arrays, where

    def start(self, refs, row, rows, place, f, sem):
        for m in range(OWNERS):
            index, lead, first = self.where(m, row)
            src = refs[index] if lead is None else refs[index].at[lead]
            pltpu.make_async_copy(src.at[pl.ds(first, rows)], place(f ^ m), sem).start()


def wait_for(ref, sem):
    pltpu.make_async_copy(ref, ref, sem).wait()


def share_rows(ref, g, first=0, span=SHARE, step=SHARE):
    return ref.at[pl.ds(pl.multiple_of(g * step + first, SHARE), span)]


def start_square(pack, refs, row, dst, f, sem):
    pack.start(refs, row, SHARE, lambda g: share_rows(dst, g), f, sem)


def start_up(pack, refs, row, dst, f, sems):
    for t in range(CHUNKS):
        lanes = pl.ds(t * D, D)
        pack.start(
            refs,
            row + t * SHARE,
            SHARE,
            lambda g, lanes=lanes: dst.at[pl.ds(pl.multiple_of(g * SHARE, SHARE), SHARE), lanes],
            f,
            sems.at[t],
        )


def start_down(pack, refs, row, dst, f, sem):
    for t in range(CHUNKS):
        pack.start(
            refs,
            row + t * SHARE,
            SHARE,
            lambda g, t=t: share_rows(dst, g, t * SHARE, SHARE, CHUNKS * SHARE),
            f,
            sem,
        )


ANY = pl.BlockSpec(memory_space=pl.ANY)
WHOLE = pl.BlockSpec(memory_space=pltpu.VMEM)


def sds(shape, dtype):
    return jax.ShapeDtypeStruct(shape, dtype)


def cost(flops, size, exps=0):
    return pl.CostEstimate(flops=int(flops), bytes_accessed=int(size), transcendentals=int(exps))


PARAMS = pltpu.CompilerParams(vmem_limit_bytes=VMEM_CAP)


def keyval_kernel(pack, local, tile, meta, x_ref, *refs):
    count = len(pack.arrays)
    wrefs, (xl_ref, k_ref, v_ref, gb_ref, bin_ref, wkv, small, sems) = refs[:count], refs[count:]
    f = meta[0]

    @pl.when((pl.program_id(0) == 0) & (pl.program_id(1) == 0))
    def _():
        for m in range(OWNERS):
            index, lead, first = pack.where(m, 2 * SHARE)
            src = wrefs[index] if lead is None else wrefs[index].at[lead]
            pltpu.make_async_copy(
                src.at[pl.ds(first, 16), pl.ds(0, 256)], small.at[m], sems.at[2]
            ).start()
        start_square(pack, wrefs, 0, wkv.at[0], f, sems.at[0])
        start_square(pack, wrefs, SHARE, wkv.at[1], f, sems.at[1])
        wait_for(small, sems.at[2])
        lane = lax.broadcasted_iota(jnp.int32, (128, D), 1)
        row = lax.broadcasted_iota(jnp.int32, (128, D), 0)
        total = jnp.zeros((16, D), F32)
        for m in range(OWNERS):
            g = f ^ m
            place = jnp.where((lane - g * SHARE == row) & (row < SHARE), 1.0, 0.0).astype(BF)
            total = total + nn(small[m, :, 0:128], place)
            wide = small[m].astype(F32)
            for u in range(6):
                i, part = u // 3, u % 3
                line = wide[12 + u : 13 + u, 0:128] if u < 4 else wide[u - 4 : u - 3, 128:256]
                at = pl.ds(pl.multiple_of((3 * g + part) * 128, 128), 128)
                bin_ref[i : i + 1, at] = line
        gb_ref[...] = total
        wait_for(wkv.at[0], sems.at[0])
        wait_for(wkv.at[1], sems.at[1])

    x = x_ref[0].astype(F32)
    normed = ln(x, gb_ref[1:2], gb_ref[6:7])
    row = pl.program_id(1) * tile + lax.broadcasted_iota(jnp.int32, (tile, D), 0)
    xl = jnp.where(row < local, normed, 0.0).astype(BF)
    xl_ref[0] = xl
    k_ref[0] = nn(xl, wkv[0]).astype(BF)
    v_ref[0] = nn(xl, wkv[1]).astype(BF)


def keyval(pack, meta, tokens, local, padded):
    clips = tokens.shape[0]
    tile = padded // 4
    block = pl.BlockSpec((1, tile, D), lambda i, j, m: (i, j, 0))
    fixed = lambda shape: pl.BlockSpec(shape, lambda i, j, m: (0,) * len(shape))
    return pl.pallas_call(
        functools.partial(keyval_kernel, pack, local, tile),
        grid_spec=pltpu.PrefetchScalarGridSpec(
            num_scalar_prefetch=1,
            grid=(clips, padded // tile),
            in_specs=[block] + [ANY] * len(pack.arrays),
            out_specs=[block, block, block, fixed((16, D)), fixed((2, FF))],
            scratch_shapes=[
                pltpu.VMEM((2, D, D), BF),
                pltpu.VMEM((OWNERS, 16, 256), BF),
                pltpu.SemaphoreType.DMA((3,)),
            ],
        ),
        out_shape=[sds((clips, padded, D), BF)] * 3 + [sds((16, D), F32), sds((2, FF), F32)],
        compiler_params=PARAMS,
        cost_estimate=cost(4 * clips * padded * D * D, clips * padded * D * 8),
        name="keyval",
    )(meta, tokens, *pack.arrays)


def spans(total, step):
    return [(at, min(step, total - at)) for at in range(0, total, step)]


def attend_kernel(pack, padded, meta, lat_ref, gb_ref, bias_ref, k_ref, v_ref, *refs):
    count = len(pack.arrays)
    wrefs, (pay_ref, q_ref, wq, qs, lv, sem) = refs[:count], refs[count:]
    f = meta[0]
    clip, pair = pl.program_id(0), pl.program_id(1)

    @pl.when((clip == 0) & (pair == 0))
    def _():
        start_square(pack, wrefs, 0, wq, f, sem.at[0])
        zl = ln(lat_ref[...].astype(F32), gb_ref[0:1], gb_ref[5:6]).astype(BF)
        wait_for(wq, sem.at[0])
        q = nn(zl, wq[...]).astype(BF).astype(F32) * 0.125
        qs[...] = q.astype(BF)
        q_ref[...] = qs[...]

    at = pl.ds(pl.multiple_of(pair * 128, 128), 128)
    rows = pl.ds(pl.multiple_of(clip * NLAT, NLAT), NLAT)
    qbd = block_diag(qs[rows, at])
    lsum = jnp.zeros((2 * NLAT, 128), F32)
    u = jnp.zeros((2 * NLAT, 128), F32)
    for first, width in spans(padded, 256):
        s = nt(qbd, k_ref[0, first : first + width, :])
        e = jnp.exp(s + bias_ref[0, :, first : first + width])
        for part in range(0, width, 128):
            lsum = lsum + e[:, part : part + 128]
        u = u + nn(e.astype(BF), v_ref[0, first : first + width, :])
    pay_ref[0, :, at] = diag_of(u).astype(BF)
    l = jnp.sum(lsum, -1, keepdims=True)
    lane = lax.broadcasted_iota(jnp.int32, (NLAT, 128), 1)
    old = jnp.where(pair == 0, 0.0, lv[...])
    new = jnp.where(lane == 2 * pair, l[:NLAT], jnp.where(lane == 2 * pair + 1, l[NLAT:], old))
    lv[...] = new

    @pl.when(pair == PAIRS - 1)
    def _():
        pay_ref[0, :, D:PAY] = split_pair(lv[...])


def split_pair(values):
    high = values.astype(BF).astype(F32)
    rest = values - high
    return jnp.where(low_lanes(values.shape[0]), high, pltpu.roll(rest, HEAD, 1)).astype(BF)


def join_pair(pay):
    wide = pay.astype(F32)
    return wide + pltpu.roll(wide, HEAD, 1)


def attend(pack, meta, lat, gb, bias, k, v):
    clips, padded = k.shape[0], k.shape[1]
    rows = lat.shape[0]
    fixed = lambda shape: pl.BlockSpec(shape, lambda i, j, m: (0,) * len(shape))
    lanes = pl.BlockSpec((1, padded, 128), lambda i, j, m: (i, 0, j))
    return pl.pallas_call(
        functools.partial(attend_kernel, pack, padded),
        grid_spec=pltpu.PrefetchScalarGridSpec(
            num_scalar_prefetch=1,
            grid=(clips, PAIRS),
            in_specs=[
                fixed((rows, D)),
                fixed((16, D)),
                pl.BlockSpec((1, 1, padded), lambda i, j, m: (i, 0, 0)),
                lanes,
                lanes,
            ]
            + [ANY] * len(pack.arrays),
            out_specs=[
                pl.BlockSpec((1, NLAT, PAY), lambda i, j, m: (i, 0, 0)),
                fixed((rows, D)),
            ],
            scratch_shapes=[
                pltpu.VMEM((D, D), BF),
                pltpu.VMEM((rows, D), BF),
                pltpu.VMEM((NLAT, 128), F32),
                pltpu.SemaphoreType.DMA((1,)),
            ],
        ),
        out_shape=[sds((clips, NLAT, PAY), BF), sds((rows, D), BF)],
        compiler_params=PARAMS,
        cost_estimate=cost(
            8 * clips * padded * NLAT * D, clips * padded * D * 4, clips * padded * NLAT * HEADS
        ),
        name="attend",
    )(meta, lat, gb, bias, k, v, *pack.arrays)


def combine_kernel(*refs):
    parts, out_ref = refs[1:-1], refs[-1]
    total = parts[0][...].astype(F32)
    for part in parts[1:]:
        total = total + part[...].astype(F32)
    l = total[:, D:PAY]
    l = l + pltpu.roll(l, HEAD, 1)
    low = low_lanes(total.shape[0])
    for j in range(PAIRS):
        den = jnp.where(low, l[:, 2 * j : 2 * j + 1], l[:, 2 * j + 1 : 2 * j + 2])
        out_ref[:, 128 * j : 128 * j + 128] = (total[:, 128 * j : 128 * j + 128] / den).astype(BF)
    out_ref[:, D:PAY] = split_pair(l)


def combine(meta, pay, received):
    rows = received[0].shape[0] if received else pay.shape[0]
    fixed = pl.BlockSpec((rows, PAY), lambda i, m: (0, 0))
    return pl.pallas_call(
        combine_kernel,
        grid_spec=pltpu.PrefetchScalarGridSpec(
            num_scalar_prefetch=1,
            grid=(1,),
            in_specs=[pl.BlockSpec((rows, PAY), lambda i, m: (m[1], 0))] + [fixed] * len(received),
            out_specs=fixed,
        ),
        out_shape=sds((rows, PAY), BF),
        name="combine",
    )(meta, pay, *received)


def first_kernel(wo_pack, ff_pack, count, meta, *refs):
    parts = refs[:count]
    lat_ref, gb_ref, bin_ref = refs[count : count + 3]
    refs = refs[count + 3 :]
    n_wo, n_ff = len(wo_pack.arrays), len(ff_pack.arrays)
    wo_refs, ff_refs, refs = refs[:n_wo], refs[n_wo : n_wo + n_ff], refs[n_wo + n_ff :]
    o_ref, l_ref, z1_ref, z2_ref, h_ref, wo, win, wout, hs, sems, hsems = refs
    f, s = meta[0], meta[1]
    start_square(wo_pack, wo_refs, SHARE, wo, f, sems.at[0])
    start_up(ff_pack, ff_refs, 0, win, f, sems.at[pl.ds(1, CHUNKS)])
    start_down(ff_pack, ff_refs, CHUNKS * SHARE, wout, f, sems.at[1 + CHUNKS])
    step = parts[0].shape[0]
    for k, part in enumerate(parts):
        rows = pl.ds(pl.multiple_of(lax.rem(s - k + count, count) * step, step), step)
        o_ref[rows, :] = part[:, :D]
        l_ref[rows, :] = join_pair(part[:, D:PAY])
    wait_for(wo, sems.at[0])
    z1 = lat_ref[...].astype(F32) + nn(o_ref[...], wo[...])
    z1_ref[...] = z1
    n = ln(z1, gb_ref[2:3], gb_ref[7:8]).astype(BF)
    y = jnp.zeros_like(z1)
    for c in range(CHUNKS):
        at = slice(c * D, c * D + D)
        wait_for(win.at[:, at], sems.at[1 + c])
        h = nn(n, win[:, at]) + bin_ref[0:1, at]
        hs[:, at] = h
        pltpu.make_async_copy(hs.at[:, at], h_ref.at[:, at], hsems.at[c]).start()
        a = gelu(h).astype(BF)
        if c == 0:
            wait_for(wout, sems.at[1 + CHUNKS])
        y = y + nn(a, wout[at, :])
    z2_ref[...] = z1 + (y + gb_ref[10:11])
    for c in range(CHUNKS):
        at = slice(c * D, c * D + D)
        pltpu.make_async_copy(hs.at[:, at], h_ref.at[:, at], hsems.at[c]).wait()


def first_block(wo_pack, ff_pack, meta, parts, lat, gb, bins):
    rows = lat.shape[0]
    n_w = len(wo_pack.arrays) + len(ff_pack.arrays)
    return pl.pallas_call(
        functools.partial(first_kernel, wo_pack, ff_pack, len(parts)),
        in_specs=[pl.BlockSpec(memory_space=pltpu.SMEM)] + [WHOLE] * (len(parts) + 3) + [ANY] * n_w,
        out_specs=[WHOLE] * 4 + [ANY],
        scratch_shapes=[
            pltpu.VMEM((D, D), BF),
            pltpu.VMEM((D, FF), BF),
            pltpu.VMEM((FF, D), BF),
            pltpu.VMEM((rows, FF), F32),
            pltpu.SemaphoreType.DMA((2 + CHUNKS,)),
            pltpu.SemaphoreType.DMA((CHUNKS,)),
        ],
        out_shape=[
            sds((rows, D), BF),
            sds((rows, 128), F32),
            sds((rows, D), F32),
            sds((rows, D), F32),
            sds((rows, FF), F32),
        ],
        compiler_params=PARAMS,
        cost_estimate=cost(18 * rows * D * D, 16 * D * D * 2),
        name="first_block",
    )(meta, *parts, lat, gb, bins, *wo_pack.arrays, *ff_pack.arrays)


def softmax_rows(scores):
    e = jnp.exp(scores - jnp.max(scores, -1, keepdims=True))
    return e / jnp.sum(e, -1, keepdims=True)


def put_vec(shares, rows, row, width):
    vec = jnp.concatenate(rows + [jnp.zeros((width - len(rows), HALF), F32)], 0).astype(BF)
    for which in range(2):
        for k in range(4):
            shares[which, k, row : row + width, :] = vec


def halves(line):
    return [line[:, i : i + HALF] for i in range(0, line.shape[1], HALF)]


def column_sum(values):
    return jnp.sum(values, 0, keepdims=True)


def put_rows(shares, f, row, grad, first=0):
    grad = grad.astype(BF)
    for g in range(OWNERS):
        rel = f ^ g
        shares[rel & 1, rel >> 1, row : row + SHARE, :] = grad[g * SHARE : g * SHARE + SHARE]


def put_down(shares, f, row, grad, u):
    grad = grad.astype(BF)
    span = CHUNKS * SHARE
    for i in range(D // span):
        rel = f ^ (u * (D // span) + i)
        shares[rel & 1, rel >> 1, row : row + span, :] = grad[i * span : i * span + span]


def ff_grads(shares, f, h, row, n, dh_ref, a_ref, dy_ref):
    for c in range(CHUNKS):
        at = pl.ds(pl.multiple_of(h * (FF // 2) + c * HALF, 128), HALF)
        put_rows(shares, f, row + c * SHARE, tn(n, dh_ref[:, at]))
    dyh = dy_ref[:, pl.ds(pl.multiple_of(h * HALF, 128), HALF)]
    for u in range(CHUNKS):
        put_down(shares, f, row + CHUNKS * SHARE, tn(a_ref[:, u * D : u * D + D], dyh), u)


def send_shares(shares, keep_ref, send_ref, sems):
    copies = [
        pltpu.make_async_copy(shares.at[0], keep_ref, sems.at[0]),
        pltpu.make_async_copy(shares.at[1], send_ref, sems.at[1]),
    ]
    for copy in copies:
        copy.start()
    for copy in copies:
        copy.wait()


def second_kernel(pack, meta, z2_ref, g4_ref, gb_ref, bin_ref, *refs):
    count = len(pack.arrays)
    wrefs, refs = refs[:count], refs[count:]
    out_ref, g3_ref, qkv_ref, o2_ref, keep_ref, send_ref = refs[:6]
    wqkv, wo, win, wout, hs, ac, dhs, shares, sems, osems = refs[6:]
    f, h = meta[0], meta[2]
    for j in range(3):
        start_square(pack, wrefs, j * SHARE, wqkv.at[j], f, sems.at[j])
    start_square(pack, wrefs, 3 * SHARE, wo, f, sems.at[3])
    start_up(pack, wrefs, 4 * SHARE, win, f, sems.at[pl.ds(4, CHUNKS)])
    start_down(pack, wrefs, (4 + CHUNKS) * SHARE, wout, f, sems.at[4 + CHUNKS])
    z2 = z2_ref[...]
    m = ln(z2, gb_ref[3:4], gb_ref[8:9]).astype(BF)
    for j in range(3):
        wait_for(wqkv.at[j], sems.at[j])
        qkv_ref[j] = nn(m, wqkv[j]).astype(BF)
    for clip in range(z2.shape[0] // NLAT):
        rows = slice(clip * NLAT, clip * NLAT + NLAT)
        for pair in range(PAIRS):
            at = slice(pair * 128, pair * 128 + 128)
            p = softmax_rows(nt(block_diag(qkv_ref[0, rows, at]), qkv_ref[1, rows, at]) * 0.125)
            o2_ref[rows, at] = diag_of(nn(p.astype(BF), qkv_ref[2, rows, at])).astype(BF)
    wait_for(wo, sems.at[3])
    z3 = z2 + nn(o2_ref[...], wo[...])
    n = ln(z3, gb_ref[4:5], gb_ref[9:10]).astype(BF)
    y = jnp.zeros_like(z3)
    for c in range(CHUNKS):
        at = slice(c * D, c * D + D)
        wait_for(win.at[:, at], sems.at[4 + c])
        hidden = nn(n, win[:, at]) + bin_ref[1:2, at]
        act, slope = gelu_both(hidden)
        hs[:, at] = slope
        ac[:, at] = act.astype(BF)
        if c == 0:
            wait_for(wout, sems.at[4 + CHUNKS])
        y = y + nn(ac[:, at], wout[at, :])
    out_ref[...] = z3 + (y + gb_ref[11:12])
    dy = g4_ref[...]
    dn = jnp.zeros_like(z3)
    dbin = []
    for c in range(CHUNKS):
        at = slice(c * D, c * D + D)
        dh = (nt(dy, wout[at, :]) * hs[:, at]).astype(BF)
        dhs[:, at] = dh
        dbin += halves(column_sum(dh.astype(F32)))
        dn = dn + nt(dh, win[:, at])
    back, dgain = ln_back(z3, gb_ref[4:5], dn)
    g4 = dy.astype(F32)
    g3_ref[...] = g4 + back
    ff_grads(shares, f, h, 0, n, dhs, ac, g4_ref)
    vec = halves(column_sum(dgain)) + halves(column_sum(dn)) + halves(column_sum(g4)) + dbin
    put_vec(shares, vec, 2 * CHUNKS * SHARE, VEC_F)
    send_shares(shares, keep_ref, send_ref, osems)


def second_block(pack, meta, z2, g4, gb, bins):
    rows = z2.shape[0]
    return pl.pallas_call(
        functools.partial(second_kernel, pack),
        in_specs=[pl.BlockSpec(memory_space=pltpu.SMEM)] + [WHOLE] * 4 + [ANY] * len(pack.arrays),
        out_specs=[WHOLE] * 4 + [ANY] * 2,
        scratch_shapes=[
            pltpu.VMEM((3, D, D), BF),
            pltpu.VMEM((D, D), BF),
            pltpu.VMEM((D, FF), BF),
            pltpu.VMEM((FF, D), BF),
            pltpu.VMEM((rows, FF), F32),
            pltpu.VMEM((rows, FF), BF),
            pltpu.VMEM((rows, FF), BF),
            pltpu.VMEM((2, 4, ROWS_F, HALF), BF),
            pltpu.SemaphoreType.DMA((5 + CHUNKS,)),
            pltpu.SemaphoreType.DMA((2,)),
        ],
        out_shape=[
            sds((rows, D), F32),
            sds((rows, D), F32),
            sds((3, rows, D), BF),
            sds((rows, D), BF),
            sds((4, ROWS_F, HALF), BF),
            sds((4, ROWS_F, HALF), BF),
        ],
        compiler_params=PARAMS,
        cost_estimate=cost(50 * rows * D * D, 12 * D * D * 4),
        name="second_block",
    )(meta, z2, g4, gb, bins, *pack.arrays)


def third_kernel(ff_pack, self_pack, wo_pack, meta, *refs):
    g3_ref, z2_ref, z1_ref, o2_ref, qkv_ref, o_ref, l_ref, gb_ref, h_ref = refs[:9]
    refs = refs[9:]
    sizes = [len(p.arrays) for p in (ff_pack, self_pack, wo_pack)]
    ff_refs, refs = refs[: sizes[0]], refs[sizes[0] :]
    self_refs, refs = refs[: sizes[1]], refs[sizes[1] :]
    wo_refs, refs = refs[: sizes[2]], refs[sizes[2] :]
    g1_ref, du_ref, dl_ref, keep_ref, send_ref = refs[:5]
    wqkv, wo1, wo0, win, wout, hs, ac, dhs, dqkv, dab, dyb, shares, sems, osems = refs[5:]
    f, h = meta[0], meta[2]
    start_square(self_pack, self_refs, 3 * SHARE, wo1, f, sems.at[3])
    for j in range(3):
        start_square(self_pack, self_refs, j * SHARE, wqkv.at[j], f, sems.at[j])
    hcopy = pltpu.make_async_copy(h_ref, hs, sems.at[4])
    hcopy.start()
    start_down(ff_pack, ff_refs, CHUNKS * SHARE, wout, f, sems.at[5])
    start_up(ff_pack, ff_refs, 0, win, f, sems.at[pl.ds(6, CHUNKS)])
    start_square(wo_pack, wo_refs, SHARE, wo0, f, sems.at[6 + CHUNKS])
    half = pl.ds(pl.multiple_of(h * HALF, 128), HALF)

    g3 = g3_ref[...]
    dab[...] = g3.astype(BF)
    wait_for(wo1, sems.at[3])
    dyb[...] = nt(dab[...], wo1[...]).astype(BF)
    for clip in range(g3.shape[0] // NLAT):
        rows = slice(clip * NLAT, clip * NLAT + NLAT)
        for pair in range(PAIRS):
            at = slice(pair * 128, pair * 128 + 128)
            q, k, v = qkv_ref[0, rows, at], qkv_ref[1, rows, at], qkv_ref[2, rows, at]
            qbd = block_diag(q)
            p = softmax_rows(nt(qbd, k) * 0.125)
            dobd = block_diag(dyb[rows, at])
            dp = nt(dobd, v)
            ds = (p * (dp - jnp.sum(p * dp, -1, keepdims=True))).astype(BF)
            dqkv[0, rows, at] = (diag_of(nn(ds, k)) * 0.125).astype(BF)
            dqkv[1, rows, at] = (tn(ds, qbd) * 0.125).astype(BF)
            dqkv[2, rows, at] = tn(p.astype(BF), dobd).astype(BF)
    row = 2 * CHUNKS * SHARE
    put_rows(shares, f, row + 3 * SHARE, tn(o2_ref[...], dab[:, half]))
    z2 = z2_ref[...]
    m = ln(z2, gb_ref[3:4], gb_ref[8:9]).astype(BF)
    dm = jnp.zeros_like(g3)
    for j in range(3):
        wait_for(wqkv.at[j], sems.at[j])
        dm = dm + nt(dqkv[j], wqkv[j])
        put_rows(shares, f, row + j * SHARE, tn(m, dqkv[j, :, half]))
    back, dgain3 = ln_back(z2, gb_ref[3:4], dm)
    g2 = g3 + back

    z1 = z1_ref[...]
    n = ln(z1, gb_ref[2:3], gb_ref[7:8]).astype(BF)
    dyb[...] = g2.astype(BF)
    hcopy.wait()
    wait_for(wout, sems.at[5])
    dn = jnp.zeros_like(g3)
    dbin = []
    for c in range(CHUNKS):
        at = slice(c * D, c * D + D)
        act, slope = gelu_both(hs[:, at])
        ac[:, at] = act.astype(BF)
        dh = (nt(dyb[...], wout[at, :]) * slope).astype(BF)
        dhs[:, at] = dh
        dbin += halves(column_sum(dh.astype(F32)))
        wait_for(win.at[:, at], sems.at[6 + c])
        dn = dn + nt(dh, win[:, at])
    back, dgain2 = ln_back(z1, gb_ref[2:3], dn)
    g1 = g2 + back
    g1_ref[...] = g1
    ff_grads(shares, f, h, 0, n, dhs, ac, dyb)
    vec = halves(column_sum(dgain2)) + halves(column_sum(dn))
    vec += halves(column_sum(dyb[...].astype(F32))) + dbin
    vec += halves(column_sum(dgain3)) + halves(column_sum(dm))
    put_vec(shares, vec, row + 5 * SHARE, VEC_S)

    dab[...] = g1.astype(BF)
    wait_for(wo0, sems.at[6 + CHUNKS])
    do = nt(dab[...], wo0[...]).astype(BF).astype(F32)
    put_rows(shares, f, row + 4 * SHARE, tn(o_ref[...], dab[:, half]))
    low = low_lanes(g3.shape[0])
    lane = lax.broadcasted_iota(jnp.int32, low.shape, 1)
    l = l_ref[...]
    dl = jnp.zeros(low.shape, F32)
    for j in range(PAIRS):
        at = slice(128 * j, 128 * j + 128)
        first, later = l[:, 2 * j : 2 * j + 1], l[:, 2 * j + 1 : 2 * j + 2]
        du_ref[:, at] = (do[:, at] / jnp.where(low, first, later)).astype(BF)
        t = do[:, at] * o_ref[:, at].astype(F32)
        t_first = -jnp.sum(jnp.where(low, t, 0.0), -1, keepdims=True) / first
        t_later = -jnp.sum(jnp.where(low, 0.0, t), -1, keepdims=True) / later
        dl = jnp.where(lane == 2 * j, t_first, jnp.where(lane == 2 * j + 1, t_later, dl))
    dl_ref[...] = dl
    send_shares(shares, keep_ref, send_ref, osems)


def third_block(ff_pack, self_pack, wo_pack, meta, g3, z2, z1, o2, qkv, o, l, gb, hidden):
    rows = z2.shape[0]
    arrays = [*ff_pack.arrays, *self_pack.arrays, *wo_pack.arrays]
    return pl.pallas_call(
        functools.partial(third_kernel, ff_pack, self_pack, wo_pack),
        in_specs=[pl.BlockSpec(memory_space=pltpu.SMEM)]
        + [WHOLE] * 8
        + [ANY] * (1 + len(arrays)),
        out_specs=[WHOLE] * 3 + [ANY] * 2,
        scratch_shapes=[
            pltpu.VMEM((3, D, D), BF),
            pltpu.VMEM((D, D), BF),
            pltpu.VMEM((D, D), BF),
            pltpu.VMEM((D, FF), BF),
            pltpu.VMEM((FF, D), BF),
            pltpu.VMEM((rows, FF), F32),
            pltpu.VMEM((rows, FF), BF),
            pltpu.VMEM((rows, FF), BF),
            pltpu.VMEM((3, rows, D), BF),
            pltpu.VMEM((rows, D), BF),
            pltpu.VMEM((rows, D), BF),
            pltpu.VMEM((2, 4, ROWS_S, HALF), BF),
            pltpu.SemaphoreType.DMA((7 + CHUNKS,)),
            pltpu.SemaphoreType.DMA((2,)),
        ],
        out_shape=[
            sds((rows, D), F32),
            sds((rows, D), BF),
            sds((rows, 128), F32),
            sds((4, ROWS_S, HALF), BF),
            sds((4, ROWS_S, HALF), BF),
        ],
        compiler_params=PARAMS,
        cost_estimate=cost(50 * rows * D * D, 16 * D * D * 4),
        name="third_block",
    )(meta, g3, z2, z1, o2, qkv, o, l, gb, hidden, *arrays)


def attend_back_kernel(padded, q_ref, du_ref, dl_ref, mask_ref, k_ref, v_ref, dk_ref, dv_ref, dq_ref, dlt):
    pair = pl.program_id(1)

    @pl.when(pair == 0)
    def _():
        dlt[...] = dl_ref[0].T

    qbd = block_diag(q_ref[0])
    dubd = block_diag(du_ref[0])
    line = jnp.concatenate([dlt[pl.ds(2 * pair, 1), :], dlt[pl.ds(2 * pair + 1, 1), :]], 1)
    dqt = jnp.zeros((128, 2 * NLAT), F32)
    for first, width in spans(padded, 256):
        rows = slice(first, first + width)
        k, v = k_ref[0, rows, :], v_ref[0, rows, :]
        mask = mask_ref[0, rows, :]
        e = jnp.exp(nt(k, qbd) + jnp.concatenate([mask, mask], 1))
        ds = (e * (nt(v, dubd) + line)).astype(BF)
        dv_ref[0, rows, :] = nn(e.astype(BF), dubd).astype(BF)
        dk_ref[0, rows, :] = nn(ds, qbd).astype(BF)
        dqt = dqt + tn(k, ds)
    upper = lax.broadcasted_iota(jnp.int32, (128, NLAT), 0) < HEAD
    dq_ref[0] = (jnp.where(upper, dqt[:, :NLAT], dqt[:, NLAT:]).T * 0.125).astype(BF)


def attend_back(q, du, dl, mask, k, v):
    clips, padded = k.shape[0], k.shape[1]
    small = pl.BlockSpec((1, NLAT, 128), lambda i, j: (i, 0, j))
    whole = pl.BlockSpec((1, NLAT, 128), lambda i, j: (i, 0, 0))
    column = pl.BlockSpec((1, padded, 128), lambda i, j: (i, 0, 0))
    lanes = pl.BlockSpec((1, padded, 128), lambda i, j: (i, 0, j))
    return pl.pallas_call(
        functools.partial(attend_back_kernel, padded),
        grid=(clips, PAIRS),
        in_specs=[small, small, whole, column, lanes, lanes],
        out_specs=[lanes, lanes, small],
        scratch_shapes=[pltpu.VMEM((128, NLAT), F32)],
        out_shape=[sds((clips, padded, D), BF)] * 2 + [sds((clips, NLAT, D), BF)],
        compiler_params=PARAMS,
        cost_estimate=cost(
            20 * clips * padded * NLAT * D, clips * padded * D * 8, clips * padded * NLAT * HEADS
        ),
        name="attend_back",
    )(q, du, dl, mask, k, v)


def keyval_grad_kernel(meta, xl_ref, dk_ref, dv_ref, keep_ref, send_ref, sum_ref, acc, sums, shares, sems):
    f = meta[0]
    clip = pl.program_id(0)

    @pl.when(clip == 0)
    def _():
        acc[...] = jnp.zeros_like(acc)
        sums[...] = jnp.zeros_like(sums)

    xt = xl_ref[0].T
    for j, ref in enumerate((dk_ref, dv_ref)):
        for c in range(0, D, 256):
            acc[j, :, c : c + 256] += nn(xt, ref[0, :, c : c + 256])
        sums[j : j + 1, :] += column_sum(ref[0].astype(F32))

    @pl.when(clip == pl.num_programs(0) - 1)
    def _():
        for j in range(2):
            for g in range(OWNERS):
                rel = f ^ g
                grad = acc[j, g * SHARE : g * SHARE + SHARE, :].astype(BF)
                shares[rel & 1, rel >> 1, j * SHARE : j * SHARE + SHARE, :] = grad
        copies = []
        for which, ref in ((0, keep_ref), (1, send_ref)):
            for k in range(4):
                copies.append(
                    pltpu.make_async_copy(
                        shares.at[which, k], ref.at[k, pl.ds(0, 2 * SHARE)], sems.at[which, k]
                    )
                )
        for copy in copies:
            copy.start()
        sum_ref[...] = sums[...]
        for copy in copies:
            copy.wait()


def keyval_grad(meta, xl, dk, dv):
    clips, padded = xl.shape[0], xl.shape[1]
    block = pl.BlockSpec((1, padded, D), lambda i, m: (i, 0, 0))
    return pl.pallas_call(
        keyval_grad_kernel,
        grid_spec=pltpu.PrefetchScalarGridSpec(
            num_scalar_prefetch=1,
            grid=(clips,),
            in_specs=[block] * 3,
            out_specs=[ANY, ANY, pl.BlockSpec((8, D), lambda i, m: (0, 0))],
            scratch_shapes=[
                pltpu.VMEM((2, D, D), F32),
                pltpu.VMEM((8, D), F32),
                pltpu.VMEM((2, 4, 2 * SHARE, D), BF),
                pltpu.SemaphoreType.DMA((2, 4)),
            ],
        ),
        out_shape=[sds((4, ROWS_K, D), BF), sds((4, ROWS_K, D), BF), sds((8, D), F32)],
        compiler_params=PARAMS,
        cost_estimate=cost(4 * clips * padded * D * D, clips * padded * D * 6),
        name="keyval_grad",
    )(meta, xl, dk, dv)


def query_grad_kernel(pack, count, meta, *refs):
    own_ref, parts, refs = refs[0], refs[1:count], refs[count:]
    lat_ref, gb_ref, sum_ref, keep_in, send_in = refs[:5]
    refs = refs[5:]
    n_w = len(pack.arrays)
    wrefs, (back_ref, keep_ref, send_ref, wq, shares, sem, osems) = refs[:n_w], refs[n_w:]
    f = meta[0]
    start_square(pack, wrefs, 0, wq, f, sem.at[0])
    total = own_ref[...].astype(F32)
    for part in parts:
        total = total + part[...].astype(F32)
    dq = total.astype(BF)
    lat = lat_ref[...].astype(F32)
    zl = ln(lat, gb_ref[0:1], gb_ref[5:6]).astype(BF)
    grad = tn(zl, dq).astype(BF)
    for g in range(OWNERS):
        rel = f ^ g
        shares[rel & 1, rel >> 1, 0:SHARE, :] = grad[g * SHARE : g * SHARE + SHARE]
    wait_for(wq, sem.at[0])
    dzl = nt(dq, wq[...])
    back, dgain = ln_back(lat, gb_ref[0:1], dzl)
    back_ref[...] = back.astype(BF)
    lines = [sum_ref[0:1], sum_ref[1:2], column_sum(dgain), column_sum(dzl)]
    vec = jnp.concatenate(lines + [jnp.zeros((VEC_K - 4, D), F32)], 0).astype(BF)
    copies = []
    for which, ref in ((0, keep_ref), (1, send_ref)):
        for k in range(4):
            shares[which, k, SHARE : SHARE + VEC_K, :] = vec
            copies.append(
                pltpu.make_async_copy(
                    shares.at[which, k],
                    ref.at[k, pl.ds(2 * SHARE, SHARE + VEC_K)],
                    osems.at[which, k],
                )
            )
    for copy in copies:
        copy.start()
    for copy in copies:
        copy.wait()


def query_grad(pack, meta, dq, parts, lat, gb, sums, keep, send):
    rows = parts[0].shape[0] if parts else dq.shape[0]
    count = 1 + len(parts)
    mine = pl.BlockSpec((rows, D), lambda i, m: (m[1], 0))
    fixed = lambda shape: pl.BlockSpec(shape, lambda i, m: (0,) * len(shape))
    return pl.pallas_call(
        functools.partial(query_grad_kernel, pack, count),
        grid_spec=pltpu.PrefetchScalarGridSpec(
            num_scalar_prefetch=1,
            grid=(1,),
            in_specs=[mine]
            + [fixed((rows, D))] * len(parts)
            + [mine, fixed((16, D)), fixed((8, D)), ANY, ANY]
            + [ANY] * len(pack.arrays),
            out_specs=[fixed((rows, D)), ANY, ANY],
            scratch_shapes=[
                pltpu.VMEM((D, D), BF),
                pltpu.VMEM((2, 4, SHARE + VEC_K, D), BF),
                pltpu.SemaphoreType.DMA((1,)),
                pltpu.SemaphoreType.DMA((2, 4)),
            ],
        ),
        out_shape=[sds((rows, D), BF), sds(keep.shape, BF), sds(send.shape, BF)],
        input_output_aliases={count + 4: 1, count + 5: 2},
        compiler_params=PARAMS,
        name="query_grad",
    )(meta, dq, *parts, lat, gb, sums, keep, send, *pack.arrays)


def token_grad_kernel(pack, meta, x_ref, gb_ref, dk_ref, dv_ref, *refs):
    count = len(pack.arrays)
    wrefs, (out_ref, wkv, sems) = refs[:count], refs[count:]

    @pl.when((pl.program_id(0) == 0) & (pl.program_id(1) == 0))
    def _():
        f = meta[0]
        start_square(pack, wrefs, 0, wkv.at[0], f, sems.at[0])
        start_square(pack, wrefs, SHARE, wkv.at[1], f, sems.at[1])
        wait_for(wkv.at[0], sems.at[0])
        wait_for(wkv.at[1], sems.at[1])

    grad = nt(dk_ref[0], wkv[0]) + nt(dv_ref[0], wkv[1])
    back, unused = ln_back(x_ref[0].astype(F32), gb_ref[1:2], grad)
    out_ref[0] = back


def token_grad(pack, meta, tokens, gb, dk, dv):
    clips, local = tokens.shape[0], tokens.shape[1]
    padded = dk.shape[1]
    tile = padded // 4
    block = pl.BlockSpec((1, tile, D), lambda i, j, m: (i, j, 0))
    return pl.pallas_call(
        functools.partial(token_grad_kernel, pack),
        grid_spec=pltpu.PrefetchScalarGridSpec(
            num_scalar_prefetch=1,
            grid=(clips, padded // tile),
            in_specs=[block, pl.BlockSpec((16, D), lambda i, j, m: (0, 0)), block, block]
            + [ANY] * len(pack.arrays),
            out_specs=block,
            scratch_shapes=[pltpu.VMEM((2, D, D), BF), pltpu.SemaphoreType.DMA((2,))],
        ),
        out_shape=sds((clips, local, D), F32),
        compiler_params=PARAMS,
        cost_estimate=cost(4 * clips * padded * D * D, clips * padded * D * 10),
        name="token_grad",
    )(meta, tokens, gb, dk, dv, *pack.arrays)


def fold_kernel(keep_ref, recv_ref, *out_refs):
    for k, ref in enumerate(out_refs):
        ref[...] = (keep_ref[k].astype(F32) + recv_ref[k].astype(F32)).astype(BF)


def fold(keep, recv):
    shape = keep.shape[1:]
    lanes = 128
    block = pl.BlockSpec((4, shape[0], lanes), lambda i: (0, 0, i))
    return pl.pallas_call(
        fold_kernel,
        grid=(shape[1] // lanes,),
        in_specs=[block, block],
        out_specs=[pl.BlockSpec((shape[0], lanes), lambda i: (0, i))] * 4,
        out_shape=[sds(shape, BF)] * 4,
        compiler_params=PARAMS,
        name="fold",
    )(keep, recv)


def sum_kernel(*refs):
    total = refs[0][...].astype(F32)
    for ref in refs[1:-1]:
        total = total + ref[...].astype(F32)
    refs[-1][...] = total.astype(BF)


def sum_of(parts):
    shape = parts[0].shape
    block = pl.BlockSpec((shape[0], 128), lambda i: (0, i))
    return pl.pallas_call(
        sum_kernel,
        grid=(shape[1] // 128,),
        in_specs=[block] * len(parts),
        out_specs=block,
        out_shape=sds(shape, BF),
        compiler_params=PARAMS,
        name="sum_parts",
    )(*parts)


def exchange(x, bit):
    return lax.ppermute(x, "fsdp", [(i, i ^ bit) for i in range(OWNERS)])


def reduce_shares(keep, send, size):
    if size == OWNERS:
        mine, first, second, third = fold(keep, exchange(send, 1))
        return sum_of([mine, exchange(first, 2), exchange(second, 4), exchange(third, 6)])
    full = jnp.stack([keep, send], 1).reshape(OWNERS, *keep.shape[1:])
    return lax.psum(full.astype(F32), "fsdp").astype(BF)


def unpack(left_f, right_f, left_s, right_s, whole_k):
    sides_f, sides_s = (left_f, right_f), (left_s, right_s)
    span = CHUNKS * SHARE

    def up(sides):
        return jnp.concatenate(
            [x[c * SHARE : c * SHARE + SHARE] for x in sides for c in range(CHUNKS)], 1
        )

    def down(sides):
        return jnp.concatenate([x[span : 2 * span] for x in sides], 1)

    def square(i):
        at = 2 * span + i * SHARE
        return jnp.concatenate([x[at : at + SHARE] for x in sides_s], 1)

    q1, k1, v1, out1, out0 = (square(i) for i in range(5))
    k0, v0, q0 = (whole_k[i * SHARE : i * SHARE + SHARE] for i in range(3))
    return (
        jnp.stack([jnp.stack([q0, k0, v0]), jnp.stack([q1, k1, v1])]).astype(F32),
        jnp.stack([out0, out1]).astype(F32),
        jnp.stack([up(sides_s), up(sides_f)]).astype(F32),
        jnp.stack([down(sides_s), down(sides_f)]).astype(F32),
    )


def per_device(size, seq, *args):
    (
        latents_in,
        inputs,
        clip_frames,
        text_mask,
        qkv_weight,
        out_weight,
        mlp_in,
        mlp_out,
        norm_gain,
        norm_bias,
        bias_in,
        bias_out,
        out_cotangent,
    ) = args
    micro, clips, nlat, _ = latents_in.shape
    count = micro * clips
    local = inputs.shape[2]
    padded = -(-local // 128) * 128
    rows = count * nlat
    s = lax.axis_index("seq")
    fsdp = lax.axis_index("fsdp")
    special = size == OWNERS
    meta = jnp.stack([fsdp if special else jnp.int32(0), s, s % 2]).astype(jnp.int32)
    lat = latents_in.reshape(rows, D)
    tokens = inputs.reshape(count, local, D)
    g4 = out_cotangent.reshape(rows, D)

    place = s * local + jnp.arange(padded, dtype=jnp.int32)
    frames = clip_frames.reshape(count, 1) * PATCHES
    text = text_mask.reshape(count, -1) > 0
    text_len = text.shape[1]
    slots = FRAMES * PATCHES
    wide = jnp.pad(text, ((0, 0), (slots, padded)))
    text_here = lax.dynamic_slice_in_dim(wide, s * local, padded, 1)
    valid = jnp.where(place[None] < slots, place[None] < frames, text_here)
    valid = valid & (jnp.arange(padded)[None] < local)
    bias = jnp.where(valid, 0.0, -1e30).astype(F32)
    mask = jnp.broadcast_to(bias[:, :, None], (count, padded, 128))

    def packs_of(qkv, out, up, down, gain, shift, up_b, down_b):
        small = jnp.concatenate(
            [
                jnp.pad(jnp.concatenate([gain, shift, down_b], 0), ((0, 0), (0, 128 - SHARE))),
                up_b.reshape(6, 128),
                jnp.zeros((14, 128), BF),
            ],
            0,
        )
        small = jnp.concatenate([small[:16], small[16:]], 1)
        small = jnp.pad(small, ((0, 0), (0, D - 256)))
        slabs = lambda i: up[i].reshape(SHARE, CHUNKS, D).transpose(1, 0, 2).reshape(CHUNKS * SHARE, D)
        return (
            jnp.concatenate([qkv[0, 1], qkv[0, 2], small], 0),
            jnp.concatenate([qkv[0, 0], out[0]], 0),
            jnp.concatenate([slabs(0), down[0]], 0),
            jnp.concatenate([qkv[1].reshape(3 * SHARE, D), out[1], slabs(1), down[1]], 0),
        )

    weights = (qkv_weight, out_weight, mlp_in, mlp_out, norm_gain, norm_bias, bias_in, bias_out)
    axes = (2, 1, 1, 1, 1, 1, 1, 1)
    if special:
        raw = packs_of(*weights)

        def core_of(x):
            return exchange(x, 1)

        def direct(x):
            p = {0: x, 2: exchange(x, 2), 4: exchange(x, 4), 6: exchange(x, 6)}
            return Pack(
                [p[m] if m % 2 == 0 else core_of(p[m - 1]) for m in range(OWNERS)],
                lambda m, row: (m, None, row),
            )

        def relayed(x):
            half = x.shape[0] // 2
            p2, p4 = exchange(x, 2), exchange(x, 4)
            a6, b6 = exchange(p2[:half], 4), exchange(p4[half:], 2)
            arrays = [x, core_of(x), p2, core_of(p2), p4, core_of(p4), a6, core_of(a6), b6, core_of(b6)]

            def where(m, row):
                if m < 6:
                    return (m, None, row)
                return (m, None, row) if row < half else (m + 2, None, row - half)

            return Pack(arrays, where)

        g1a, g1b = direct(raw[0]), direct(raw[1])
        g2, g34 = relayed(raw[2]), relayed(raw[3])
    else:
        full = []
        for w, axis in zip(weights, axes):
            whole = lax.all_gather(w, "fsdp", axis=axis, tiled=True)
            shape = whole.shape
            parts = whole.reshape(*shape[:axis], OWNERS, shape[axis] // OWNERS, *shape[axis + 1 :])
            full.append(jnp.moveaxis(parts, axis, 0))
        raw = jax.vmap(packs_of)(*full)
        g1a, g1b, g2, g34 = [Pack([x], lambda m, row: (0, m, row)) for x in raw]

    def shift_to(x, k):
        return lax.ppermute(x, "seq", [(i, (i + k) % seq) for i in range(seq)])

    def scatter_rows(x):
        step = x.shape[0] // seq
        out = []
        for k in range(1, seq):
            piece = lax.dynamic_slice_in_dim(x, ((s + k) % seq) * step, step, 0)
            out.append(shift_to(piece, k))
        return out

    def gather_rows(x):
        return [x] + [shift_to(x, k) for k in range(1, seq)]

    xl, k, v, gb, bins = keyval(g1a, meta, tokens, local, padded)
    pay, q = attend(g1b, meta, lat, gb, bias[:, None, :], k, v)
    pay = pay.reshape(rows, PAY)
    share = combine(meta, pay, scatter_rows(pay))
    o, l, z1, z2, hidden = first_block(g1b, g2, meta, gather_rows(share), lat, gb, bins)
    out, g3, qkv2, o2, keep_f, send_f = second_block(g34, meta, z2, g4, gb, bins)

    g1, du, dl, keep_s, send_s = third_block(g2, g34, g1b, meta, g3, z2, z1, o2, qkv2, o, l, gb, hidden)
    cube = lambda x: x.reshape(count, nlat, x.shape[-1])
    dk, dv, dq = attend_back(cube(q), cube(du), cube(dl), mask, k, v)
    dq = dq.reshape(rows, D)
    dq_parts = scatter_rows(dq)
    keep_k, send_k, sums = keyval_grad(meta, xl, dk, dv)
    back, keep_k, send_k = query_grad(g1b, meta, dq, dq_parts, lat, gb, sums, keep_k, send_k)
    token_grads = token_grad(g1a, meta, tokens, gb, dk, dv)

    lat_grad = g1 + place_rows(gather_rows(back), s, seq)

    mine_f = reduce_shares(keep_f, send_f, size)
    mine_s = reduce_shares(keep_s, send_s, size)
    mine_k = reduce_shares(keep_k, send_k, size)
    pair = [(i, i ^ 1) for i in range(seq)]
    first = s % 2 == 0

    def both(mine):
        other = lax.ppermute(mine, "seq", pair)
        return jnp.where(first, mine, other), jnp.where(first, other, mine)

    if special:
        own = lax.dynamic_slice_in_dim(mine_k, s * (ROWS_K // seq), ROWS_K // seq, 0)
        pieces = gather_rows(sum_of([own] + scatter_rows(mine_k)))
        whole_k = place_rows(pieces, s, seq)
    else:
        whole_k = lax.psum(mine_k.astype(F32), "seq")
    shares = (*both(mine_f), *both(mine_s), whole_k)
    if special:
        grads = unpack(*shares)
        head = lambda x: x.astype(F32)
    else:
        wide = jax.vmap(unpack)(*shares)
        grads = []
        for x, w, axis in zip(wide, weights, axes):
            x = jnp.moveaxis(x, 0, axis)
            x = x.reshape(*x.shape[:axis], -1, *x.shape[axis + 2 :])
            grads.append(lax.dynamic_slice_in_dim(x, fsdp * w.shape[axis], w.shape[axis], axis))
        head = lambda x: x[0].astype(F32)
    vec_f = head(shares[0])[-VEC_F:].reshape(-1, D)
    vec_s = head(shares[2])[-VEC_S:].reshape(-1, D)
    vec_k = head(whole_k)[-VEC_K:]
    step = norm_gain.shape[1]
    k0, v0 = grads[0][0, 1], grads[0][0, 2]
    own_k, own_v = qkv_weight[0, 1].astype(F32), qkv_weight[0, 2].astype(F32)
    own_gain, own_shift = norm_gain[1].astype(F32), norm_bias[1].astype(F32)
    db1 = jnp.sum(own_k * vec_k[0] + own_v * vec_k[1], -1)
    dg1 = (jnp.sum(own_k * k0 + own_v * v0, -1) - own_shift * db1) / own_gain
    lines = jnp.stack([vec_k[2], vec_s[0], vec_s[7], vec_f[0], vec_k[3], vec_s[1], vec_s[8], vec_f[1], vec_s[2], vec_f[2]])
    cut = lax.dynamic_slice_in_dim(lines, fsdp * step, step, 1)
    wide_bias = jnp.stack([vec_s[3:7].reshape(FF), vec_f[3:7].reshape(FF)])
    return (
        out.reshape(latents_in.shape),
        lat_grad.reshape(latents_in.shape),
        token_grads.reshape(inputs.shape),
        *grads,
        jnp.stack([cut[0], dg1, cut[1], cut[2], cut[3]]),
        jnp.stack([cut[4], db1, cut[5], cut[6], cut[7]]),
        lax.dynamic_slice_in_dim(wide_bias, fsdp * bias_in.shape[1], bias_in.shape[1], 1),
        cut[8:10],
    )


def place_rows(pieces, s, seq):
    step = pieces[0].shape[0]
    whole = jnp.zeros((seq * step, *pieces[0].shape[1:]), F32)
    for k, piece in enumerate(pieces):
        at = ((s - k) % seq) * step
        whole = lax.dynamic_update_slice_in_dim(whole, piece.astype(F32), at, 0)
    return whole


def solution(mesh):
    in_specs = (
        P(None, "fsdp", None, None),
        P(None, "fsdp", "seq", None),
        P(None, "fsdp"),
        P(None, "fsdp", None),
        P(None, None, "fsdp", None),
        P(None, "fsdp", None),
        P(None, "fsdp", None),
        P(None, "fsdp", None),
        P(None, "fsdp"),
        P(None, "fsdp"),
        P(None, "fsdp"),
        P(None, "fsdp"),
        P(None, "fsdp", None, None),
    )
    out_specs = (
        P(None, "fsdp", None, None),
        P(None, "fsdp", None, None),
        P(None, "fsdp", "seq", None),
        P(None, None, "fsdp", None),
        P(None, "fsdp", None),
        P(None, "fsdp", None),
        P(None, "fsdp", None),
        P(None, "fsdp"),
        P(None, "fsdp"),
        P(None, "fsdp"),
        P(None, "fsdp"),
    )
    step = functools.partial(per_device, mesh.shape["fsdp"], mesh.shape["seq"])
    return jax.shard_map(step, mesh=mesh, in_specs=in_specs, out_specs=out_specs, check_vma=False)
```

```python
import functools

import jax
import jax.numpy as jnp
from jax import lax
from jax.experimental import pallas as pl
from jax.experimental.pallas import tpu as pltpu
from jax.sharding import PartitionSpec as P

D = 768
HEADS = 12
HEAD = 64
PAIRS = HEADS // 2
FF = 3072
NLAT = 128
PATCHES = 392
FRAMES = 16
OWNERS = 8
SHARE = D // OWNERS
CHUNKS = FF // D
HALF = D // 2
PAY = D + 128
KEYVAL_ROWS = 208
FORWARD_PAIRS = 3
BACK_PAIRS = 2
TOKEN_TILES = 2
GRAD_TILES = 1
TOKEN_ROWS = 416
VEC = 16
VEC_K = 32
SPAN = CHUNKS * SHARE
ROWS_F = 2 * SPAN + VEC
ROWS_A = ROWS_F + 4 * SHARE + VEC
ROWS_B = 2 * SPAN + SHARE + VEC
ROWS_K = 3 * SHARE + VEC_K
EPS = 1e-06
F32 = jnp.float32
BF = jnp.bfloat16
GELU_C = 0.7978845608028654
GELU_A = 0.044715
VMEM_CAP = 60 * 1024 * 1024


def nn(a, b):
    return lax.dot_general(a, b, (((1,), (0,)), ((), ())), preferred_element_type=F32)


def nt(a, b):
    return lax.dot_general(a, b, (((1,), (1,)), ((), ())), preferred_element_type=F32)


def tn(a, b):
    return lax.dot_general(a, b, (((0,), (0,)), ((), ())), preferred_element_type=F32)


def ln_parts(x):
    center = x - jnp.mean(x, -1, keepdims=True)
    rstd = lax.rsqrt(jnp.mean(center * center, -1, keepdims=True) + EPS)
    return center, rstd


def ln(x, gain, bias):
    center, rstd = ln_parts(x)
    return center * rstd * gain + bias


def ln_back(x, gain, grad):
    center, rstd = ln_parts(x)
    xhat = center * rstd
    dx = grad * gain
    back = rstd * (dx - jnp.mean(dx, -1, keepdims=True) - xhat * jnp.mean(dx * xhat, -1, keepdims=True))
    return back, grad * xhat


def gelu(h):
    return h * (0.5 * (1.0 + jnp.tanh(GELU_C * (h + GELU_A * h * h * h))))


def gelu_both(h):
    square = h * h
    t = jnp.tanh(GELU_C * (h + GELU_A * h * square))
    cdf = 0.5 * (1.0 + t)
    slope = cdf + 0.5 * h * (1.0 - t * t) * (GELU_C * (1.0 + 3.0 * GELU_A * square))
    return h * cdf, slope


def low_lanes(rows):
    return lax.broadcasted_iota(jnp.int32, (rows, 128), 1) < HEAD


def block_diag(pair):
    wide = pair.astype(F32)
    low = low_lanes(pair.shape[0])
    return jnp.concatenate([jnp.where(low, wide, 0.0), jnp.where(low, 0.0, wide)], 0).astype(BF)


def diag_of(both):
    rows = both.shape[0] // 2
    return jnp.where(low_lanes(rows), both[:rows], both[rows:])


class Pack:
    def __init__(self, arrays, where):
        self.arrays, self.where = arrays, where

    def start(self, refs, row, rows, place, f, sem):
        for m in range(OWNERS):
            index, lead, first = self.where(m, row)
            src = refs[index] if lead is None else refs[index].at[lead]
            pltpu.make_async_copy(src.at[pl.ds(first, rows)], place(f ^ m), sem).start()


def wait_for(ref, sem):
    pltpu.make_async_copy(ref, ref, sem).wait()


def share_rows(ref, g, first=0, span=SHARE, step=SHARE):
    return ref.at[pl.ds(pl.multiple_of(g * step + first, SHARE), span)]


def start_square(pack, refs, row, dst, f, sem):
    pack.start(refs, row, SHARE, lambda g: share_rows(dst, g), f, sem)


def start_up(pack, refs, row, dst, f, sems):
    for t in range(CHUNKS):
        lanes = pl.ds(t * D, D)
        pack.start(
            refs,
            row + t * SHARE,
            SHARE,
            lambda g, lanes=lanes: dst.at[pl.ds(pl.multiple_of(g * SHARE, SHARE), SHARE), lanes],
            f,
            sems.at[t],
        )


def start_down(pack, refs, row, dst, f, sem):
    for t in range(CHUNKS):
        pack.start(
            refs,
            row + t * SHARE,
            SHARE,
            lambda g, t=t: share_rows(dst, g, t * SHARE, SHARE, CHUNKS * SHARE),
            f,
            sem,
        )


ANY = pl.BlockSpec(memory_space=pl.ANY)
WHOLE = pl.BlockSpec(memory_space=pltpu.VMEM)


def sds(shape, dtype):
    return jax.ShapeDtypeStruct(shape, dtype)


def cost(flops, size, exps=0):
    return pl.CostEstimate(flops=1, bytes_accessed=1, transcendentals=0)


PARAMS = pltpu.CompilerParams(vmem_limit_bytes=VMEM_CAP)


def keyval_kernel(pack, local, tile, meta, x_ref, *refs):
    count = len(pack.arrays)
    wrefs, (xl_ref, k_ref, v_ref, gb_ref, bin_ref, wkv, small, sems) = refs[:count], refs[count:]
    f = meta[0]

    @pl.when((pl.program_id(0) == 0) & (pl.program_id(1) == 0))
    def _():
        for m in range(OWNERS):
            index, lead, first = pack.where(m, 3 * SHARE)
            src = wrefs[index] if lead is None else wrefs[index].at[lead]
            pltpu.make_async_copy(
                src.at[pl.ds(first, 16), pl.ds(0, 256)], small.at[m], sems.at[2]
            ).start()
        start_square(pack, wrefs, 0, wkv.at[0], f, sems.at[0])
        start_square(pack, wrefs, SHARE, wkv.at[1], f, sems.at[1])
        wait_for(small, sems.at[2])
        lane = lax.broadcasted_iota(jnp.int32, (128, D), 1)
        row = lax.broadcasted_iota(jnp.int32, (128, D), 0)
        total = jnp.zeros((16, D), F32)
        for m in range(OWNERS):
            g = f ^ m
            place = jnp.where((lane - g * SHARE == row) & (row < SHARE), 1.0, 0.0).astype(BF)
            total = total + nn(small[m, :, 0:128], place)
            wide = small[m].astype(F32)
            for u in range(6):
                i, part = u // 3, u % 3
                line = wide[12 + u : 13 + u, 0:128] if u < 4 else wide[u - 4 : u - 3, 128:256]
                at = pl.ds(pl.multiple_of((3 * g + part) * 128, 128), 128)
                bin_ref[i : i + 1, at] = line
        gb_ref[...] = total
        wait_for(wkv.at[0], sems.at[0])
        wait_for(wkv.at[1], sems.at[1])

    for first in range(0, tile, KEYVAL_ROWS):
        part = slice(first, first + KEYVAL_ROWS)
        normed = ln(x_ref[0, part, :].astype(F32), gb_ref[1:2], gb_ref[6:7])
        row = lax.broadcasted_iota(jnp.int32, (KEYVAL_ROWS, D), 0)
        row = row + (pl.program_id(1) * tile + first)
        xl = jnp.where(row < local, normed, 0.0).astype(BF)
        xl_ref[0, part, :] = xl
        k_ref[0, part, :] = nn(xl, wkv[0]).astype(BF)
        v_ref[0, part, :] = nn(xl, wkv[1]).astype(BF)


def keyval(pack, meta, tokens, local, padded):
    clips = tokens.shape[0]
    tile = padded // 2
    block = pl.BlockSpec((1, tile, D), lambda i, j, m: (i, j, 0))
    fixed = lambda shape: pl.BlockSpec(shape, lambda i, j, m: (0,) * len(shape))
    return pl.pallas_call(
        functools.partial(keyval_kernel, pack, local, tile),
        grid_spec=pltpu.PrefetchScalarGridSpec(
            num_scalar_prefetch=1,
            grid=(clips, padded // tile),
            in_specs=[block] + [ANY] * len(pack.arrays),
            out_specs=[block, block, block, fixed((16, D)), fixed((2, FF))],
            scratch_shapes=[
                pltpu.VMEM((2, D, D), BF),
                pltpu.VMEM((OWNERS, 16, 256), BF),
                pltpu.SemaphoreType.DMA((3,)),
            ],
        ),
        out_shape=[sds((clips, padded, D), BF)] * 3 + [sds((16, D), F32), sds((2, FF), F32)],
        compiler_params=PARAMS,
        cost_estimate=cost(4 * clips * padded * D * D, clips * padded * D * 8),
        name="keyval",
    )(meta, tokens, *pack.arrays)


def attend_kernel(pack, padded, meta, lat_ref, gb_ref, bias_ref, k_ref, v_ref, *refs):
    count = len(pack.arrays)
    wrefs, (pay_ref, q_ref, wq, qs, lv, sem) = refs[:count], refs[count:]
    f = meta[0]
    clip, group = pl.program_id(0), pl.program_id(1)

    @pl.when((clip == 0) & (group == 0))
    def _():
        start_square(pack, wrefs, 2 * SHARE, wq, f, sem.at[0])
        zl = ln(lat_ref[...].astype(F32), gb_ref[0:1], gb_ref[5:6]).astype(BF)
        wait_for(wq, sem.at[0])
        q = nn(zl, wq[...]).astype(BF).astype(F32) * 0.125
        qs[...] = q.astype(BF)
        q_ref[...] = qs[...]

    rows = pl.ds(pl.multiple_of(clip * NLAT, NLAT), NLAT)
    lane = lax.broadcasted_iota(jnp.int32, (NLAT, 128), 1)
    new = jnp.where(group == 0, 0.0, lv[...])
    for p in range(FORWARD_PAIRS):
        pair = group * FORWARD_PAIRS + p
        at = pl.ds(pl.multiple_of(pair * 128, 128), 128)
        mine = slice(p * 128, p * 128 + 128)
        e = jnp.exp(nt(block_diag(qs[rows, at]), k_ref[0, :, mine]) + bias_ref[0])
        pay_ref[0, :, at] = diag_of(nn(e.astype(BF), v_ref[0, :, mine])).astype(BF)
        l = jnp.sum(e, -1, keepdims=True)
        new = jnp.where(lane == 2 * pair, l[:NLAT], jnp.where(lane == 2 * pair + 1, l[NLAT:], new))
    lv[...] = new

    @pl.when(group == PAIRS // FORWARD_PAIRS - 1)
    def _():
        pay_ref[0, :, D:PAY] = split_pair(lv[...])


def split_pair(values):
    high = values.astype(BF).astype(F32)
    rest = values - high
    return jnp.where(low_lanes(values.shape[0]), high, pltpu.roll(rest, HEAD, 1)).astype(BF)


def join_pair(pay):
    wide = pay.astype(F32)
    return wide + pltpu.roll(wide, HEAD, 1)


def attend(pack, meta, lat, gb, bias, k, v):
    clips, padded = k.shape[0], k.shape[1]
    rows = lat.shape[0]
    fixed = lambda shape: pl.BlockSpec(shape, lambda i, j, m: (0,) * len(shape))
    lanes = pl.BlockSpec((1, padded, 128 * FORWARD_PAIRS), lambda i, j, m: (i, 0, j))
    return pl.pallas_call(
        functools.partial(attend_kernel, pack, padded),
        grid_spec=pltpu.PrefetchScalarGridSpec(
            num_scalar_prefetch=1,
            grid=(clips, PAIRS // FORWARD_PAIRS),
            in_specs=[
                fixed((rows, D)),
                fixed((16, D)),
                pl.BlockSpec((1, 1, padded), lambda i, j, m: (i, 0, 0)),
                lanes,
                lanes,
            ]
            + [ANY] * len(pack.arrays),
            out_specs=[
                pl.BlockSpec((1, NLAT, PAY), lambda i, j, m: (i, 0, 0)),
                fixed((rows, D)),
            ],
            scratch_shapes=[
                pltpu.VMEM((D, D), BF),
                pltpu.VMEM((rows, D), BF),
                pltpu.VMEM((NLAT, 128), F32),
                pltpu.SemaphoreType.DMA((1,)),
            ],
        ),
        out_shape=[sds((clips, NLAT, PAY), BF), sds((rows, D), BF)],
        compiler_params=PARAMS,
        cost_estimate=cost(
            8 * clips * padded * NLAT * D, clips * padded * D * 4, clips * padded * NLAT * HEADS
        ),
        name="attend",
    )(meta, lat, gb, bias, k, v, *pack.arrays)


def combine_kernel(*refs):
    parts, out_ref = refs[1:-1], refs[-1]
    total = parts[0][...].astype(F32)
    for part in parts[1:]:
        total = total + part[...].astype(F32)
    l = total[:, D:PAY]
    l = l + pltpu.roll(l, HEAD, 1)
    low = low_lanes(total.shape[0])
    for j in range(PAIRS):
        den = jnp.where(low, l[:, 2 * j : 2 * j + 1], l[:, 2 * j + 1 : 2 * j + 2])
        out_ref[:, 128 * j : 128 * j + 128] = (total[:, 128 * j : 128 * j + 128] / den).astype(BF)
    out_ref[:, D:PAY] = split_pair(l)


def combine(meta, pay, received):
    rows = received[0].shape[0] if received else pay.shape[0]
    fixed = pl.BlockSpec((rows, PAY), lambda i, m: (0, 0))
    return pl.pallas_call(
        combine_kernel,
        grid_spec=pltpu.PrefetchScalarGridSpec(
            num_scalar_prefetch=1,
            grid=(1,),
            in_specs=[pl.BlockSpec((rows, PAY), lambda i, m: (m[1], 0))] + [fixed] * len(received),
            out_specs=fixed,
        ),
        out_shape=sds((rows, PAY), BF),
        name="combine",
    )(meta, pay, *received)


def first_kernel(pack, count, meta, *refs):
    parts = refs[:count]
    lat_ref, gb_ref, bin_ref = refs[count : count + 3]
    refs = refs[count + 3 :]
    wrefs, refs = refs[: len(pack.arrays)], refs[len(pack.arrays) :]
    o_ref, l_ref, z1_ref, z2_ref, h_ref, wo, win, wout, hs, sems, hsems = refs
    f, s = meta[0], meta[1]
    start_square(pack, wrefs, 0, wo, f, sems.at[0])
    start_up(pack, wrefs, SHARE, win, f, sems.at[pl.ds(1, CHUNKS)])
    start_down(pack, wrefs, SHARE + SPAN, wout, f, sems.at[1 + CHUNKS])
    step = parts[0].shape[0]
    for k, part in enumerate(parts):
        rows = pl.ds(pl.multiple_of(lax.rem(s - k + count, count) * step, step), step)
        o_ref[rows, :] = part[:, :D]
        l_ref[rows, :] = join_pair(part[:, D:PAY])
    wait_for(wo, sems.at[0])
    z1 = lat_ref[...].astype(F32) + nn(o_ref[...], wo[...])
    z1_ref[...] = z1
    n = ln(z1, gb_ref[2:3], gb_ref[7:8]).astype(BF)
    y = jnp.zeros_like(z1)
    for c in range(CHUNKS):
        at = slice(c * D, c * D + D)
        wait_for(win.at[:, at], sems.at[1 + c])
        h = nn(n, win[:, at]) + bin_ref[0:1, at]
        hs[:, at] = h
        pltpu.make_async_copy(hs.at[:, at], h_ref.at[:, at], hsems.at[c]).start()
        a = gelu(h).astype(BF)
        if c == 0:
            wait_for(wout, sems.at[1 + CHUNKS])
        y = y + nn(a, wout[at, :])
    z2_ref[...] = z1 + (y + gb_ref[10:11])
    for c in range(CHUNKS):
        at = slice(c * D, c * D + D)
        pltpu.make_async_copy(hs.at[:, at], h_ref.at[:, at], hsems.at[c]).wait()


def first_block(pack, meta, parts, lat, gb, bins):
    rows = lat.shape[0]
    n_w = len(pack.arrays)
    return pl.pallas_call(
        functools.partial(first_kernel, pack, len(parts)),
        in_specs=[pl.BlockSpec(memory_space=pltpu.SMEM)] + [WHOLE] * (len(parts) + 3) + [ANY] * n_w,
        out_specs=[WHOLE] * 4 + [ANY],
        scratch_shapes=[
            pltpu.VMEM((D, D), BF),
            pltpu.VMEM((D, FF), BF),
            pltpu.VMEM((FF, D), BF),
            pltpu.VMEM((rows, FF), F32),
            pltpu.SemaphoreType.DMA((2 + CHUNKS,)),
            pltpu.SemaphoreType.DMA((CHUNKS,)),
        ],
        out_shape=[
            sds((rows, D), BF),
            sds((rows, 128), F32),
            sds((rows, D), F32),
            sds((rows, D), F32),
            sds((rows, FF), F32),
        ],
        compiler_params=PARAMS,
        cost_estimate=cost(18 * rows * D * D, 16 * D * D * 2),
        name="first_block",
    )(meta, *parts, lat, gb, bins, *pack.arrays)


def softmax_rows(scores):
    e = jnp.exp(scores - jnp.max(scores, -1, keepdims=True))
    return e / jnp.sum(e, -1, keepdims=True)


def put_vec(shares, rows, row, width):
    vec = jnp.concatenate(rows + [jnp.zeros((width - len(rows), HALF), F32)], 0).astype(BF)
    for which in range(2):
        for k in range(4):
            shares[which, k, row : row + width, :] = vec


def halves(line):
    return [line[:, i : i + HALF] for i in range(0, line.shape[1], HALF)]


def column_sum(values):
    return jnp.sum(values, 0, keepdims=True)


def put_rows(shares, f, row, grad, first=0):
    grad = grad.astype(BF)
    for g in range(OWNERS):
        rel = f ^ g
        shares[rel & 1, rel >> 1, row : row + SHARE, :] = grad[g * SHARE : g * SHARE + SHARE]


def put_down(shares, f, row, grad, u):
    grad = grad.astype(BF)
    span = CHUNKS * SHARE
    for i in range(D // span):
        rel = f ^ (u * (D // span) + i)
        shares[rel & 1, rel >> 1, row : row + span, :] = grad[i * span : i * span + span]


def ff_grads(shares, f, h, row, n, dh_ref, a_ref, dy_ref):
    for c in range(CHUNKS):
        at = pl.ds(pl.multiple_of(h * (FF // 2) + c * HALF, 128), HALF)
        put_rows(shares, f, row + c * SHARE, tn(n, dh_ref[:, at]))
    dyh = dy_ref[:, pl.ds(pl.multiple_of(h * HALF, 128), HALF)]
    for u in range(CHUNKS):
        put_down(shares, f, row + CHUNKS * SHARE, tn(a_ref[:, u * D : u * D + D], dyh), u)


def send_shares(shares, keep_ref, send_ref, first, sems):
    rows = pl.ds(first, shares.shape[2])
    copies = []
    for which, ref in ((0, keep_ref), (1, send_ref)):
        for k in range(4):
            copies.append(
                pltpu.make_async_copy(shares.at[which, k], ref.at[k, rows], sems.at[which, k])
            )
    for copy in copies:
        copy.start()
    for copy in copies:
        copy.wait()


def second_kernel(pack, meta, z2_ref, g4_ref, gb_ref, bin_ref, *refs):
    count = len(pack.arrays)
    wrefs, refs = refs[:count], refs[count:]
    out_ref, g3_ref, qkv_ref, o2_ref, keep_ref, send_ref = refs[:6]
    wqkv, wo, win, wout, hs, ac, dhs, shares, sems, osems = refs[6:]
    f, h = meta[0], meta[2]
    for j in range(3):
        start_square(pack, wrefs, j * SHARE, wqkv.at[j], f, sems.at[j])
    start_square(pack, wrefs, 3 * SHARE, wo, f, sems.at[3])
    start_up(pack, wrefs, 4 * SHARE, win, f, sems.at[pl.ds(4, CHUNKS)])
    start_down(pack, wrefs, (4 + CHUNKS) * SHARE, wout, f, sems.at[4 + CHUNKS])
    z2 = z2_ref[...]
    m = ln(z2, gb_ref[3:4], gb_ref[8:9]).astype(BF)
    for j in range(3):
        wait_for(wqkv.at[j], sems.at[j])
        qkv_ref[j] = nn(m, wqkv[j]).astype(BF)
    for clip in range(z2.shape[0] // NLAT):
        rows = slice(clip * NLAT, clip * NLAT + NLAT)
        for pair in range(PAIRS):
            at = slice(pair * 128, pair * 128 + 128)
            p = softmax_rows(nt(block_diag(qkv_ref[0, rows, at]), qkv_ref[1, rows, at]) * 0.125)
            o2_ref[rows, at] = diag_of(nn(p.astype(BF), qkv_ref[2, rows, at])).astype(BF)
    wait_for(wo, sems.at[3])
    z3 = z2 + nn(o2_ref[...], wo[...])
    n = ln(z3, gb_ref[4:5], gb_ref[9:10]).astype(BF)
    y = jnp.zeros_like(z3)
    for c in range(CHUNKS):
        at = slice(c * D, c * D + D)
        wait_for(win.at[:, at], sems.at[4 + c])
        hidden = nn(n, win[:, at]) + bin_ref[1:2, at]
        act, slope = gelu_both(hidden)
        hs[:, at] = slope
        ac[:, at] = act.astype(BF)
        if c == 0:
            wait_for(wout, sems.at[4 + CHUNKS])
        y = y + nn(ac[:, at], wout[at, :])
    out_ref[...] = z3 + (y + gb_ref[11:12])
    dy = g4_ref[...]
    dn = jnp.zeros_like(z3)
    dbin = []
    for c in range(CHUNKS):
        at = slice(c * D, c * D + D)
        dh = (nt(dy, wout[at, :]) * hs[:, at]).astype(BF)
        dhs[:, at] = dh
        dbin += halves(column_sum(dh.astype(F32)))
        dn = dn + nt(dh, win[:, at])
    back, dgain = ln_back(z3, gb_ref[4:5], dn)
    g4 = dy.astype(F32)
    g3_ref[...] = g4 + back
    ff_grads(shares, f, h, 0, n, dhs, ac, g4_ref)
    vec = halves(column_sum(dgain)) + halves(column_sum(dn)) + halves(column_sum(g4)) + dbin
    put_vec(shares, vec, 2 * SPAN, VEC)
    send_shares(shares, keep_ref, send_ref, 0, osems)


def second_block(pack, meta, z2, g4, gb, bins):
    rows = z2.shape[0]
    return pl.pallas_call(
        functools.partial(second_kernel, pack),
        in_specs=[pl.BlockSpec(memory_space=pltpu.SMEM)] + [WHOLE] * 4 + [ANY] * len(pack.arrays),
        out_specs=[WHOLE] * 4 + [ANY] * 2,
        scratch_shapes=[
            pltpu.VMEM((3, D, D), BF),
            pltpu.VMEM((D, D), BF),
            pltpu.VMEM((D, FF), BF),
            pltpu.VMEM((FF, D), BF),
            pltpu.VMEM((rows, FF), F32),
            pltpu.VMEM((rows, FF), BF),
            pltpu.VMEM((rows, FF), BF),
            pltpu.VMEM((2, 4, ROWS_F, HALF), BF),
            pltpu.SemaphoreType.DMA((5 + CHUNKS,)),
            pltpu.SemaphoreType.DMA((2, 4)),
        ],
        out_shape=[
            sds((rows, D), F32),
            sds((rows, D), F32),
            sds((3, rows, D), BF),
            sds((rows, D), BF),
            sds((4, ROWS_A, HALF), BF),
            sds((4, ROWS_A, HALF), BF),
        ],
        compiler_params=PARAMS,
        cost_estimate=cost(50 * rows * D * D, 12 * D * D * 4),
        name="second_block",
    )(meta, z2, g4, gb, bins, *pack.arrays)


def third_kernel(pack, meta, g3_ref, z2_ref, o2_ref, qkv_ref, gb_ref, keep_in, send_in, *refs):
    count = len(pack.arrays)
    wrefs, (g2_ref, keep_ref, send_ref) = refs[:count], refs[count : count + 3]
    wqkv, wo, dqkv, dab, dob, shares, sems, osems = refs[count + 3 :]
    f, h = meta[0], meta[2]
    start_square(pack, wrefs, 3 * SHARE, wo, f, sems.at[3])
    for j in range(3):
        start_square(pack, wrefs, j * SHARE, wqkv.at[j], f, sems.at[j])
    half = pl.ds(pl.multiple_of(h * HALF, 128), HALF)
    g3 = g3_ref[...]
    dab[...] = g3.astype(BF)
    put_rows(shares, f, 3 * SHARE, tn(o2_ref[...], dab[:, half]))
    z2 = z2_ref[...]
    m = ln(z2, gb_ref[3:4], gb_ref[8:9]).astype(BF)
    wait_for(wo, sems.at[3])
    dob[...] = nt(dab[...], wo[...]).astype(BF)
    for clip in range(g3.shape[0] // NLAT):
        rows = slice(clip * NLAT, clip * NLAT + NLAT)
        for pair in range(PAIRS):
            at = slice(pair * 128, pair * 128 + 128)
            q, k, v = qkv_ref[0, rows, at], qkv_ref[1, rows, at], qkv_ref[2, rows, at]
            qbd = block_diag(q)
            p = softmax_rows(nt(qbd, k) * 0.125)
            dobd = block_diag(dob[rows, at])
            dp = nt(dobd, v)
            ds = (p * (dp - jnp.sum(p * dp, -1, keepdims=True))).astype(BF)
            dqkv[0, rows, at] = (diag_of(nn(ds, k)) * 0.125).astype(BF)
            dqkv[1, rows, at] = (tn(ds, qbd) * 0.125).astype(BF)
            dqkv[2, rows, at] = tn(p.astype(BF), dobd).astype(BF)
    dm = jnp.zeros_like(g3)
    for j in range(3):
        wait_for(wqkv.at[j], sems.at[j])
        dm = dm + nt(dqkv[j], wqkv[j])
        put_rows(shares, f, j * SHARE, tn(m, dqkv[j, :, half]))
    back, dgain = ln_back(z2, gb_ref[3:4], dm)
    g2_ref[...] = g3 + back
    put_vec(shares, halves(column_sum(dgain)) + halves(column_sum(dm)), 4 * SHARE, VEC)
    send_shares(shares, keep_ref, send_ref, ROWS_F, osems)


def third_block(pack, meta, g3, z2, o2, qkv, gb, keep, send):
    rows = z2.shape[0]
    return pl.pallas_call(
        functools.partial(third_kernel, pack),
        in_specs=[pl.BlockSpec(memory_space=pltpu.SMEM)]
        + [WHOLE] * 5
        + [ANY] * (2 + len(pack.arrays)),
        out_specs=[WHOLE] + [ANY] * 2,
        scratch_shapes=[
            pltpu.VMEM((3, D, D), BF),
            pltpu.VMEM((D, D), BF),
            pltpu.VMEM((3, rows, D), BF),
            pltpu.VMEM((rows, D), BF),
            pltpu.VMEM((rows, D), BF),
            pltpu.VMEM((2, 4, ROWS_A - ROWS_F, HALF), BF),
            pltpu.SemaphoreType.DMA((4,)),
            pltpu.SemaphoreType.DMA((2, 4)),
        ],
        out_shape=[sds((rows, D), F32), sds(keep.shape, BF), sds(send.shape, BF)],
        input_output_aliases={6: 1, 7: 2},
        compiler_params=PARAMS,
        cost_estimate=cost(14 * rows * D * D, 4 * D * D * 4),
        name="third_block",
    )(meta, g3, z2, o2, qkv, gb, keep, send, *pack.arrays)


def fourth_kernel(pack, meta, g2_ref, z1_ref, o_ref, l_ref, gb_ref, h_ref, *refs):
    wrefs, refs = refs[: len(pack.arrays)], refs[len(pack.arrays) :]
    g1_ref, du_ref, dl_ref, keep_ref, send_ref = refs[:5]
    wo, win, wout, hs, ac, dhs, dab, dyb, shares, sems, osems = refs[5:]
    f, h = meta[0], meta[2]
    start_down(pack, wrefs, SHARE + SPAN, wout, f, sems.at[5])
    hcopy = pltpu.make_async_copy(h_ref, hs, sems.at[4])
    hcopy.start()
    start_up(pack, wrefs, SHARE, win, f, sems.at[pl.ds(0, CHUNKS)])
    start_square(pack, wrefs, 0, wo, f, sems.at[6])
    half = pl.ds(pl.multiple_of(h * HALF, 128), HALF)
    z1 = z1_ref[...]
    n = ln(z1, gb_ref[2:3], gb_ref[7:8]).astype(BF)
    g2 = g2_ref[...]
    dyb[...] = g2.astype(BF)
    wait_for(wout, sems.at[5])
    hcopy.wait()
    dn = jnp.zeros_like(g2)
    dbin = []
    for c in range(CHUNKS):
        at = slice(c * D, c * D + D)
        act, slope = gelu_both(hs[:, at])
        ac[:, at] = act.astype(BF)
        dh = (nt(dyb[...], wout[at, :]) * slope).astype(BF)
        dhs[:, at] = dh
        dbin += halves(column_sum(dh.astype(F32)))
        wait_for(win.at[:, at], sems.at[c])
        dn = dn + nt(dh, win[:, at])
    back, dgain = ln_back(z1, gb_ref[2:3], dn)
    g1 = g2 + back
    g1_ref[...] = g1
    ff_grads(shares, f, h, 0, n, dhs, ac, dyb)
    vec = halves(column_sum(dgain)) + halves(column_sum(dn))
    vec += halves(column_sum(dyb[...].astype(F32))) + dbin
    put_vec(shares, vec, 2 * SPAN + SHARE, VEC)

    dab[...] = g1.astype(BF)
    wait_for(wo, sems.at[6])
    do = nt(dab[...], wo[...]).astype(BF).astype(F32)
    put_rows(shares, f, 2 * SPAN, tn(o_ref[...], dab[:, half]))
    low = low_lanes(g2.shape[0])
    lane = lax.broadcasted_iota(jnp.int32, low.shape, 1)
    l = l_ref[...]
    dl = jnp.zeros(low.shape, F32)
    for j in range(PAIRS):
        at = slice(128 * j, 128 * j + 128)
        first, later = l[:, 2 * j : 2 * j + 1], l[:, 2 * j + 1 : 2 * j + 2]
        du_ref[:, at] = (do[:, at] / jnp.where(low, first, later)).astype(BF)
        t = do[:, at] * o_ref[:, at].astype(F32)
        t_first = -jnp.sum(jnp.where(low, t, 0.0), -1, keepdims=True) / first
        t_later = -jnp.sum(jnp.where(low, 0.0, t), -1, keepdims=True) / later
        dl = jnp.where(lane == 2 * j, t_first, jnp.where(lane == 2 * j + 1, t_later, dl))
    dl_ref[...] = dl
    send_shares(shares, keep_ref, send_ref, 0, osems)


def fourth_block(pack, meta, g2, z1, o, l, gb, hidden):
    rows = z1.shape[0]
    arrays = pack.arrays
    return pl.pallas_call(
        functools.partial(fourth_kernel, pack),
        in_specs=[pl.BlockSpec(memory_space=pltpu.SMEM)] + [WHOLE] * 5 + [ANY] * (1 + len(arrays)),
        out_specs=[WHOLE] * 3 + [ANY] * 2,
        scratch_shapes=[
            pltpu.VMEM((D, D), BF),
            pltpu.VMEM((D, FF), BF),
            pltpu.VMEM((FF, D), BF),
            pltpu.VMEM((rows, FF), F32),
            pltpu.VMEM((rows, FF), BF),
            pltpu.VMEM((rows, FF), BF),
            pltpu.VMEM((rows, D), BF),
            pltpu.VMEM((rows, D), BF),
            pltpu.VMEM((2, 4, ROWS_B, HALF), BF),
            pltpu.SemaphoreType.DMA((7,)),
            pltpu.SemaphoreType.DMA((2, 4)),
        ],
        out_shape=[
            sds((rows, D), F32),
            sds((rows, D), BF),
            sds((rows, 128), F32),
            sds((4, ROWS_B, HALF), BF),
            sds((4, ROWS_B, HALF), BF),
        ],
        compiler_params=PARAMS,
        cost_estimate=cost(30 * rows * D * D, 12 * D * D * 4),
        name="fourth_block",
    )(meta, g2, z1, o, l, gb, hidden, *arrays)


def attend_back_kernel(q_ref, du_ref, dl_ref, mask_ref, k_ref, v_ref, dk_ref, dv_ref, dq_ref, dlt):
    group = pl.program_id(1)

    @pl.when(group == 0)
    def _():
        dlt[...] = dl_ref[0].T

    mask = mask_ref[0]
    mask = jnp.concatenate([mask, mask], 1)
    upper = lax.broadcasted_iota(jnp.int32, (128, NLAT), 0) < HEAD
    for p in range(BACK_PAIRS):
        pair = group * BACK_PAIRS + p
        mine = slice(p * 128, p * 128 + 128)
        qbd, dubd = block_diag(q_ref[0, :, mine]), block_diag(du_ref[0, :, mine])
        line = [dlt[pl.ds(2 * pair + i, 1), :] for i in range(2)]
        k, v = k_ref[0, :, mine], v_ref[0, :, mine]
        e = jnp.exp(nt(k, qbd) + mask)
        ds = (e * (nt(v, dubd) + jnp.concatenate(line, 1))).astype(BF)
        dv_ref[0, :, mine] = nn(e.astype(BF), dubd).astype(BF)
        dk_ref[0, :, mine] = nn(ds, qbd).astype(BF)
        dqt = tn(k, ds)
        dqt = jnp.where(upper, dqt[:, :NLAT], dqt[:, NLAT:])
        dq_ref[0, :, mine] = (dqt.T * 0.125).astype(BF)


def attend_back(q, du, dl, mask, k, v):
    clips, padded = k.shape[0], k.shape[1]
    wide = 128 * BACK_PAIRS
    small = pl.BlockSpec((1, NLAT, wide), lambda i, j: (i, 0, j))
    whole = pl.BlockSpec((1, NLAT, 128), lambda i, j: (i, 0, 0))
    column = pl.BlockSpec((1, padded, 128), lambda i, j: (i, 0, 0))
    lanes = pl.BlockSpec((1, padded, wide), lambda i, j: (i, 0, j))
    return pl.pallas_call(
        attend_back_kernel,
        grid=(clips, PAIRS // BACK_PAIRS),
        in_specs=[small, small, whole, column, lanes, lanes],
        out_specs=[lanes, lanes, small],
        scratch_shapes=[pltpu.VMEM((128, NLAT), F32)],
        out_shape=[sds((clips, padded, D), BF)] * 2 + [sds((clips, NLAT, D), BF)],
        compiler_params=PARAMS,
        cost_estimate=cost(0, 0),
        name="attend_back",
    )(q, du, dl, mask, k, v)


def keyval_grad_kernel(meta, xl_ref, dk_ref, dv_ref, keep_ref, send_ref, sum_ref, acc, shares, sems):
    f = meta[0]
    step = pl.program_id(0)
    first = step == 0
    xt = xl_ref[0].T
    for j, ref in enumerate((dk_ref, dv_ref)):
        grad = nn(xt, ref[0])
        acc[j] = grad + jnp.where(first, 0.0, acc[j])
        line = column_sum(ref[0].astype(F32))
        sum_ref[j : j + 1, :] = line + jnp.where(first, 0.0, sum_ref[j : j + 1, :])

    @pl.when(step == pl.num_programs(0) - 1)
    def _():
        for j in range(2):
            for g in range(OWNERS):
                rel = f ^ g
                grad = acc[j, g * SHARE : g * SHARE + SHARE, :].astype(BF)
                shares[rel & 1, rel >> 1, j * SHARE : j * SHARE + SHARE, :] = grad
        send_shares(shares, keep_ref, send_ref, 0, sems)


def keyval_grad(meta, xl, dk, dv):
    clips, padded = xl.shape[0], xl.shape[1]
    tile = padded // GRAD_TILES
    at = lambda i, m: (i // GRAD_TILES, lax.rem(i, GRAD_TILES), 0)
    block = pl.BlockSpec((1, tile, D), at)
    return pl.pallas_call(
        keyval_grad_kernel,
        grid_spec=pltpu.PrefetchScalarGridSpec(
            num_scalar_prefetch=1,
            grid=(clips * GRAD_TILES,),
            in_specs=[block] * 3,
            out_specs=[ANY, ANY, pl.BlockSpec((8, D), lambda i, m: (0, 0))],
            scratch_shapes=[
                pltpu.VMEM((2, D, D), F32),
                pltpu.VMEM((2, 4, 2 * SHARE, D), BF),
                pltpu.SemaphoreType.DMA((2, 4)),
            ],
        ),
        out_shape=[sds((4, ROWS_K, D), BF), sds((4, ROWS_K, D), BF), sds((8, D), F32)],
        compiler_params=PARAMS,
        cost_estimate=cost(4 * clips * padded * D * D, clips * padded * D * 6),
        name="keyval_grad",
    )(meta, xl, dk, dv)


def query_grad_kernel(pack, count, meta, *refs):
    own_ref, parts, refs = refs[0], refs[1:count], refs[count:]
    lat_ref, gb_ref, sum_ref, keep_in, send_in = refs[:5]
    refs = refs[5:]
    n_w = len(pack.arrays)
    wrefs, (back_ref, keep_ref, send_ref, wq, shares, sem, osems) = refs[:n_w], refs[n_w:]
    f = meta[0]
    start_square(pack, wrefs, 2 * SHARE, wq, f, sem.at[0])
    total = own_ref[...].astype(F32)
    for part in parts:
        total = total + part[...].astype(F32)
    dq = total.astype(BF)
    lat = lat_ref[...].astype(F32)
    zl = ln(lat, gb_ref[0:1], gb_ref[5:6]).astype(BF)
    grad = tn(zl, dq).astype(BF)
    for g in range(OWNERS):
        rel = f ^ g
        shares[rel & 1, rel >> 1, 0:SHARE, :] = grad[g * SHARE : g * SHARE + SHARE]
    wait_for(wq, sem.at[0])
    dzl = nt(dq, wq[...])
    back, dgain = ln_back(lat, gb_ref[0:1], dzl)
    back_ref[...] = back.astype(BF)
    lines = [sum_ref[0:1], sum_ref[1:2], column_sum(dgain), column_sum(dzl)]
    vec = jnp.concatenate(lines + [jnp.zeros((VEC_K - 4, D), F32)], 0).astype(BF)
    copies = []
    for which, ref in ((0, keep_ref), (1, send_ref)):
        for k in range(4):
            shares[which, k, SHARE : SHARE + VEC_K, :] = vec
            copies.append(
                pltpu.make_async_copy(
                    shares.at[which, k],
                    ref.at[k, pl.ds(2 * SHARE, SHARE + VEC_K)],
                    osems.at[which, k],
                )
            )
    for copy in copies:
        copy.start()
    for copy in copies:
        copy.wait()


def query_grad(pack, meta, dq, parts, lat, gb, sums, keep, send):
    rows = parts[0].shape[0] if parts else dq.shape[0]
    count = 1 + len(parts)
    mine = pl.BlockSpec((rows, D), lambda i, m: (m[1], 0))
    fixed = lambda shape: pl.BlockSpec(shape, lambda i, m: (0,) * len(shape))
    return pl.pallas_call(
        functools.partial(query_grad_kernel, pack, count),
        grid_spec=pltpu.PrefetchScalarGridSpec(
            num_scalar_prefetch=1,
            grid=(1,),
            in_specs=[mine]
            + [fixed((rows, D))] * len(parts)
            + [mine, fixed((16, D)), fixed((8, D)), ANY, ANY]
            + [ANY] * len(pack.arrays),
            out_specs=[fixed((rows, D)), ANY, ANY],
            scratch_shapes=[
                pltpu.VMEM((D, D), BF),
                pltpu.VMEM((2, 4, SHARE + VEC_K, D), BF),
                pltpu.SemaphoreType.DMA((1,)),
                pltpu.SemaphoreType.DMA((2, 4)),
            ],
        ),
        out_shape=[sds((rows, D), BF), sds(keep.shape, BF), sds(send.shape, BF)],
        input_output_aliases={count + 4: 1, count + 5: 2},
        compiler_params=PARAMS,
        name="query_grad",
    )(meta, dq, *parts, lat, gb, sums, keep, send, *pack.arrays)


def token_grad_kernel(pack, local, meta, x_ref, gb_ref, dk_ref, dv_ref, *refs):
    count = len(pack.arrays)
    wrefs, (out_ref, wkv, lines, sems, osems) = refs[:count], refs[count:]
    clip, at = pl.program_id(0), pl.program_id(1)
    clips, tiles = pl.num_programs(0), pl.num_programs(1)
    tile = x_ref.shape[1]
    n_clips, n_tiles = out_ref.shape[0] // (local * PAIRS), -(-local // tile)

    @pl.when((clip == 0) & (at == 0))
    def _():
        f = meta[0]
        start_square(pack, wrefs, 0, wkv.at[0], f, sems.at[0])
        start_square(pack, wrefs, SHARE, wkv.at[1], f, sems.at[1])
        wait_for(wkv.at[0], sems.at[0])
        wait_for(wkv.at[1], sems.at[1])

    for first in range(0, tile, TOKEN_ROWS):
        rows = slice(first, first + TOKEN_ROWS)
        grad = nt(dk_ref[0, rows, :], wkv[0]) + nt(dv_ref[0, rows, :], wkv[1])
        back, unused = ln_back(x_ref[0, rows, :].astype(F32), gb_ref[1:2], grad)
        base = (clip * local + at * tile + first) * PAIRS
        for t in range(PAIRS):
            lines[pl.ds(base + t, TOKEN_ROWS, stride=PAIRS), :] = back[:, 128 * t : 128 * t + 128]

    def piece(c, i):
        first = (c * local + i * tile) * PAIRS // 8 * 8
        last = (c * local + min((i + 1) * tile, local)) * PAIRS
        last = last if c == n_clips - 1 and i == n_tiles - 1 else last // 8 * 8
        where = pl.ds(first, last - first)
        slot = c * n_tiles + i
        return pltpu.make_async_copy(lines.at[where], out_ref.at[where], osems.at[slot])

    for c in range(n_clips):
        for i in range(n_tiles):

            @pl.when((clip == c) & (at == i))
            def _(c=c, i=i):
                piece(c, i).start()

    @pl.when((clip == n_clips - 1) & (at == n_tiles - 1))
    def _():
        for c in range(n_clips):
            for i in range(n_tiles):
                piece(c, i).wait()


def token_grad(pack, meta, tokens, gb, dk, dv):
    clips, local = tokens.shape[0], tokens.shape[1]
    padded = dk.shape[1]
    tile = padded // TOKEN_TILES
    block = pl.BlockSpec((1, tile, D), lambda i, j, m: (i, j, 0))
    rows = clips * local * PAIRS
    return pl.pallas_call(
        functools.partial(token_grad_kernel, pack, local),
        grid_spec=pltpu.PrefetchScalarGridSpec(
            num_scalar_prefetch=1,
            grid=(clips, padded // tile),
            in_specs=[block, pl.BlockSpec((16, D), lambda i, j, m: (0, 0)), block, block]
            + [ANY] * len(pack.arrays),
            out_specs=ANY,
            scratch_shapes=[
                pltpu.VMEM((2, D, D), BF),
                pltpu.VMEM((rows + (padded - local) * PAIRS + 8, 128), F32),
                pltpu.SemaphoreType.DMA((2,)),
                pltpu.SemaphoreType.DMA((clips * TOKEN_TILES,)),
            ],
        ),
        out_shape=sds((rows, 128), F32),
        compiler_params=PARAMS,
        cost_estimate=cost(4 * clips * padded * D * D, clips * padded * D * 10),
        name="token_grad",
    )(meta, tokens, gb, dk, dv, *pack.arrays)


def fold_kernel(keep_ref, recv_ref, *out_refs):
    for k, ref in enumerate(out_refs):
        ref[...] = (keep_ref[k].astype(F32) + recv_ref[k].astype(F32)).astype(BF)


def row_block(rows):
    return rows // 2 if rows % 32 == 0 else rows


def fold(keep, recv):
    rows, lanes = keep.shape[1:]
    step = row_block(rows)
    block = pl.BlockSpec((4, step, lanes), lambda i: (0, i, 0))
    return pl.pallas_call(
        fold_kernel,
        grid=(rows // step,),
        in_specs=[block, block],
        out_specs=[pl.BlockSpec((step, lanes), lambda i: (i, 0))] * 4,
        out_shape=[sds((rows, lanes), BF)] * 4,
        compiler_params=PARAMS,
        name="fold",
    )(keep, recv)


def split_kernel(keep_ref, recv_ref, keep_p, keep_q, send_p, send_q):
    half = keep_p.shape[1]
    for first, pairs in (
        (0, ((0, keep_p, 0), (2, keep_p, 1), (1, send_p, 0), (3, send_p, 1))),
        (half, ((0, keep_q, 0), (1, keep_q, 1), (2, send_q, 0), (3, send_q, 1))),
    ):
        for k, ref, at in pairs:
            rows = slice(first, first + half)
            ref[at] = (keep_ref[k, rows, :].astype(F32) + recv_ref[k, rows, :].astype(F32)).astype(BF)


def split(keep, recv):
    rows, lanes = keep.shape[1:]
    step = 128
    block = pl.BlockSpec((4, rows, step), lambda i: (0, 0, i))
    return pl.pallas_call(
        split_kernel,
        grid=(lanes // step,),
        in_specs=[block, block],
        out_specs=[pl.BlockSpec((2, rows // 2, step), lambda i: (0, 0, i))] * 4,
        out_shape=[sds((2, rows // 2, lanes), BF)] * 4,
        compiler_params=PARAMS,
        name="split",
    )(keep, recv)


def turn_kernel(keep_p, keep_q, recv_p, recv_q, own_ref, send_p, send_q):
    half = keep_p.shape[1]
    for first, keep, recv, send in ((0, keep_p, recv_p, send_p), (half, keep_q, recv_q, send_q)):
        own_ref[first : first + half, :] = (keep[0].astype(F32) + recv[0].astype(F32)).astype(BF)
        send[...] = (keep[1].astype(F32) + recv[1].astype(F32)).astype(BF)


def turn(keep_p, keep_q, recv_p, recv_q):
    half, lanes = keep_p.shape[1:]
    step = 128
    block = pl.BlockSpec((2, half, step), lambda i: (0, 0, i))
    out = lambda n: pl.BlockSpec((n, step), lambda i: (0, i))
    return pl.pallas_call(
        turn_kernel,
        grid=(lanes // step,),
        in_specs=[block] * 4,
        out_specs=[out(2 * half), out(half), out(half)],
        out_shape=[sds((2 * half, lanes), BF), sds((half, lanes), BF), sds((half, lanes), BF)],
        compiler_params=PARAMS,
        name="turn",
    )(keep_p, keep_q, recv_p, recv_q)


def join_kernel(own_ref, recv_p, recv_q, out_ref):
    half = recv_p.shape[0]
    for first, recv in ((0, recv_p), (half, recv_q)):
        rows = slice(first, first + half)
        out_ref[rows, :] = (own_ref[rows, :].astype(F32) + recv[...].astype(F32)).astype(BF)


def join(own, recv_p, recv_q):
    rows, lanes = own.shape
    step = 128
    block = lambda n: pl.BlockSpec((n, step), lambda i: (0, i))
    return pl.pallas_call(
        join_kernel,
        grid=(lanes // step,),
        in_specs=[block(rows), block(rows // 2), block(rows // 2)],
        out_specs=block(rows),
        out_shape=sds((rows, lanes), BF),
        compiler_params=PARAMS,
        name="join",
    )(own, recv_p, recv_q)


def sum_kernel(*refs):
    total = refs[0][...].astype(F32)
    for ref in refs[1:-1]:
        total = total + ref[...].astype(F32)
    refs[-1][...] = total.astype(BF)


def sum_of(parts):
    rows, lanes = parts[0].shape
    step = row_block(rows)
    block = pl.BlockSpec((step, lanes), lambda i: (i, 0))
    return pl.pallas_call(
        sum_kernel,
        grid=(rows // step,),
        in_specs=[block] * len(parts),
        out_specs=block,
        out_shape=sds((rows, lanes), BF),
        compiler_params=PARAMS,
        name="sum_parts",
    )(*parts)


def after(x, *others):
    return lax.optimization_barrier((x, others))[0]


def exchange(x, bit):
    return lax.ppermute(x, "fsdp", [(i, i ^ bit) for i in range(OWNERS)])


def sum_over_fsdp(keep, send):
    full = jnp.stack([keep, send], 1).reshape(OWNERS, *keep.shape[1:])
    return lax.psum(full.astype(F32), "fsdp").astype(BF)


def finish_latent_kernel(count, meta, ma_ref, oa_ref, mb_ref, ob_ref, g1_ref, *refs):
    pieces, refs = refs[:count], refs[count:]
    lat_ref, qkv_ref, outw_ref, up_ref, down_ref, line_ref = refs
    s, h = meta[1], meta[2]
    step = pieces[0].shape[0]
    for k, piece in enumerate(pieces):
        rows = pl.ds(pl.multiple_of(lax.rem(s - k + count, count) * step, step), step)
        lat_ref[rows, :] = g1_ref[rows, :] + piece[...].astype(F32)
    for a_ref, b_ref, side in ((ma_ref, mb_ref, h), (oa_ref, ob_ref, 1 - h)):
        half = pl.ds(pl.multiple_of(side * HALF, 128), HALF)
        for layer, ref in ((1, a_ref), (0, b_ref)):
            for c in range(CHUNKS):
                at = pl.ds(pl.multiple_of(side * (FF // 2) + c * HALF, 128), HALF)
                up_ref[layer, :, at] = ref[c * SHARE : c * SHARE + SHARE, :].astype(F32)
            down_ref[layer, :, half] = ref[SPAN : 2 * SPAN, :].astype(F32)
        for i in range(4):
            first = ROWS_F + i * SHARE
            value = a_ref[first : first + SHARE, :].astype(F32)
            if i < 3:
                qkv_ref[0, i, :, half] = value
            else:
                outw_ref[1, :, half] = value
        outw_ref[0, :, half] = b_ref[2 * SPAN : 2 * SPAN + SHARE, :].astype(F32)
    last = ma_ref[2 * SPAN : ROWS_F, :].astype(F32)
    middle = ma_ref[ROWS_A - VEC : ROWS_A, :].astype(F32)
    first = mb_ref[ROWS_B - VEC : ROWS_B, :].astype(F32)
    line_ref[...] = jnp.zeros_like(line_ref)
    picks = [(first, 0), (middle, 0), (last, 0), (first, 1), (middle, 1), (last, 1), (first, 2), (last, 2)]
    picks += [(first, 3 + c) for c in range(CHUNKS)] + [(last, 3 + c) for c in range(CHUNKS)]
    for i, (vec, row) in enumerate(picks):
        for part in range(2):
            at = slice(part * HALF, part * HALF + HALF)
            line_ref[i : i + 1, at] = vec[2 * row + part : 2 * row + part + 1, :]


def finish_latent(meta, mine_f, other_f, mine_s, other_s, g1, pieces):
    rows = g1.shape[0]
    whole = lambda shape: pl.BlockSpec(shape, lambda i: (0,) * len(shape))
    return pl.pallas_call(
        functools.partial(finish_latent_kernel, len(pieces)),
        grid=(1,),
        in_specs=[pl.BlockSpec(memory_space=pltpu.SMEM)] + [WHOLE] * (5 + len(pieces)),
        out_specs=[
            whole((rows, D)),
            pl.BlockSpec((1, 3, SHARE, D), lambda i: (1, 0, 0, 0)),
            whole((2, SHARE, D)),
            whole((2, SHARE, FF)),
            whole((2, CHUNKS * SHARE, D)),
            whole((16, D)),
        ],
        out_shape=[
            sds((rows, D), F32),
            sds((2, 3, SHARE, D), F32),
            sds((2, SHARE, D), F32),
            sds((2, SHARE, FF), F32),
            sds((2, CHUNKS * SHARE, D), F32),
            sds((16, D), F32),
        ],
        compiler_params=PARAMS,
        name="finish_latent",
    )(meta, mine_f, other_f, mine_s, other_s, g1, *pieces)


def finish_token_kernel(count, meta, *refs):
    pieces, refs = refs[:count], refs[count:]
    w_ref, gain_ref, shift_ref, line_ref, qkv_in, qkv_ref, gain_out, shift_out, bin_out, bout_out, whole = refs
    f, s = meta[0], meta[1]
    step = pieces[0].shape[0]
    for k, piece in enumerate(pieces):
        rows = pl.ds(pl.multiple_of(lax.rem(s - k + count, count) * step, step), step)
        whole[rows, :] = piece[...].astype(F32)
    dk, dv, dq = (whole[i * SHARE : i * SHARE + SHARE, :] for i in range(3))
    qkv_ref[0, 0], qkv_ref[0, 1], qkv_ref[0, 2] = dq, dk, dv
    vec = whole[3 * SHARE : 3 * SHARE + 8, :]
    wk, wv = w_ref[0].astype(F32), w_ref[1].astype(F32)
    shift_sum = jnp.sum(wk * vec[0:1] + wv * vec[1:2], -1, keepdims=True)
    gain_sum = jnp.sum(wk * dk + wv * dv, -1, keepdims=True)
    lane = lax.broadcasted_iota(jnp.int32, (SHARE, 128), 1)
    turned = jnp.where(lane == 0, shift_sum, jnp.where(lane == 1, gain_sum, 0.0)).T
    db, total = turned[0:1, :SHARE], turned[1:2, :SHARE]
    dg = (total - shift_ref[1:2, :].astype(F32) * db) / gain_ref[1:2, :].astype(F32)
    lines = jnp.concatenate([line_ref[...], vec], 0)
    cut = pltpu.roll(lines, lax.rem(D - f * SHARE, D), 1)[:, :SHARE]
    gain_out[0:1, :], gain_out[1:2, :], gain_out[2:5, :] = cut[18:19], dg, cut[0:3]
    shift_out[0:1, :], shift_out[1:2, :], shift_out[2:5, :] = cut[19:20], db, cut[3:6]
    bout_out[...] = cut[6:8]
    wide = jnp.concatenate([line_ref[8 + c : 9 + c, :] for c in range(CHUNKS)], 1)
    other = jnp.concatenate([line_ref[12 + c : 13 + c, :] for c in range(CHUNKS)], 1)
    both = jnp.concatenate([wide, other], 0)
    span = CHUNKS * SHARE
    total = jnp.zeros((2, span), F32)
    for g in range(OWNERS):
        total = jnp.where(f == g, both[:, g * span : g * span + span], total)
    bin_out[...] = total


def finish_token(meta, pieces, weights, gain, shift, lines, qkv):
    whole = lambda shape: pl.BlockSpec(shape, lambda i: (0,) * len(shape))
    count = len(pieces)
    return pl.pallas_call(
        functools.partial(finish_token_kernel, count),
        grid=(1,),
        in_specs=[pl.BlockSpec(memory_space=pltpu.SMEM)] + [WHOLE] * (count + 4) + [ANY],
        out_specs=[
            pl.BlockSpec((1, 3, SHARE, D), lambda i: (0, 0, 0, 0)),
            whole((5, SHARE)),
            whole((5, SHARE)),
            whole((2, CHUNKS * SHARE)),
            whole((2, SHARE)),
        ],
        out_shape=[
            sds(qkv.shape, F32),
            sds((5, SHARE), F32),
            sds((5, SHARE), F32),
            sds((2, CHUNKS * SHARE), F32),
            sds((2, SHARE), F32),
        ],
        scratch_shapes=[pltpu.VMEM((ROWS_K, D), F32)],
        input_output_aliases={count + 5: 0},
        compiler_params=PARAMS,
        name="finish_token",
    )(meta, *pieces, weights, gain, shift, lines, qkv)


def unpack(left_a, right_a, left_b, right_b, whole_k):
    sides_a, sides_b = (left_a, right_a), (left_b, right_b)

    def up(sides):
        return jnp.concatenate(
            [x[c * SHARE : c * SHARE + SHARE] for x in sides for c in range(CHUNKS)], 1
        )

    def rows(sides, at, span=SHARE):
        return jnp.concatenate([x[at : at + span] for x in sides], 1)

    q1, k1, v1, out1 = (rows(sides_a, ROWS_F + i * SHARE) for i in range(4))
    out0 = rows(sides_b, 2 * SPAN)
    k0, v0, q0 = (whole_k[i * SHARE : i * SHARE + SHARE] for i in range(3))
    return (
        jnp.stack([jnp.stack([q0, k0, v0]), jnp.stack([q1, k1, v1])]).astype(F32),
        jnp.stack([out0, out1]).astype(F32),
        jnp.stack([up(sides_b), up(sides_a)]).astype(F32),
        jnp.stack([rows(sides_b, SPAN, SPAN), rows(sides_a, SPAN, SPAN)]).astype(F32),
    )


def per_device(size, seq, *args):
    (
        latents_in,
        inputs,
        clip_frames,
        text_mask,
        qkv_weight,
        out_weight,
        mlp_in,
        mlp_out,
        norm_gain,
        norm_bias,
        bias_in,
        bias_out,
        out_cotangent,
    ) = args
    micro, clips, nlat, _ = latents_in.shape
    count = micro * clips
    local = inputs.shape[2]
    padded = -(-local // 128) * 128
    rows = count * nlat
    s = lax.axis_index("seq")
    fsdp = lax.axis_index("fsdp")
    special = size == OWNERS
    meta = jnp.stack([fsdp if special else jnp.int32(0), s, s % 2]).astype(jnp.int32)
    lat = latents_in.reshape(rows, D)
    tokens = inputs.reshape(count, local, D)
    g4 = out_cotangent.reshape(rows, D)

    place = s * local + jnp.arange(padded, dtype=jnp.int32)
    frames = clip_frames.reshape(count, 1) * PATCHES
    text = text_mask.reshape(count, -1) > 0
    text_len = text.shape[1]
    slots = FRAMES * PATCHES
    wide = jnp.pad(text, ((0, 0), (slots, padded)))
    text_here = lax.dynamic_slice_in_dim(wide, s * local, padded, 1)
    valid = jnp.where(place[None] < slots, place[None] < frames, text_here)
    valid = valid & (jnp.arange(padded)[None] < local)
    bias = jnp.where(valid, 0.0, -1e30).astype(F32)
    mask = jnp.broadcast_to(bias[:, :, None], (count, padded, 128))

    def slabs(up):
        return up.reshape(SHARE, CHUNKS, D).transpose(1, 0, 2).reshape(SPAN, D)

    def pack_keyval(qkv, out, up, down, gain, shift, up_b, down_b):
        small = jnp.concatenate(
            [
                jnp.pad(jnp.concatenate([gain, shift, down_b], 0), ((0, 0), (0, 128 - SHARE))),
                up_b.reshape(6, 128),
                jnp.zeros((14, 128), BF),
            ],
            0,
        )
        small = jnp.concatenate([small[:16], small[16:]], 1)
        small = jnp.pad(small, ((0, 0), (0, D - 256)))
        return jnp.concatenate([qkv[0, 1], qkv[0, 2], qkv[0, 0], small], 0)

    def pack_first(qkv, out, up, down, *rest):
        return jnp.concatenate([out[0], slabs(up[0]), down[0]], 0)

    def pack_last(qkv, out, up, down, *rest):
        return jnp.concatenate([qkv[1].reshape(3 * SHARE, D), out[1], slabs(up[1]), down[1]], 0)

    packers = (pack_keyval, pack_first, pack_last)
    weights = (qkv_weight, out_weight, mlp_in, mlp_out, norm_gain, norm_bias, bias_in, bias_out)
    axes = (2, 1, 1, 1, 1, 1, 1, 1)
    def shift_to(x, k):
        return lax.ppermute(x, "seq", [(i, (i + k) % seq) for i in range(seq)])

    def scatter_rows(x):
        step = x.shape[0] // seq
        out = []
        for k in range(1, seq):
            piece = lax.dynamic_slice_in_dim(x, ((s + k) % seq) * step, step, 0)
            out.append(shift_to(piece, k))
        return out

    def gather_rows(x):
        return [x] + [shift_to(x, k) for k in range(1, seq)]

    pair = [(i, i ^ 1) for i in range(seq)]

    if special:
        def direct(x):
            return {0: x, 2: exchange(x, 2), 4: exchange(x, 4), 6: exchange(x, 6)}

        def direct_pack(p, later):
            arrays = [p[m] if m % 2 == 0 else exchange(later(p[m - 1]), 1) for m in range(OWNERS)]
            return Pack(arrays, lambda m, row: (m, None, row))

        def relay_pack(parts):
            half = parts[3].shape[0]
            arrays = []
            for x in parts:
                arrays += [x, exchange(x, 1)]

            def where(m, row):
                if m < 6:
                    return (m, None, row)
                return (m, None, row) if row < half else (m + 2, None, row - half)

            return Pack(arrays, where)

        x1 = pack_keyval(*weights)
        p1 = direct(x1)
        x3 = pack_last(*after(weights, x1))
        x3_2, x3_4 = exchange(x3, 2), exchange(x3, 4)
        bias, tokens = after((bias, tokens), x3)
        g1 = direct_pack(p1, lambda x: after(x, p1[2]))
        xl, k, v, gb, bins = keyval(g1, meta, tokens, local, padded)
        mask = after(mask, k)
        pay, q = attend(g1, meta, lat, gb, bias[:, None, :], k, v)
        pay = pay.reshape(rows, PAY)
        arrived = scatter_rows(pay)
        x2 = pack_first(*after(weights, k))
        x3_2, x3_4, x2 = after((x3_2, x3_4, x2), pay)
        half = x3.shape[0] // 2
        turn_2, turn_4 = x3_2[:half], x3_4[half:]
        x2_2, x2_4 = exchange(x2, 2), exchange(x2, 4)
        share = combine(meta, pay, arrived)
        parts = gather_rows(share)
        turn_2, turn_4, x2_2, x2_4 = after((turn_2, turn_4, x2_2, x2_4), parts)
        half = SHARE + SPAN
        x2_6a, x2_6b = exchange(x2_2[:half], 4), exchange(x2_4[half:], 2)
        g2 = relay_pack([x2, x2_2, x2_4, x2_6a, x2_6b])
        x3_6a, x3_6b = exchange(turn_2, 4), exchange(turn_4, 2)
        o, l, z1, z2, hidden = first_block(g2, meta, parts, lat, gb, bins)
        x3_6a, x3_6b = after((x3_6a, x3_6b), z2)
        g34 = relay_pack([x3, x3_2, x3_4, x3_6a, x3_6b])
    else:
        full = []
        for w, axis in zip(weights, axes):
            whole = lax.all_gather(w, "fsdp", axis=axis, tiled=True)
            shape = whole.shape
            parts = whole.reshape(*shape[:axis], OWNERS, shape[axis] // OWNERS, *shape[axis + 1 :])
            full.append(jnp.moveaxis(parts, axis, 0))
        raw = [jax.vmap(packer)(*full) for packer in packers]
        g1, g2, g34 = [Pack([x], lambda m, row: (0, m, row)) for x in raw]
        xl, k, v, gb, bins = keyval(g1, meta, tokens, local, padded)
        pay, q = attend(g1, meta, lat, gb, bias[:, None, :], k, v)
        pay = pay.reshape(rows, PAY)
        share = combine(meta, pay, scatter_rows(pay))
        o, l, z1, z2, hidden = first_block(g2, meta, gather_rows(share), lat, gb, bins)
    out, g3, qkv2, o2, keep_a, send_a = second_block(g34, meta, z2, g4, gb, bins)

    g2_lat, keep_a, send_a = third_block(g34, meta, g3, z2, o2, qkv2, gb, keep_a, send_a)
    grad_one, du, dl, keep_b, send_b = fourth_block(g2, meta, g2_lat, z1, o, l, gb, hidden)
    cube = lambda x: x.reshape(count, nlat, x.shape[-1])
    shapes = (latents_in.shape, inputs.shape)
    if special:
        recv_a, recv_b = exchange(send_a, 1), exchange(send_b, 1)
        split_a = split(*after((keep_a, recv_a), du))
        split_b = split(*after((keep_b, recv_b), *split_a))
        du, dl = after((du, dl), *split_a, *split_b)
        dk, dv, dq = attend_back(cube(q), cube(du), cube(dl), mask, k, v)
        dq = dq.reshape(rows, D)
        first_a = (*split_a[:2], exchange(split_a[2], 2), exchange(split_a[3], 4))
        first_b = (*split_b[:2], exchange(split_b[2], 2), exchange(split_b[3], 4))
        first_a = after(first_a, dq)
        dq_parts = scatter_rows(dq)
        keep_k, send_k, sums = keyval_grad(meta, *after((xl, dk, dv), first_a[2]))
        turn_a = turn(*after(first_a, sums))
        turn_b = turn(*after(first_b, sums))
        dq, dq_parts = after((dq, dq_parts), *turn_a, *turn_b)
        back, keep_k, send_k = query_grad(g1, meta, dq, dq_parts, lat, gb, sums, keep_k, send_k)
        recv_k = exchange(send_k, 1)
        mine_a = join(*after((turn_a[0], exchange(turn_a[1], 4), exchange(turn_a[2], 2)), back))
        mine_b = join(*after((turn_b[0], exchange(turn_b[1], 4), exchange(turn_b[2], 2)), back))
        fold_k = fold(*after((keep_k, recv_k), mine_a, mine_b))
        other_a = lax.ppermute(mine_a, "seq", pair)
        other_b = lax.ppermute(mine_b, "seq", pair)
        hop_k = [exchange(x, 2 * i) for i, x in enumerate(fold_k) if i]
        token_grads = token_grad(g1, meta, tokens, gb, *after((dk, dv), mine_a, mine_b, *fold_k))
        mine_k = sum_of(after([fold_k[0]] + hop_k, token_grads))
        back_rows = gather_rows(after(back, mine_k))
        own = lax.dynamic_slice_in_dim(mine_k, s * (ROWS_K // seq), ROWS_K // seq, 0)
        pieces = gather_rows(sum_of([own] + scatter_rows(mine_k)))
        lat_grad, qkv_grad, outw_grad, up_grad, down_grad, lines = finish_latent(
            meta, mine_a, other_a, mine_b, other_b, grad_one, back_rows
        )
        qkv_grad, gain_grad, shift_grad, bin_grad, bout_grad = finish_token(
            meta, pieces, qkv_weight[0, 1:3], norm_gain, norm_bias, lines, qkv_grad
        )
        return (
            out.reshape(shapes[0]),
            lat_grad.reshape(shapes[0]),
            token_grads.reshape(shapes[1]),
            qkv_grad,
            outw_grad,
            up_grad,
            down_grad,
            gain_grad,
            shift_grad,
            bin_grad,
            bout_grad,
        )

    dk, dv, dq = attend_back(cube(q), cube(du), cube(dl), mask, k, v)
    dq = dq.reshape(rows, D)
    keep_k, send_k, sums = keyval_grad(meta, xl, dk, dv)
    back, keep_k, send_k = query_grad(g1, meta, dq, scatter_rows(dq), lat, gb, sums, keep_k, send_k)
    token_grads = token_grad(g1, meta, tokens, gb, dk, dv)
    lat_grad = grad_one + place_rows(gather_rows(back), s, seq)
    mine_a, mine_b, mine_k = (
        sum_over_fsdp(*x) for x in ((keep_a, send_a), (keep_b, send_b), (keep_k, send_k))
    )

    def both(mine):
        other = lax.ppermute(mine, "seq", pair)
        return jnp.where(s % 2 == 0, mine, other), jnp.where(s % 2 == 0, other, mine)

    whole_k = lax.psum(mine_k.astype(F32), "seq")
    shares = (*both(mine_a), *both(mine_b), whole_k)
    wide = jax.vmap(unpack)(*shares)
    grads = []
    for x, w, axis in zip(wide, weights, axes):
        x = jnp.moveaxis(x, 0, axis)
        x = x.reshape(*x.shape[:axis], -1, *x.shape[axis + 2 :])
        grads.append(lax.dynamic_slice_in_dim(x, fsdp * w.shape[axis], w.shape[axis], axis))
    last = shares[0][0, 2 * SPAN : ROWS_F].astype(F32).reshape(-1, D)
    middle = shares[0][0, -VEC:].astype(F32).reshape(-1, D)
    early = shares[2][0, -VEC:].astype(F32).reshape(-1, D)
    vec_k = whole_k[0][-VEC_K:]
    step = norm_gain.shape[1]
    k0, v0 = grads[0][0, 1], grads[0][0, 2]
    own_k, own_v = qkv_weight[0, 1].astype(F32), qkv_weight[0, 2].astype(F32)
    own_gain, own_shift = norm_gain[1].astype(F32), norm_bias[1].astype(F32)
    db1 = jnp.sum(own_k * vec_k[0] + own_v * vec_k[1], -1)
    dg1 = (jnp.sum(own_k * k0 + own_v * v0, -1) - own_shift * db1) / own_gain
    lines = [vec_k[2], early[0], middle[0], last[0], vec_k[3], early[1], middle[1], last[1], early[2], last[2]]
    lines = jnp.stack(lines)
    cut = lax.dynamic_slice_in_dim(lines, fsdp * step, step, 1)
    wide_bias = jnp.stack([early[3:7].reshape(FF), last[3:7].reshape(FF)])
    return (
        out.reshape(shapes[0]),
        lat_grad.reshape(shapes[0]),
        token_grads.reshape(shapes[1]),
        *grads,
        jnp.stack([cut[0], dg1, cut[1], cut[2], cut[3]]),
        jnp.stack([cut[4], db1, cut[5], cut[6], cut[7]]),
        lax.dynamic_slice_in_dim(wide_bias, fsdp * bias_in.shape[1], bias_in.shape[1], 1),
        cut[8:10],
    )


def place_rows(pieces, s, seq):
    step = pieces[0].shape[0]
    whole = jnp.zeros((seq * step, *pieces[0].shape[1:]), F32)
    for k, piece in enumerate(pieces):
        at = ((s - k) % seq) * step
        whole = lax.dynamic_update_slice_in_dim(whole, piece.astype(F32), at, 0)
    return whole


def solution(mesh):
    in_specs = (
        P(None, "fsdp", None, None),
        P(None, "fsdp", "seq", None),
        P(None, "fsdp"),
        P(None, "fsdp", None),
        P(None, None, "fsdp", None),
        P(None, "fsdp", None),
        P(None, "fsdp", None),
        P(None, "fsdp", None),
        P(None, "fsdp"),
        P(None, "fsdp"),
        P(None, "fsdp"),
        P(None, "fsdp"),
        P(None, "fsdp", None, None),
    )
    out_specs = (
        P(None, "fsdp", None, None),
        P(None, "fsdp", None, None),
        P(None, "fsdp", "seq", None),
        P(None, None, "fsdp", None),
        P(None, "fsdp", None),
        P(None, "fsdp", None),
        P(None, "fsdp", None),
        P(None, "fsdp"),
        P(None, "fsdp"),
        P(None, "fsdp"),
        P(None, "fsdp"),
    )
    step = functools.partial(per_device, mesh.shape["fsdp"], mesh.shape["seq"])
    return jax.shard_map(step, mesh=mesh, in_specs=in_specs, out_specs=out_specs, check_vma=False)
```

```python
import functools

import jax
import jax.numpy as jnp
from jax import lax
from jax.experimental import pallas as pl
from jax.experimental.layout import Layout, with_layout_constraint
from jax.experimental.pallas import tpu as pltpu
from jax.sharding import PartitionSpec as P

D = 768
HEADS = 12
HEAD = 64
PAIRS = HEADS // 2
FF = 3072
NLAT = 128
PATCHES = 392
FRAMES = 16
OWNERS = 8
SHARE = D // OWNERS
CHUNKS = FF // D
HALF = D // 2
PAY = D + 128
KEYVAL_ROWS = 208
FORWARD_PAIRS = 3
BACK_PAIRS = 2
TOKEN_TILES = 2
GRAD_TILES = 1
TOKEN_ROWS = 416
VEC = 16
VEC_B = 32
VEC_K = 32
SPAN = CHUNKS * SHARE
ROWS_F = 2 * SPAN + VEC
ROWS_A = ROWS_F + 4 * SHARE + VEC
ROWS_B = 2 * SPAN + SHARE + VEC_B
ROWS_K = 3 * SHARE + VEC_K
EPS = 1e-06
F32 = jnp.float32
BF = jnp.bfloat16
GELU_C = 0.7978845608028654
GELU_A = 0.044715
VMEM_CAP = 60 * 1024 * 1024


def nn(a, b):
    return lax.dot_general(a, b, (((1,), (0,)), ((), ())), preferred_element_type=F32)


def nt(a, b):
    return lax.dot_general(a, b, (((1,), (1,)), ((), ())), preferred_element_type=F32)


def tn(a, b):
    return lax.dot_general(a, b, (((0,), (0,)), ((), ())), preferred_element_type=F32)


def ln_parts(x):
    center = x - jnp.mean(x, -1, keepdims=True)
    rstd = lax.rsqrt(jnp.mean(center * center, -1, keepdims=True) + EPS)
    return center, rstd


def ln(x, gain, bias):
    center, rstd = ln_parts(x)
    return center * rstd * gain + bias


def ln_back(x, gain, grad):
    center, rstd = ln_parts(x)
    xhat = center * rstd
    dx = grad * gain
    back = rstd * (dx - jnp.mean(dx, -1, keepdims=True) - xhat * jnp.mean(dx * xhat, -1, keepdims=True))
    return back, grad * xhat


def gelu(h):
    return h * (0.5 * (1.0 + jnp.tanh(GELU_C * (h + GELU_A * h * h * h))))


def gelu_both(h):
    square = h * h
    t = jnp.tanh(GELU_C * (h + GELU_A * h * square))
    cdf = 0.5 * (1.0 + t)
    slope = cdf + 0.5 * h * (1.0 - t * t) * (GELU_C * (1.0 + 3.0 * GELU_A * square))
    return h * cdf, slope


def low_lanes(rows):
    return lax.broadcasted_iota(jnp.int32, (rows, 128), 1) < HEAD


def block_diag(pair):
    wide = pair.astype(F32)
    low = low_lanes(pair.shape[0])
    return jnp.concatenate([jnp.where(low, wide, 0.0), jnp.where(low, 0.0, wide)], 0).astype(BF)


def diag_of(both):
    rows = both.shape[0] // 2
    return jnp.where(low_lanes(rows), both[:rows], both[rows:])


class Pack:
    def __init__(self, arrays, where):
        self.arrays, self.where = arrays, where

    def start(self, refs, row, rows, place, f, sem, shares=range(OWNERS)):
        for m in shares:
            index, lead, first = self.where(m, row)
            src = refs[index] if lead is None else refs[index].at[lead]
            pltpu.make_async_copy(src.at[pl.ds(first, rows)], place(f ^ m), sem).start()


def wait_for(ref, sem):
    pltpu.make_async_copy(ref, ref, sem).wait()


def share_rows(ref, g, first=0, span=SHARE, step=SHARE):
    return ref.at[pl.ds(pl.multiple_of(g * step + first, SHARE), span)]


def start_square(pack, refs, row, dst, f, sem):
    pack.start(refs, row, SHARE, lambda g: share_rows(dst, g), f, sem)


def start_up(pack, refs, row, dst, f, sems):
    for t in range(CHUNKS):
        lanes = pl.ds(t * D, D)
        pack.start(
            refs,
            row + t * SHARE,
            SHARE,
            lambda g, lanes=lanes: dst.at[pl.ds(pl.multiple_of(g * SHARE, SHARE), SHARE), lanes],
            f,
            sems.at[t],
        )


def start_down(pack, refs, row, dst, f, sems):
    for i in range(CHUNKS):
        for t in range(CHUNKS):
            pack.start(
                refs,
                row + t * SHARE,
                SHARE,
                lambda g, t=t: share_rows(dst, g, t * SHARE, SHARE, SPAN),
                f,
                sems.at[i],
                (2 * i, 2 * i + 1),
            )


def chunk_at(f, i):
    return pl.ds(pl.multiple_of(((f >> 1) ^ i) * D, D), D)


ANY = pl.BlockSpec(memory_space=pl.ANY)
WHOLE = pl.BlockSpec(memory_space=pltpu.VMEM)


def sds(shape, dtype):
    return jax.ShapeDtypeStruct(shape, dtype)


def cost(flops, size, exps=0):
    return pl.CostEstimate(flops=1, bytes_accessed=1, transcendentals=0)


PARAMS = pltpu.CompilerParams(vmem_limit_bytes=VMEM_CAP)


def keyval_kernel(pack, local, tile, meta, x_ref, *refs):
    count = len(pack.arrays)
    wrefs, (xl_ref, k_ref, v_ref, gb_ref, bin_ref, wkv, small, sems) = refs[:count], refs[count:]
    f = meta[0]

    @pl.when((pl.program_id(0) == 0) & (pl.program_id(1) == 0))
    def _():
        for m in range(OWNERS):
            index, lead, first = pack.where(m, 3 * SHARE)
            src = wrefs[index] if lead is None else wrefs[index].at[lead]
            pltpu.make_async_copy(
                src.at[pl.ds(first, 16), pl.ds(0, 256)], small.at[m], sems.at[2]
            ).start()
        start_square(pack, wrefs, 0, wkv.at[0], f, sems.at[0])
        start_square(pack, wrefs, SHARE, wkv.at[1], f, sems.at[1])
        wait_for(small, sems.at[2])
        lane = lax.broadcasted_iota(jnp.int32, (128, D), 1)
        row = lax.broadcasted_iota(jnp.int32, (128, D), 0)
        total = jnp.zeros((16, D), F32)
        for m in range(OWNERS):
            g = f ^ m
            place = jnp.where((lane - g * SHARE == row) & (row < SHARE), 1.0, 0.0).astype(BF)
            total = total + nn(small[m, :, 0:128], place)
            wide = small[m].astype(F32)
            for u in range(6):
                i, part = u // 3, u % 3
                line = wide[12 + u : 13 + u, 0:128] if u < 4 else wide[u - 4 : u - 3, 128:256]
                at = pl.ds(pl.multiple_of((3 * g + part) * 128, 128), 128)
                bin_ref[i : i + 1, at] = line
        gb_ref[...] = total
        wait_for(wkv.at[0], sems.at[0])
        wait_for(wkv.at[1], sems.at[1])

    for first in range(0, tile, KEYVAL_ROWS):
        part = slice(first, first + KEYVAL_ROWS)
        normed = ln(x_ref[0, part, :].astype(F32), gb_ref[1:2], gb_ref[6:7])
        row = lax.broadcasted_iota(jnp.int32, (KEYVAL_ROWS, D), 0)
        row = row + (pl.program_id(1) * tile + first)
        xl = jnp.where(row < local, normed, 0.0).astype(BF)
        xl_ref[0, part, :] = xl
        k_ref[0, part, :] = nn(xl, wkv[0]).astype(BF)
        v_ref[0, part, :] = nn(xl, wkv[1]).astype(BF)


def keyval(pack, meta, tokens, local, padded):
    clips = tokens.shape[0]
    tile = padded // 2
    block = pl.BlockSpec((1, tile, D), lambda i, j, m: (i, j, 0))
    fixed = lambda shape: pl.BlockSpec(shape, lambda i, j, m: (0,) * len(shape))
    return pl.pallas_call(
        functools.partial(keyval_kernel, pack, local, tile),
        grid_spec=pltpu.PrefetchScalarGridSpec(
            num_scalar_prefetch=1,
            grid=(clips, padded // tile),
            in_specs=[block] + [ANY] * len(pack.arrays),
            out_specs=[block, block, block, fixed((16, D)), fixed((2, FF))],
            scratch_shapes=[
                pltpu.VMEM((2, D, D), BF),
                pltpu.VMEM((OWNERS, 16, 256), BF),
                pltpu.SemaphoreType.DMA((3,)),
            ],
        ),
        out_shape=[sds((clips, padded, D), BF)] * 3 + [sds((16, D), F32), sds((2, FF), F32)],
        compiler_params=PARAMS,
        cost_estimate=cost(4 * clips * padded * D * D, clips * padded * D * 8),
        name="keyval",
    )(meta, tokens, *pack.arrays)


def attend_kernel(pack, padded, meta, lat_ref, gb_ref, bias_ref, k_ref, v_ref, *refs):
    count = len(pack.arrays)
    wrefs, (pay_ref, q_ref, wq, qs, lv, sem) = refs[:count], refs[count:]
    f = meta[0]
    clip, group = pl.program_id(0), pl.program_id(1)

    @pl.when((clip == 0) & (group == 0))
    def _():
        start_square(pack, wrefs, 2 * SHARE, wq, f, sem.at[0])
        zl = ln(lat_ref[...].astype(F32), gb_ref[0:1], gb_ref[5:6]).astype(BF)
        wait_for(wq, sem.at[0])
        q = nn(zl, wq[...]).astype(BF).astype(F32) * 0.125
        qs[...] = q.astype(BF)
        q_ref[...] = qs[...]

    rows = pl.ds(pl.multiple_of(clip * NLAT, NLAT), NLAT)
    lane = lax.broadcasted_iota(jnp.int32, (NLAT, 128), 1)
    new = jnp.where(group == 0, 0.0, lv[...])
    for p in range(FORWARD_PAIRS):
        pair = group * FORWARD_PAIRS + p
        at = pl.ds(pl.multiple_of(pair * 128, 128), 128)
        mine = slice(p * 128, p * 128 + 128)
        e = jnp.exp(nt(block_diag(qs[rows, at]), k_ref[0, :, mine]) + bias_ref[0])
        pay_ref[0, :, at] = diag_of(nn(e.astype(BF), v_ref[0, :, mine])).astype(BF)
        l = jnp.sum(e, -1, keepdims=True)
        new = jnp.where(lane == 2 * pair, l[:NLAT], jnp.where(lane == 2 * pair + 1, l[NLAT:], new))
    lv[...] = new

    @pl.when(group == PAIRS // FORWARD_PAIRS - 1)
    def _():
        pay_ref[0, :, D:PAY] = split_pair(lv[...])


def split_pair(values):
    high = values.astype(BF).astype(F32)
    rest = values - high
    return jnp.where(low_lanes(values.shape[0]), high, pltpu.roll(rest, HEAD, 1)).astype(BF)


def join_pair(pay):
    wide = pay.astype(F32)
    return wide + pltpu.roll(wide, HEAD, 1)


def attend(pack, meta, lat, gb, bias, k, v):
    clips, padded = k.shape[0], k.shape[1]
    rows = lat.shape[0]
    fixed = lambda shape: pl.BlockSpec(shape, lambda i, j, m: (0,) * len(shape))
    lanes = pl.BlockSpec((1, padded, 128 * FORWARD_PAIRS), lambda i, j, m: (i, 0, j))
    return pl.pallas_call(
        functools.partial(attend_kernel, pack, padded),
        grid_spec=pltpu.PrefetchScalarGridSpec(
            num_scalar_prefetch=1,
            grid=(clips, PAIRS // FORWARD_PAIRS),
            in_specs=[
                fixed((rows, D)),
                fixed((16, D)),
                pl.BlockSpec((1, 1, padded), lambda i, j, m: (i, 0, 0)),
                lanes,
                lanes,
            ]
            + [ANY] * len(pack.arrays),
            out_specs=[
                pl.BlockSpec((1, NLAT, PAY), lambda i, j, m: (i, 0, 0)),
                fixed((rows, D)),
            ],
            scratch_shapes=[
                pltpu.VMEM((D, D), BF),
                pltpu.VMEM((rows, D), BF),
                pltpu.VMEM((NLAT, 128), F32),
                pltpu.SemaphoreType.DMA((1,)),
            ],
        ),
        out_shape=[sds((clips, NLAT, PAY), BF), sds((rows, D), BF)],
        compiler_params=PARAMS,
        cost_estimate=cost(
            8 * clips * padded * NLAT * D, clips * padded * D * 4, clips * padded * NLAT * HEADS
        ),
        name="attend",
    )(meta, lat, gb, bias, k, v, *pack.arrays)


def combine_kernel(*refs):
    parts, out_ref = refs[1:-1], refs[-1]
    total = parts[0][...].astype(F32)
    for part in parts[1:]:
        total = total + part[...].astype(F32)
    l = total[:, D:PAY]
    l = l + pltpu.roll(l, HEAD, 1)
    low = low_lanes(total.shape[0])
    for j in range(PAIRS):
        den = jnp.where(low, l[:, 2 * j : 2 * j + 1], l[:, 2 * j + 1 : 2 * j + 2])
        out_ref[:, 128 * j : 128 * j + 128] = (total[:, 128 * j : 128 * j + 128] / den).astype(BF)
    out_ref[:, D:PAY] = split_pair(l)


def combine(meta, pay, received):
    rows = received[0].shape[0] if received else pay.shape[0]
    fixed = pl.BlockSpec((rows, PAY), lambda i, m: (0, 0))
    return pl.pallas_call(
        combine_kernel,
        grid_spec=pltpu.PrefetchScalarGridSpec(
            num_scalar_prefetch=1,
            grid=(1,),
            in_specs=[pl.BlockSpec((rows, PAY), lambda i, m: (m[1], 0))] + [fixed] * len(received),
            out_specs=fixed,
        ),
        out_shape=sds((rows, PAY), BF),
        name="combine",
    )(meta, pay, *received)


def first_kernel(pack, count, meta, *refs):
    parts = refs[:count]
    lat_ref, gb_ref, bin_ref = refs[count : count + 3]
    refs = refs[count + 3 :]
    wrefs, refs = refs[: len(pack.arrays)], refs[len(pack.arrays) :]
    o_ref, l_ref, z1_ref, z2_ref, h_ref, wo, win, wout, hs, sems, hsems = refs
    f, s = meta[0], meta[1]
    start_square(pack, wrefs, 0, wo, f, sems.at[0])
    start_up(pack, wrefs, SHARE, win, f, sems.at[pl.ds(1, CHUNKS)])
    start_down(pack, wrefs, SHARE + SPAN, wout, f, sems.at[pl.ds(1 + CHUNKS, CHUNKS)])
    step = parts[0].shape[0]
    for k, part in enumerate(parts):
        rows = pl.ds(pl.multiple_of(lax.rem(s - k + count, count) * step, step), step)
        o_ref[rows, :] = part[:, :D]
        l_ref[rows, :] = join_pair(part[:, D:PAY])
    wait_for(wo, sems.at[0])
    z1 = lat_ref[...].astype(F32) + nn(o_ref[...], wo[...])
    z1_ref[...] = z1
    n = ln(z1, gb_ref[2:3], gb_ref[7:8]).astype(BF)
    y = jnp.zeros_like(z1)
    copies = []
    for i in range(CHUNKS):
        at = chunk_at(f, i)
        wait_for(win.at[:, at], sems.at[1 + ((f >> 1) ^ i)])
        h = nn(n, win[:, at]) + bin_ref[0:1, at]
        hs[:, at] = h
        copies.append(pltpu.make_async_copy(hs.at[:, at], h_ref.at[:, at], hsems.at[i]))
        copies[-1].start()
        a = gelu(h).astype(BF)
        wait_for(wout.at[at], sems.at[1 + CHUNKS + i])
        y = y + nn(a, wout[at, :])
    z2_ref[...] = z1 + (y + gb_ref[10:11])
    for copy in copies:
        copy.wait()


def first_block(pack, meta, parts, lat, gb, bins):
    rows = lat.shape[0]
    n_w = len(pack.arrays)
    return pl.pallas_call(
        functools.partial(first_kernel, pack, len(parts)),
        in_specs=[pl.BlockSpec(memory_space=pltpu.SMEM)] + [WHOLE] * (len(parts) + 3) + [ANY] * n_w,
        out_specs=[WHOLE] * 4 + [ANY],
        scratch_shapes=[
            pltpu.VMEM((D, D), BF),
            pltpu.VMEM((D, FF), BF),
            pltpu.VMEM((FF, D), BF),
            pltpu.VMEM((rows, FF), F32),
            pltpu.SemaphoreType.DMA((1 + 2 * CHUNKS,)),
            pltpu.SemaphoreType.DMA((CHUNKS,)),
        ],
        out_shape=[
            sds((rows, D), BF),
            sds((rows, 128), F32),
            sds((rows, D), F32),
            sds((rows, D), F32),
            sds((rows, FF), F32),
        ],
        compiler_params=PARAMS,
        cost_estimate=cost(18 * rows * D * D, 16 * D * D * 2),
        name="first_block",
    )(meta, *parts, lat, gb, bins, *pack.arrays)


def softmax_rows(scores):
    e = jnp.exp(scores - jnp.max(scores, -1, keepdims=True))
    return e / jnp.sum(e, -1, keepdims=True)


def put_vec(shares, rows, row, width):
    vec = jnp.concatenate(rows + [jnp.zeros((width - len(rows), HALF), F32)], 0).astype(BF)
    for which in range(2):
        for k in range(4):
            shares[which, k, row : row + width, :] = vec


def halves(line):
    return [line[:, i : i + HALF] for i in range(0, line.shape[1], HALF)]


def column_sum(values):
    return jnp.sum(values, 0, keepdims=True)


def put_rows(shares, f, row, grad, first=0):
    grad = grad.astype(BF)
    for g in range(OWNERS):
        rel = f ^ g
        shares[rel & 1, rel >> 1, row : row + SHARE, :] = grad[g * SHARE : g * SHARE + SHARE]


def put_down(shares, f, row, grad, u):
    grad = grad.astype(BF)
    span = CHUNKS * SHARE
    for i in range(D // span):
        rel = f ^ (u * (D // span) + i)
        shares[rel & 1, rel >> 1, row : row + span, :] = grad[i * span : i * span + span]


def ff_grads(shares, f, h, row, n, dh_ref, a_ref, dy_ref):
    for c in range(CHUNKS):
        at = pl.ds(pl.multiple_of(h * (FF // 2) + c * HALF, 128), HALF)
        put_rows(shares, f, row + c * SHARE, tn(n, dh_ref[:, at]))
    dyh = dy_ref[:, pl.ds(pl.multiple_of(h * HALF, 128), HALF)]
    for u in range(CHUNKS):
        put_down(shares, f, row + CHUNKS * SHARE, tn(a_ref[:, u * D : u * D + D], dyh), u)


def share_copies(shares, keep_ref, send_ref, first, rows, sems):
    at = pl.ds(first, rows)
    return [
        pltpu.make_async_copy(shares.at[which, k, at], ref.at[k, at], sems.at[which, k])
        for which, ref in ((0, keep_ref), (1, send_ref))
        for k in range(4)
    ]


def start_all(copies):
    for copy in copies:
        copy.start()


def wait_all(copies):
    for copy in copies:
        copy.wait()


def second_kernel(pack, meta, z2_ref, g4_ref, gb_ref, bin_ref, *refs):
    count = len(pack.arrays)
    wrefs, (out_ref, g2_ref, keep_ref, send_ref) = refs[:count], refs[count : count + 4]
    wqkv, wo, win, wout, qkv, o2, probs, hs, ac, dhs, dqkv, dab, dob, shares, sems, osems = refs[count + 4 :]
    f, h = meta[0], meta[2]
    for j in range(3):
        start_square(pack, wrefs, j * SHARE, wqkv.at[j], f, sems.at[j])
    start_square(pack, wrefs, 3 * SHARE, wo, f, sems.at[3])
    start_up(pack, wrefs, 4 * SHARE, win, f, sems.at[pl.ds(4, CHUNKS)])
    start_down(pack, wrefs, 4 * SHARE + SPAN, wout, f, sems.at[pl.ds(4 + CHUNKS, CHUNKS)])
    z2 = z2_ref[...]
    m = ln(z2, gb_ref[3:4], gb_ref[8:9]).astype(BF)
    for j in range(3):
        wait_for(wqkv.at[j], sems.at[j])
        qkv[j] = nn(m, wqkv[j]).astype(BF)
    tiles = []
    for clip in range(z2.shape[0] // NLAT):
        for pair in range(PAIRS):
            tiles.append((slice(clip * NLAT, clip * NLAT + NLAT), slice(pair * 128, pair * 128 + 128)))
    for i, (rows, at) in enumerate(tiles):
        p = softmax_rows(nt(block_diag(qkv[0, rows, at]), qkv[1, rows, at]) * 0.125)
        probs[i] = p
        o2[rows, at] = diag_of(nn(p.astype(BF), qkv[2, rows, at])).astype(BF)
    wait_for(wo, sems.at[3])
    z3 = z2 + nn(o2[...], wo[...])
    n = ln(z3, gb_ref[4:5], gb_ref[9:10]).astype(BF)
    y = jnp.zeros_like(z3)
    for c in range(CHUNKS):
        wait_for(win.at[:, c * D : c * D + D], sems.at[4 + c])
    for i in range(CHUNKS):
        wait_for(wout.at[chunk_at(f, i)], sems.at[4 + CHUNKS + i])
    for i in range(CHUNKS):
        at = slice(i * D, i * D + D)
        act, slope = gelu_both(nn(n, win[:, at]) + bin_ref[1:2, at])
        hs[:, at] = slope
        a = act.astype(BF)
        ac[:, at] = a
        y = y + nn(a, wout[at, :])
    out_ref[...] = z3 + (y + gb_ref[11:12])
    dy = g4_ref[...]
    dn = jnp.zeros_like(z3)
    dbin = []
    for c in range(CHUNKS):
        at = slice(c * D, c * D + D)
        dh = (nt(dy, wout[at, :]) * hs[:, at]).astype(BF)
        dhs[:, at] = dh
        dbin += halves(column_sum(dh.astype(F32)))
        dn = dn + nt(dh, win[:, at])
    back, dgain = ln_back(z3, gb_ref[4:5], dn)
    g4 = dy.astype(F32)
    g3 = g4 + back
    ff_grads(shares, f, h, 0, n, dhs, ac, g4_ref)
    vec = halves(column_sum(dgain)) + halves(column_sum(dn)) + halves(column_sum(g4)) + dbin
    put_vec(shares, vec, 2 * SPAN, VEC)
    early = share_copies(shares, keep_ref, send_ref, 0, ROWS_F, osems.at[0])
    start_all(early)

    half = pl.ds(pl.multiple_of(h * HALF, 128), HALF)
    dab[...] = g3.astype(BF)
    dob[...] = nt(dab[...], wo[...]).astype(BF)
    put_rows(shares, f, ROWS_F + 3 * SHARE, tn(o2[...], dab[:, half]))
    for i, (rows, at) in enumerate(tiles):
        q, k, v = qkv[0, rows, at], qkv[1, rows, at], qkv[2, rows, at]
        p = probs[i]
        dobd = block_diag(dob[rows, at])
        dp = nt(dobd, v)
        ds = (p * (dp - jnp.sum(p * dp, -1, keepdims=True))).astype(BF)
        dqkv[0, rows, at] = (diag_of(nn(ds, k)) * 0.125).astype(BF)
        dqkv[1, rows, at] = (tn(ds, block_diag(q)) * 0.125).astype(BF)
        dqkv[2, rows, at] = tn(p.astype(BF), dobd).astype(BF)
    dm = jnp.zeros_like(g3)
    for j in range(3):
        dm = dm + nt(dqkv[j], wqkv[j])
        put_rows(shares, f, ROWS_F + j * SHARE, tn(m, dqkv[j, :, half]))
    back, dgain = ln_back(z2, gb_ref[3:4], dm)
    g2_ref[...] = g3 + back
    put_vec(shares, halves(column_sum(dgain)) + halves(column_sum(dm)), ROWS_F + 4 * SHARE, VEC)
    late = share_copies(shares, keep_ref, send_ref, ROWS_F, ROWS_A - ROWS_F, osems.at[1])
    start_all(late)
    wait_all(early + late)


def second_block(pack, meta, z2, g4, gb, bins):
    rows = z2.shape[0]
    square = pltpu.VMEM((rows, D), BF)
    return pl.pallas_call(
        functools.partial(second_kernel, pack),
        in_specs=[pl.BlockSpec(memory_space=pltpu.SMEM)] + [WHOLE] * 4 + [ANY] * len(pack.arrays),
        out_specs=[WHOLE] * 2 + [ANY] * 2,
        scratch_shapes=[
            pltpu.VMEM((3, D, D), BF),
            pltpu.VMEM((D, D), BF),
            pltpu.VMEM((D, FF), BF),
            pltpu.VMEM((FF, D), BF),
            pltpu.VMEM((3, rows, D), BF),
            square,
            pltpu.VMEM((rows // NLAT * PAIRS, 2 * NLAT, NLAT), F32),
            pltpu.VMEM((rows, FF), F32),
            pltpu.VMEM((rows, FF), BF),
            pltpu.VMEM((rows, FF), BF),
            pltpu.VMEM((3, rows, D), BF),
            square,
            square,
            pltpu.VMEM((2, 4, ROWS_A, HALF), BF),
            pltpu.SemaphoreType.DMA((4 + 2 * CHUNKS,)),
            pltpu.SemaphoreType.DMA((2, 2, 4)),
        ],
        out_shape=[
            sds((rows, D), F32),
            sds((rows, D), F32),
            sds((4, ROWS_A, HALF), BF),
            sds((4, ROWS_A, HALF), BF),
        ],
        compiler_params=PARAMS,
        cost_estimate=cost(0, 0),
        name="second_block",
    )(meta, z2, g4, gb, bins, *pack.arrays)


def fourth_kernel(pack, meta, g2_ref, z1_ref, o_ref, l_ref, gb_ref, h_ref, *refs):
    wrefs, refs = refs[: len(pack.arrays)], refs[len(pack.arrays) :]
    g1_ref, du_ref, dl_ref, keep_ref, send_ref = refs[:5]
    wo, win, wout, hs, ac, dhs, dab, dyb, shares, sems, osems = refs[5:]
    f, h = meta[0], meta[2]
    hcopy = pltpu.make_async_copy(h_ref, hs, sems.at[1])
    hcopy.start()
    start_down(pack, wrefs, SHARE + SPAN, wout, f, sems.at[pl.ds(2, CHUNKS)])
    start_up(pack, wrefs, SHARE, win, f, sems.at[pl.ds(2 + CHUNKS, CHUNKS)])
    start_square(pack, wrefs, 0, wo, f, sems.at[0])
    half = pl.ds(pl.multiple_of(h * HALF, 128), HALF)
    z1 = z1_ref[...]
    n = ln(z1, gb_ref[2:3], gb_ref[7:8]).astype(BF)
    g2 = g2_ref[...]
    dyb[...] = g2.astype(BF)
    hcopy.wait()
    for c in range(CHUNKS):
        at = slice(c * D, c * D + D)
        act, slope = gelu_both(hs[:, at])
        ac[:, at] = act.astype(BF)
        hs[:, at] = slope
    for i in range(CHUNKS):
        wait_for(wout.at[chunk_at(f, i)], sems.at[2 + i])
    for c in range(CHUNKS):
        wait_for(win.at[:, c * D : c * D + D], sems.at[2 + CHUNKS + c])
    dn = jnp.zeros_like(g2)
    dbin = []
    for c in range(CHUNKS):
        at = slice(c * D, c * D + D)
        dh = (nt(dyb[...], wout[at, :]) * hs[:, at]).astype(BF)
        dhs[:, at] = dh
        dbin += halves(column_sum(dh.astype(F32)))
        dn = dn + nt(dh, win[:, at])
    back, dgain = ln_back(z1, gb_ref[2:3], dn)
    g1 = g2 + back
    g1_ref[...] = g1
    ff_grads(shares, f, h, 0, n, dhs, ac, dyb)
    vec = halves(column_sum(dgain)) + halves(column_sum(dn))
    vec += halves(column_sum(dyb[...].astype(F32))) + dbin
    put_vec(shares, vec, 2 * SPAN + SHARE, VEC_B)

    dab[...] = g1.astype(BF)
    wait_for(wo, sems.at[0])
    do = nt(dab[...], wo[...]).astype(BF).astype(F32)
    put_rows(shares, f, 2 * SPAN, tn(o_ref[...], dab[:, half]))
    low = low_lanes(g2.shape[0])
    lane = lax.broadcasted_iota(jnp.int32, low.shape, 1)
    l = l_ref[...]
    dl = jnp.zeros(low.shape, F32)
    for j in range(PAIRS):
        at = slice(128 * j, 128 * j + 128)
        first, later = l[:, 2 * j : 2 * j + 1], l[:, 2 * j + 1 : 2 * j + 2]
        du_ref[:, at] = (do[:, at] / jnp.where(low, first, later)).astype(BF)
        t = do[:, at] * o_ref[:, at].astype(F32)
        t_first = -jnp.sum(jnp.where(low, t, 0.0), -1, keepdims=True) / first
        t_later = -jnp.sum(jnp.where(low, 0.0, t), -1, keepdims=True) / later
        dl = jnp.where(lane == 2 * j, t_first, jnp.where(lane == 2 * j + 1, t_later, dl))
    dl_ref[...] = dl
    late = share_copies(shares, keep_ref, send_ref, 0, ROWS_B, osems)
    start_all(late)
    wait_all(late)


def fourth_block(pack, meta, g2, z1, o, l, gb, hidden):
    rows = z1.shape[0]
    arrays = pack.arrays
    return pl.pallas_call(
        functools.partial(fourth_kernel, pack),
        in_specs=[pl.BlockSpec(memory_space=pltpu.SMEM)] + [WHOLE] * 5 + [ANY] * (1 + len(arrays)),
        out_specs=[WHOLE] * 3 + [ANY] * 2,
        scratch_shapes=[
            pltpu.VMEM((D, D), BF),
            pltpu.VMEM((D, FF), BF),
            pltpu.VMEM((FF, D), BF),
            pltpu.VMEM((rows, FF), F32),
            pltpu.VMEM((rows, FF), BF),
            pltpu.VMEM((rows, FF), BF),
            pltpu.VMEM((rows, D), BF),
            pltpu.VMEM((rows, D), BF),
            pltpu.VMEM((2, 4, ROWS_B, HALF), BF),
            pltpu.SemaphoreType.DMA((2 + 2 * CHUNKS,)),
            pltpu.SemaphoreType.DMA((2, 4)),
        ],
        out_shape=[
            sds((rows, D), F32),
            sds((rows, D), BF),
            sds((rows, 128), F32),
            sds((4, ROWS_B, HALF), BF),
            sds((4, ROWS_B, HALF), BF),
        ],
        compiler_params=PARAMS,
        cost_estimate=cost(30 * rows * D * D, 12 * D * D * 4),
        name="fourth_block",
    )(meta, g2, z1, o, l, gb, hidden, *arrays)


def attend_back_kernel(q_ref, du_ref, dl_ref, mask_ref, k_ref, v_ref, dk_ref, dv_ref, dq_ref, dlt):
    group = pl.program_id(1)

    @pl.when(group == 0)
    def _():
        dlt[...] = dl_ref[0].T

    mask = mask_ref[0]
    mask = jnp.concatenate([mask, mask], 1)
    upper = lax.broadcasted_iota(jnp.int32, (128, NLAT), 0) < HEAD
    for p in range(BACK_PAIRS):
        pair = group * BACK_PAIRS + p
        mine = slice(p * 128, p * 128 + 128)
        qbd, dubd = block_diag(q_ref[0, :, mine]), block_diag(du_ref[0, :, mine])
        line = [dlt[pl.ds(2 * pair + i, 1), :] for i in range(2)]
        k, v = k_ref[0, :, mine], v_ref[0, :, mine]
        e = jnp.exp(nt(k, qbd) + mask)
        ds = (e * (nt(v, dubd) + jnp.concatenate(line, 1))).astype(BF)
        dv_ref[0, :, mine] = nn(e.astype(BF), dubd).astype(BF)
        dk_ref[0, :, mine] = nn(ds, qbd).astype(BF)
        dqt = tn(k, ds)
        dqt = jnp.where(upper, dqt[:, :NLAT], dqt[:, NLAT:])
        dq_ref[0, :, mine] = (dqt.T * 0.125).astype(BF)


def attend_back(q, du, dl, mask, k, v):
    clips, padded = k.shape[0], k.shape[1]
    wide = 128 * BACK_PAIRS
    small = pl.BlockSpec((1, NLAT, wide), lambda i, j: (i, 0, j))
    whole = pl.BlockSpec((1, NLAT, 128), lambda i, j: (i, 0, 0))
    column = pl.BlockSpec((1, padded, 128), lambda i, j: (i, 0, 0))
    lanes = pl.BlockSpec((1, padded, wide), lambda i, j: (i, 0, j))
    return pl.pallas_call(
        attend_back_kernel,
        grid=(clips, PAIRS // BACK_PAIRS),
        in_specs=[small, small, whole, column, lanes, lanes],
        out_specs=[lanes, lanes, small],
        scratch_shapes=[pltpu.VMEM((128, NLAT), F32)],
        out_shape=[sds((clips, padded, D), BF)] * 2 + [sds((clips, NLAT, D), BF)],
        compiler_params=PARAMS,
        cost_estimate=cost(0, 0),
        name="attend_back",
    )(q, du, dl, mask, k, v)


def keyval_grad_kernel(meta, xl_ref, dk_ref, dv_ref, keep_ref, send_ref, sum_ref, acc, shares, sems):
    f = meta[0]
    step = pl.program_id(0)
    first = step == 0
    xt = xl_ref[0].T
    for j, ref in enumerate((dk_ref, dv_ref)):
        grad = nn(xt, ref[0])
        acc[j] = grad + jnp.where(first, 0.0, acc[j])
        line = column_sum(ref[0].astype(F32))
        sum_ref[j : j + 1, :] = line + jnp.where(first, 0.0, sum_ref[j : j + 1, :])

    @pl.when(step == pl.num_programs(0) - 1)
    def _():
        for j in range(2):
            for g in range(OWNERS):
                rel = f ^ g
                grad = acc[j, g * SHARE : g * SHARE + SHARE, :].astype(BF)
                shares[rel & 1, rel >> 1, j * SHARE : j * SHARE + SHARE, :] = grad
        copies = share_copies(shares, keep_ref, send_ref, 0, 2 * SHARE, sems)
        start_all(copies)
        wait_all(copies)


def keyval_grad(meta, xl, dk, dv):
    clips, padded = xl.shape[0], xl.shape[1]
    tile = padded // GRAD_TILES
    at = lambda i, m: (i // GRAD_TILES, lax.rem(i, GRAD_TILES), 0)
    block = pl.BlockSpec((1, tile, D), at)
    return pl.pallas_call(
        keyval_grad_kernel,
        grid_spec=pltpu.PrefetchScalarGridSpec(
            num_scalar_prefetch=1,
            grid=(clips * GRAD_TILES,),
            in_specs=[block] * 3,
            out_specs=[ANY, ANY, pl.BlockSpec((8, D), lambda i, m: (0, 0))],
            scratch_shapes=[
                pltpu.VMEM((2, D, D), F32),
                pltpu.VMEM((2, 4, 2 * SHARE, D), BF),
                pltpu.SemaphoreType.DMA((2, 4)),
            ],
        ),
        out_shape=[sds((4, ROWS_K, D), BF), sds((4, ROWS_K, D), BF), sds((8, D), F32)],
        compiler_params=PARAMS,
        cost_estimate=cost(4 * clips * padded * D * D, clips * padded * D * 6),
        name="keyval_grad",
    )(meta, xl, dk, dv)


def query_grad_kernel(pack, count, meta, *refs):
    own_ref, parts, refs = refs[0], refs[1:count], refs[count:]
    lat_ref, gb_ref, sum_ref, keep_in, send_in = refs[:5]
    refs = refs[5:]
    n_w = len(pack.arrays)
    wrefs, (back_ref, keep_ref, send_ref, wq, shares, sem, osems) = refs[:n_w], refs[n_w:]
    f = meta[0]
    start_square(pack, wrefs, 2 * SHARE, wq, f, sem.at[0])
    total = own_ref[...].astype(F32)
    for part in parts:
        total = total + part[...].astype(F32)
    dq = total.astype(BF)
    lat = lat_ref[...].astype(F32)
    zl = ln(lat, gb_ref[0:1], gb_ref[5:6]).astype(BF)
    grad = tn(zl, dq).astype(BF)
    for g in range(OWNERS):
        rel = f ^ g
        shares[rel & 1, rel >> 1, 0:SHARE, :] = grad[g * SHARE : g * SHARE + SHARE]
    wait_for(wq, sem.at[0])
    dzl = nt(dq, wq[...])
    back, dgain = ln_back(lat, gb_ref[0:1], dzl)
    back_ref[...] = back.astype(BF)
    lines = [sum_ref[0:1], sum_ref[1:2], column_sum(dgain), column_sum(dzl)]
    vec = jnp.concatenate(lines + [jnp.zeros((VEC_K - 4, D), F32)], 0).astype(BF)
    copies = []
    for which, ref in ((0, keep_ref), (1, send_ref)):
        for k in range(4):
            shares[which, k, SHARE : SHARE + VEC_K, :] = vec
            copies.append(
                pltpu.make_async_copy(
                    shares.at[which, k],
                    ref.at[k, pl.ds(2 * SHARE, SHARE + VEC_K)],
                    osems.at[which, k],
                )
            )
    for copy in copies:
        copy.start()
    for copy in copies:
        copy.wait()


def query_grad(pack, meta, dq, parts, lat, gb, sums, keep, send):
    rows = parts[0].shape[0] if parts else dq.shape[0]
    count = 1 + len(parts)
    mine = pl.BlockSpec((rows, D), lambda i, m: (m[1], 0))
    fixed = lambda shape: pl.BlockSpec(shape, lambda i, m: (0,) * len(shape))
    return pl.pallas_call(
        functools.partial(query_grad_kernel, pack, count),
        grid_spec=pltpu.PrefetchScalarGridSpec(
            num_scalar_prefetch=1,
            grid=(1,),
            in_specs=[mine]
            + [fixed((rows, D))] * len(parts)
            + [mine, fixed((16, D)), fixed((8, D)), ANY, ANY]
            + [ANY] * len(pack.arrays),
            out_specs=[fixed((rows, D)), ANY, ANY],
            scratch_shapes=[
                pltpu.VMEM((D, D), BF),
                pltpu.VMEM((2, 4, SHARE + VEC_K, D), BF),
                pltpu.SemaphoreType.DMA((1,)),
                pltpu.SemaphoreType.DMA((2, 4)),
            ],
        ),
        out_shape=[sds((rows, D), BF), sds(keep.shape, BF), sds(send.shape, BF)],
        input_output_aliases={count + 4: 1, count + 5: 2},
        compiler_params=PARAMS,
        name="query_grad",
    )(meta, dq, *parts, lat, gb, sums, keep, send, *pack.arrays)


def token_grad_kernel(pack, local, meta, x_ref, gb_ref, dk_ref, dv_ref, *refs):
    count = len(pack.arrays)
    wrefs, (out_ref, wkv, lines, sems, osems) = refs[:count], refs[count:]
    clip, at = pl.program_id(0), pl.program_id(1)
    clips, tiles = pl.num_programs(0), pl.num_programs(1)
    tile = x_ref.shape[1]
    n_clips, n_tiles = out_ref.shape[0] // (local * PAIRS), -(-local // tile)

    @pl.when((clip == 0) & (at == 0))
    def _():
        f = meta[0]
        start_square(pack, wrefs, 0, wkv.at[0], f, sems.at[0])
        start_square(pack, wrefs, SHARE, wkv.at[1], f, sems.at[1])
        wait_for(wkv.at[0], sems.at[0])
        wait_for(wkv.at[1], sems.at[1])

    for first in range(0, tile, TOKEN_ROWS):
        rows = slice(first, first + TOKEN_ROWS)
        grad = nt(dk_ref[0, rows, :], wkv[0]) + nt(dv_ref[0, rows, :], wkv[1])
        back, unused = ln_back(x_ref[0, rows, :].astype(F32), gb_ref[1:2], grad)
        base = (clip * local + at * tile + first) * PAIRS
        for t in range(PAIRS):
            lines[pl.ds(base + t, TOKEN_ROWS, stride=PAIRS), :] = back[:, 128 * t : 128 * t + 128]

    def piece(c, i):
        first = (c * local + i * tile) * PAIRS // 8 * 8
        last = (c * local + min((i + 1) * tile, local)) * PAIRS
        last = last if c == n_clips - 1 and i == n_tiles - 1 else last // 8 * 8
        where = pl.ds(first, last - first)
        slot = c * n_tiles + i
        return pltpu.make_async_copy(lines.at[where], out_ref.at[where], osems.at[slot])

    for c in range(n_clips):
        for i in range(n_tiles):

            @pl.when((clip == c) & (at == i))
            def _(c=c, i=i):
                piece(c, i).start()

    @pl.when((clip == n_clips - 1) & (at == n_tiles - 1))
    def _():
        for c in range(n_clips):
            for i in range(n_tiles):
                piece(c, i).wait()


def token_grad(pack, meta, tokens, gb, dk, dv):
    clips, local = tokens.shape[0], tokens.shape[1]
    padded = dk.shape[1]
    tile = padded // TOKEN_TILES
    block = pl.BlockSpec((1, tile, D), lambda i, j, m: (i, j, 0))
    rows = clips * local * PAIRS
    return pl.pallas_call(
        functools.partial(token_grad_kernel, pack, local),
        grid_spec=pltpu.PrefetchScalarGridSpec(
            num_scalar_prefetch=1,
            grid=(clips, padded // tile),
            in_specs=[block, pl.BlockSpec((16, D), lambda i, j, m: (0, 0)), block, block]
            + [ANY] * len(pack.arrays),
            out_specs=ANY,
            scratch_shapes=[
                pltpu.VMEM((2, D, D), BF),
                pltpu.VMEM((rows + (padded - local) * PAIRS + 8, 128), F32),
                pltpu.SemaphoreType.DMA((2,)),
                pltpu.SemaphoreType.DMA((clips * TOKEN_TILES,)),
            ],
        ),
        out_shape=sds((rows, 128), F32),
        compiler_params=PARAMS,
        cost_estimate=cost(4 * clips * padded * D * D, clips * padded * D * 10),
        name="token_grad",
    )(meta, tokens, gb, dk, dv, *pack.arrays)


def fold_kernel(keep_ref, recv_ref, *out_refs):
    for k, ref in enumerate(out_refs):
        ref[...] = (keep_ref[k].astype(F32) + recv_ref[k].astype(F32)).astype(BF)


def row_block(rows):
    return rows // 2 if rows % 32 == 0 else rows


def fold(keep, recv):
    rows, lanes = keep.shape[1:]
    step = row_block(rows)
    block = pl.BlockSpec((4, step, lanes), lambda i: (0, i, 0))
    return pl.pallas_call(
        fold_kernel,
        grid=(rows // step,),
        in_specs=[block, block],
        out_specs=[pl.BlockSpec((step, lanes), lambda i: (i, 0))] * 4,
        out_shape=[sds((rows, lanes), BF)] * 4,
        compiler_params=PARAMS,
        name="fold",
    )(keep, recv)


def split_kernel(keep_ref, recv_ref, keep_p, keep_q, send_p, send_q):
    half = keep_p.shape[1]
    for first, pairs in (
        (0, ((0, keep_p, 0), (2, keep_p, 1), (1, send_p, 0), (3, send_p, 1))),
        (half, ((0, keep_q, 0), (1, keep_q, 1), (2, send_q, 0), (3, send_q, 1))),
    ):
        for k, ref, at in pairs:
            rows = slice(first, first + half)
            ref[at] = (keep_ref[k, rows, :].astype(F32) + recv_ref[k, rows, :].astype(F32)).astype(BF)


def split(keep, recv):
    rows, lanes = keep.shape[1:]
    step = 128
    block = pl.BlockSpec((4, rows, step), lambda i: (0, 0, i))
    return pl.pallas_call(
        split_kernel,
        grid=(lanes // step,),
        in_specs=[block, block],
        out_specs=[pl.BlockSpec((2, rows // 2, step), lambda i: (0, 0, i))] * 4,
        out_shape=[sds((2, rows // 2, lanes), BF)] * 4,
        compiler_params=PARAMS,
        name="split",
    )(keep, recv)


def turn_kernel(keep_p, keep_q, recv_p, recv_q, own_ref, send_p, send_q):
    half = keep_p.shape[1]
    for first, keep, recv, send in ((0, keep_p, recv_p, send_p), (half, keep_q, recv_q, send_q)):
        own_ref[first : first + half, :] = (keep[0].astype(F32) + recv[0].astype(F32)).astype(BF)
        send[...] = (keep[1].astype(F32) + recv[1].astype(F32)).astype(BF)


def turn(keep_p, keep_q, recv_p, recv_q):
    half, lanes = keep_p.shape[1:]
    step = 128
    block = pl.BlockSpec((2, half, step), lambda i: (0, 0, i))
    out = lambda n: pl.BlockSpec((n, step), lambda i: (0, i))
    return pl.pallas_call(
        turn_kernel,
        grid=(lanes // step,),
        in_specs=[block] * 4,
        out_specs=[out(2 * half), out(half), out(half)],
        out_shape=[sds((2 * half, lanes), BF), sds((half, lanes), BF), sds((half, lanes), BF)],
        compiler_params=PARAMS,
        name="turn",
    )(keep_p, keep_q, recv_p, recv_q)


def join_kernel(own_ref, recv_p, recv_q, out_ref):
    half = recv_p.shape[0]
    for first, recv in ((0, recv_p), (half, recv_q)):
        rows = slice(first, first + half)
        out_ref[rows, :] = (own_ref[rows, :].astype(F32) + recv[...].astype(F32)).astype(BF)


def join(own, recv_p, recv_q):
    rows, lanes = own.shape
    step = 128
    block = lambda n: pl.BlockSpec((n, step), lambda i: (0, i))
    return pl.pallas_call(
        join_kernel,
        grid=(lanes // step,),
        in_specs=[block(rows), block(rows // 2), block(rows // 2)],
        out_specs=block(rows),
        out_shape=sds((rows, lanes), BF),
        compiler_params=PARAMS,
        cost_estimate=pl.CostEstimate(flops=0, bytes_accessed=10 * rows * lanes, transcendentals=0),
        name="join",
    )(own, recv_p, recv_q)


def sum_kernel(*refs):
    total = refs[0][...].astype(F32)
    for ref in refs[1:-1]:
        total = total + ref[...].astype(F32)
    refs[-1][...] = total.astype(BF)


def sum_of(parts):
    rows, lanes = parts[0].shape
    step = row_block(rows)
    block = pl.BlockSpec((step, lanes), lambda i: (i, 0))
    return pl.pallas_call(
        sum_kernel,
        grid=(rows // step,),
        in_specs=[block] * len(parts),
        out_specs=block,
        out_shape=sds((rows, lanes), BF),
        compiler_params=PARAMS,
        name="sum_parts",
    )(*parts)


def chunk_sums_kernel(meta, *refs):
    parts, outs = refs[:4], refs[4:]
    count = len(outs)
    step = outs[0].shape[0]
    for k, out in enumerate(outs):
        rows = pl.ds(pl.multiple_of(lax.rem(meta[1] + k, count) * step, step), step)
        total = parts[0][rows, :].astype(F32)
        for part in parts[1:]:
            total = total + part[rows, :].astype(F32)
        out[...] = total.astype(BF)


def chunk_sums(meta, parts, count=4):
    rows, lanes = parts[0].shape
    return pl.pallas_call(
        chunk_sums_kernel,
        in_specs=[pl.BlockSpec(memory_space=pltpu.SMEM)] + [WHOLE] * len(parts),
        out_specs=[WHOLE] * count,
        out_shape=[sds((rows // count, lanes), BF)] * count,
        compiler_params=PARAMS,
        name="chunk_sums",
    )(meta, *parts)


def after(x, *others):
    return lax.optimization_barrier((x, others))[0]


def exchange(x, bit):
    return lax.ppermute(x, "fsdp", [(i, i ^ bit) for i in range(OWNERS)])


def sum_over_fsdp(keep, send):
    full = jnp.stack([keep, send], 1).reshape(OWNERS, *keep.shape[1:])
    return lax.psum(full.astype(F32), "fsdp").astype(BF)


def finish_latent_kernel(count, meta, ma_ref, oa_ref, mb_ref, ob_ref, g1_ref, *refs):
    pieces, refs = refs[:count], refs[count:]
    lat_ref, qkv_ref, outw_ref, up_ref, down_ref, line_ref = refs
    s, h = meta[1], meta[2]
    step = pieces[0].shape[0]
    for k, piece in enumerate(pieces):
        rows = pl.ds(pl.multiple_of(lax.rem(s - k + count, count) * step, step), step)
        lat_ref[rows, :] = g1_ref[rows, :] + piece[...].astype(F32)
    for a_ref, b_ref, side in ((ma_ref, mb_ref, h), (oa_ref, ob_ref, 1 - h)):
        half = pl.ds(pl.multiple_of(side * HALF, 128), HALF)
        for layer, ref in ((1, a_ref), (0, b_ref)):
            for c in range(CHUNKS):
                at = pl.ds(pl.multiple_of(side * (FF // 2) + c * HALF, 128), HALF)
                up_ref[layer, :, at] = ref[c * SHARE : c * SHARE + SHARE, :].astype(F32)
            down_ref[layer, :, half] = ref[SPAN : 2 * SPAN, :].astype(F32)
        for i in range(4):
            first = ROWS_F + i * SHARE
            value = a_ref[first : first + SHARE, :].astype(F32)
            if i < 3:
                qkv_ref[0, i, :, half] = value
            else:
                outw_ref[1, :, half] = value
        outw_ref[0, :, half] = b_ref[2 * SPAN : 2 * SPAN + SHARE, :].astype(F32)
    last = ma_ref[2 * SPAN : ROWS_F, :].astype(F32)
    middle = ma_ref[ROWS_A - VEC : ROWS_A, :].astype(F32)
    first = mb_ref[ROWS_B - VEC_B : ROWS_B, :].astype(F32)
    line_ref[...] = jnp.zeros_like(line_ref)
    picks = [(first, 0), (middle, 0), (last, 0), (first, 1), (middle, 1), (last, 1), (first, 2), (last, 2)]
    picks += [(first, 3 + c) for c in range(CHUNKS)] + [(last, 3 + c) for c in range(CHUNKS)]
    for i, (vec, row) in enumerate(picks):
        for part in range(2):
            at = slice(part * HALF, part * HALF + HALF)
            line_ref[i : i + 1, at] = vec[2 * row + part : 2 * row + part + 1, :]


def finish_latent(meta, mine_f, other_f, mine_s, other_s, g1, pieces):
    rows = g1.shape[0]
    whole = lambda shape: pl.BlockSpec(shape, lambda i: (0,) * len(shape))
    return pl.pallas_call(
        functools.partial(finish_latent_kernel, len(pieces)),
        grid=(1,),
        in_specs=[pl.BlockSpec(memory_space=pltpu.SMEM)] + [WHOLE] * (5 + len(pieces)),
        out_specs=[
            whole((rows, D)),
            pl.BlockSpec((1, 3, SHARE, D), lambda i: (1, 0, 0, 0)),
            whole((2, SHARE, D)),
            whole((2, SHARE, FF)),
            whole((2, CHUNKS * SHARE, D)),
            whole((16, D)),
        ],
        out_shape=[
            sds((rows, D), F32),
            sds((2, 3, SHARE, D), F32),
            sds((2, SHARE, D), F32),
            sds((2, SHARE, FF), F32),
            sds((2, CHUNKS * SHARE, D), F32),
            sds((16, D), F32),
        ],
        compiler_params=PARAMS,
        name="finish_latent",
    )(meta, mine_f, other_f, mine_s, other_s, g1, *pieces)


def finish_token_kernel(count, meta, *refs):
    pieces, refs = refs[:count], refs[count:]
    w_ref, gain_ref, shift_ref, line_ref, qkv_in, qkv_ref, gain_out, shift_out, bin_out, bout_out, whole = refs
    f, s = meta[0], meta[1]
    step = pieces[0].shape[0]
    for k, piece in enumerate(pieces):
        rows = pl.ds(pl.multiple_of(lax.rem(s - k + count, count) * step, step), step)
        whole[rows, :] = piece[...].astype(F32)
    dk, dv, dq = (whole[i * SHARE : i * SHARE + SHARE, :] for i in range(3))
    qkv_ref[0, 0], qkv_ref[0, 1], qkv_ref[0, 2] = dq, dk, dv
    vec = whole[3 * SHARE : 3 * SHARE + 8, :]
    wk, wv = w_ref[0].astype(F32), w_ref[1].astype(F32)
    shift_sum = jnp.sum(wk * vec[0:1] + wv * vec[1:2], -1, keepdims=True)
    gain_sum = jnp.sum(wk * dk + wv * dv, -1, keepdims=True)
    lane = lax.broadcasted_iota(jnp.int32, (SHARE, 128), 1)
    turned = jnp.where(lane == 0, shift_sum, jnp.where(lane == 1, gain_sum, 0.0)).T
    db, total = turned[0:1, :SHARE], turned[1:2, :SHARE]
    dg = (total - shift_ref[1:2, :].astype(F32) * db) / gain_ref[1:2, :].astype(F32)
    lines = jnp.concatenate([line_ref[...], vec], 0)
    cut = pltpu.roll(lines, lax.rem(D - f * SHARE, D), 1)[:, :SHARE]
    gain_out[0:1, :], gain_out[1:2, :], gain_out[2:5, :] = cut[18:19], dg, cut[0:3]
    shift_out[0:1, :], shift_out[1:2, :], shift_out[2:5, :] = cut[19:20], db, cut[3:6]
    bout_out[...] = cut[6:8]
    wide = jnp.concatenate([line_ref[8 + c : 9 + c, :] for c in range(CHUNKS)], 1)
    other = jnp.concatenate([line_ref[12 + c : 13 + c, :] for c in range(CHUNKS)], 1)
    both = jnp.concatenate([wide, other], 0)
    span = CHUNKS * SHARE
    total = jnp.zeros((2, span), F32)
    for g in range(OWNERS):
        total = jnp.where(f == g, both[:, g * span : g * span + span], total)
    bin_out[...] = total


def finish_token(meta, pieces, weights, gain, shift, lines, qkv):
    whole = lambda shape: pl.BlockSpec(shape, lambda i: (0,) * len(shape))
    count = len(pieces)
    return pl.pallas_call(
        functools.partial(finish_token_kernel, count),
        grid=(1,),
        in_specs=[pl.BlockSpec(memory_space=pltpu.SMEM)] + [WHOLE] * (count + 4) + [ANY],
        out_specs=[
            pl.BlockSpec((1, 3, SHARE, D), lambda i: (0, 0, 0, 0)),
            whole((5, SHARE)),
            whole((5, SHARE)),
            whole((2, CHUNKS * SHARE)),
            whole((2, SHARE)),
        ],
        out_shape=[
            sds(qkv.shape, F32),
            sds((5, SHARE), F32),
            sds((5, SHARE), F32),
            sds((2, CHUNKS * SHARE), F32),
            sds((2, SHARE), F32),
        ],
        scratch_shapes=[pltpu.VMEM((ROWS_K, D), F32)],
        input_output_aliases={count + 5: 0},
        compiler_params=PARAMS,
        name="finish_token",
    )(meta, *pieces, weights, gain, shift, lines, qkv)


def unpack(left_a, right_a, left_b, right_b, whole_k):
    sides_a, sides_b = (left_a, right_a), (left_b, right_b)

    def up(sides):
        return jnp.concatenate(
            [x[c * SHARE : c * SHARE + SHARE] for x in sides for c in range(CHUNKS)], 1
        )

    def rows(sides, at, span=SHARE):
        return jnp.concatenate([x[at : at + span] for x in sides], 1)

    q1, k1, v1, out1 = (rows(sides_a, ROWS_F + i * SHARE) for i in range(4))
    out0 = rows(sides_b, 2 * SPAN)
    k0, v0, q0 = (whole_k[i * SHARE : i * SHARE + SHARE] for i in range(3))
    return (
        jnp.stack([jnp.stack([q0, k0, v0]), jnp.stack([q1, k1, v1])]).astype(F32),
        jnp.stack([out0, out1]).astype(F32),
        jnp.stack([up(sides_b), up(sides_a)]).astype(F32),
        jnp.stack([rows(sides_b, SPAN, SPAN), rows(sides_a, SPAN, SPAN)]).astype(F32),
    )


def per_device(size, seq, *args):
    (
        latents_in,
        inputs,
        clip_frames,
        text_mask,
        qkv_weight,
        out_weight,
        mlp_in,
        mlp_out,
        norm_gain,
        norm_bias,
        bias_in,
        bias_out,
        out_cotangent,
    ) = args
    micro, clips, nlat, _ = latents_in.shape
    count = micro * clips
    local = inputs.shape[2]
    padded = -(-local // 128) * 128
    rows = count * nlat
    s = lax.axis_index("seq")
    fsdp = lax.axis_index("fsdp")
    special = size == OWNERS
    meta = jnp.stack([fsdp if special else jnp.int32(0), s, s % 2]).astype(jnp.int32)
    lat = latents_in.reshape(rows, D)
    tokens = inputs.reshape(count, local, D)
    g4 = out_cotangent.reshape(rows, D)

    place = s * local + jnp.arange(padded, dtype=jnp.int32)
    frames = clip_frames.reshape(count, 1) * PATCHES
    text = text_mask.reshape(count, -1) > 0
    text_len = text.shape[1]
    slots = FRAMES * PATCHES
    wide = jnp.pad(text, ((0, 0), (slots, padded)))
    text_here = lax.dynamic_slice_in_dim(wide, s * local, padded, 1)
    valid = jnp.where(place[None] < slots, place[None] < frames, text_here)
    valid = valid & (jnp.arange(padded)[None] < local)
    bias = jnp.where(valid, 0.0, -1e30).astype(F32)
    mask = jnp.broadcast_to(bias[:, :, None], (count, padded, 128))

    def slabs(up):
        return up.reshape(SHARE, CHUNKS, D).transpose(1, 0, 2).reshape(SPAN, D)

    def pack_keyval(qkv, out, up, down, gain, shift, up_b, down_b):
        small = jnp.concatenate(
            [
                jnp.pad(jnp.concatenate([gain, shift, down_b], 0), ((0, 0), (0, 128 - SHARE))),
                up_b.reshape(6, 128),
                jnp.zeros((14, 128), BF),
            ],
            0,
        )
        small = jnp.concatenate([small[:16], small[16:]], 1)
        small = jnp.pad(small, ((0, 0), (0, D - 256)))
        return jnp.concatenate([qkv[0, 1], qkv[0, 2], qkv[0, 0], small], 0)

    def pack_first(qkv, out, up, down, *rest):
        return jnp.concatenate([out[0], slabs(up[0]), down[0]], 0)

    def pack_last(qkv, out, up, down, *rest):
        return jnp.concatenate([qkv[1].reshape(3 * SHARE, D), out[1], slabs(up[1]), down[1]], 0)

    packers = (pack_keyval, pack_first, pack_last)
    weights = (qkv_weight, out_weight, mlp_in, mlp_out, norm_gain, norm_bias, bias_in, bias_out)
    axes = (2, 1, 1, 1, 1, 1, 1, 1)
    def shift_to(x, k):
        return lax.ppermute(x, "seq", [(i, (i + k) % seq) for i in range(seq)])

    def scatter_rows(x):
        step = x.shape[0] // seq
        out = []
        for k in range(1, seq):
            piece = lax.dynamic_slice_in_dim(x, ((s + k) % seq) * step, step, 0)
            out.append(shift_to(piece, k))
        return out

    def gather_rows(x):
        return [x] + [shift_to(x, k) for k in range(1, seq)]

    pair = [(i, i ^ 1) for i in range(seq)]

    if special:
        def direct(x):
            return {0: x, 2: exchange(x, 2), 4: exchange(x, 4), 6: exchange(x, 6)}

        def direct_pack(p, later):
            arrays = [p[m] if m % 2 == 0 else exchange(later(p[m - 1]), 1) for m in range(OWNERS)]
            return Pack(arrays, lambda m, row: (m, None, row))

        def relay_pack(parts):
            half = parts[3].shape[0]
            arrays = []
            for x in parts:
                arrays += [x, exchange(x, 1)]

            def where(m, row):
                if m < 6:
                    return (m, None, row)
                return (m, None, row) if row < half else (m + 2, None, row - half)

            return Pack(arrays, where)

        x1 = pack_keyval(*weights)
        p1 = direct(x1)
        x3 = pack_last(*after(weights, x1))
        x3_2, x3_4 = exchange(x3, 2), exchange(x3, 4)
        tokens = with_layout_constraint(tokens, Layout(major_to_minor=(0, 1, 2)))
        bias, tokens = after((bias, tokens), x3)
        g1 = direct_pack(p1, lambda x: after(x, p1[2], tokens))
        xl, k, v, gb, bins = keyval(g1, meta, tokens, local, padded)
        mask = after(bias, k)
        mask = jnp.broadcast_to(mask[:, :, None], (count, padded, 128))
        pay, q = attend(g1, meta, lat, gb, bias[:, None, :], k, v)
        pay = pay.reshape(rows, PAY)
        arrived = scatter_rows(pay)
        x2 = pack_first(*after(weights, k))
        x3_2, x3_4, x2 = after((x3_2, x3_4, x2), pay)
        half = x3.shape[0] // 2
        turn_2, turn_4 = x3_2[:half], x3_4[half:]
        x2_2, x2_4 = exchange(x2, 2), exchange(x2, 4)
        share = combine(meta, after(pay, mask), arrived)
        parts = gather_rows(share)
        turn_2, turn_4, x2_2, x2_4 = after((turn_2, turn_4, x2_2, x2_4), parts)
        half = SHARE + SPAN
        x2_6a, x2_6b = exchange(x2_2[:half], 4), exchange(x2_4[half:], 2)
        x3_6a, x3_6b = exchange(turn_2, 4), exchange(turn_4, 2)
        g2 = relay_pack([x2, *after((x2_2, x2_4), x2_6a, x2_6b), x2_6a, x2_6b])
        o, l, z1, z2, hidden = first_block(g2, meta, parts, lat, gb, bins)
        x3_6a, x3_6b = after((x3_6a, x3_6b), z2)
        g34 = relay_pack([x3, x3_2, x3_4, x3_6a, x3_6b])
    else:
        full = []
        for w, axis in zip(weights, axes):
            whole = lax.all_gather(w, "fsdp", axis=axis, tiled=True)
            shape = whole.shape
            parts = whole.reshape(*shape[:axis], OWNERS, shape[axis] // OWNERS, *shape[axis + 1 :])
            full.append(jnp.moveaxis(parts, axis, 0))
        raw = [jax.vmap(packer)(*full) for packer in packers]
        g1, g2, g34 = [Pack([x], lambda m, row: (0, m, row)) for x in raw]
        xl, k, v, gb, bins = keyval(g1, meta, tokens, local, padded)
        pay, q = attend(g1, meta, lat, gb, bias[:, None, :], k, v)
        pay = pay.reshape(rows, PAY)
        share = combine(meta, pay, scatter_rows(pay))
        o, l, z1, z2, hidden = first_block(g2, meta, gather_rows(share), lat, gb, bins)
    out, g2_lat, keep_a, send_a = second_block(g34, meta, z2, g4, gb, bins)

    grad_one, du, dl, keep_b, send_b = fourth_block(g2, meta, g2_lat, z1, o, l, gb, hidden)
    cube = lambda x: x.reshape(count, nlat, x.shape[-1])
    shapes = (latents_in.shape, inputs.shape)
    if special:
        recv_a, recv_b = exchange(send_a, 1), exchange(send_b, 1)
        split_a = split(*after((keep_a, recv_a), du))
        split_b = split(*after((keep_b, recv_b), *split_a))
        du, dl = after((du, dl), *split_a, *split_b)
        dk, dv, dq = attend_back(cube(q), cube(du), cube(dl), mask, k, v)
        dq = dq.reshape(rows, D)
        first_a = (*split_a[:2], exchange(split_a[2], 2), exchange(split_a[3], 4))
        first_b = (*split_b[:2], exchange(split_b[2], 2), exchange(split_b[3], 4))
        turn_a = turn(*after(first_a, dq))
        second_a = (turn_a[0], exchange(turn_a[1], 4), exchange(turn_a[2], 2))
        keep_k, send_k, sums = keyval_grad(meta, *after((xl, dk, dv), *turn_a))
        dq = after(dq, sums)
        dq_parts = scatter_rows(dq)
        turn_b = turn(*after(first_b, sums))
        second_b = (turn_b[0], exchange(turn_b[1], 4), exchange(turn_b[2], 2))
        mine_a = join(*after(second_a, *turn_b))
        mine_b = join(*after(second_b, mine_a))
        dq, dq_parts = after((dq, dq_parts), mine_b)
        back, keep_k, send_k = query_grad(g1, meta, dq, dq_parts, lat, gb, sums, keep_k, send_k)
        recv_k = exchange(send_k, 1)
        fold_k = fold(keep_k, recv_k)
        other_a = lax.ppermute(mine_a, "seq", pair)
        other_b = lax.ppermute(mine_b, "seq", pair)
        hop_k = [exchange(x, 2 * i) for i, x in enumerate(fold_k) if i]
        token_grads = token_grad(g1, meta, tokens, gb, *after((dk, dv), mine_a, mine_b, *fold_k))
        mine_k = chunk_sums(meta, after([fold_k[0]] + hop_k, token_grads), seq)
        back_rows = gather_rows(after(back, *mine_k))
        sent = [shift_to(x, i) for i, x in enumerate(mine_k) if i]
        pieces = gather_rows(sum_of([mine_k[0]] + sent))
        lat_grad, qkv_grad, outw_grad, up_grad, down_grad, lines = finish_latent(
            meta, mine_a, other_a, mine_b, other_b, grad_one, back_rows
        )
        qkv_grad, gain_grad, shift_grad, bin_grad, bout_grad = finish_token(
            meta, pieces, qkv_weight[0, 1:3], norm_gain, norm_bias, lines, qkv_grad
        )
        return (
            out.reshape(shapes[0]),
            lat_grad.reshape(shapes[0]),
            token_grads.reshape(shapes[1]),
            qkv_grad,
            outw_grad,
            up_grad,
            down_grad,
            gain_grad,
            shift_grad,
            bin_grad,
            bout_grad,
        )

    dk, dv, dq = attend_back(cube(q), cube(du), cube(dl), mask, k, v)
    dq = dq.reshape(rows, D)
    keep_k, send_k, sums = keyval_grad(meta, xl, dk, dv)
    back, keep_k, send_k = query_grad(g1, meta, dq, scatter_rows(dq), lat, gb, sums, keep_k, send_k)
    token_grads = token_grad(g1, meta, tokens, gb, dk, dv)
    lat_grad = grad_one + place_rows(gather_rows(back), s, seq)
    mine_a, mine_b, mine_k = (
        sum_over_fsdp(*x) for x in ((keep_a, send_a), (keep_b, send_b), (keep_k, send_k))
    )

    def both(mine):
        other = lax.ppermute(mine, "seq", pair)
        return jnp.where(s % 2 == 0, mine, other), jnp.where(s % 2 == 0, other, mine)

    whole_k = lax.psum(mine_k.astype(F32), "seq")
    shares = (*both(mine_a), *both(mine_b), whole_k)
    wide = jax.vmap(unpack)(*shares)
    grads = []
    for x, w, axis in zip(wide, weights, axes):
        x = jnp.moveaxis(x, 0, axis)
        x = x.reshape(*x.shape[:axis], -1, *x.shape[axis + 2 :])
        grads.append(lax.dynamic_slice_in_dim(x, fsdp * w.shape[axis], w.shape[axis], axis))
    last = shares[0][0, 2 * SPAN : ROWS_F].astype(F32).reshape(-1, D)
    middle = shares[0][0, -VEC:].astype(F32).reshape(-1, D)
    early = shares[2][0, -VEC_B:].astype(F32).reshape(-1, D)
    vec_k = whole_k[0][-VEC_K:]
    step = norm_gain.shape[1]
    k0, v0 = grads[0][0, 1], grads[0][0, 2]
    own_k, own_v = qkv_weight[0, 1].astype(F32), qkv_weight[0, 2].astype(F32)
    own_gain, own_shift = norm_gain[1].astype(F32), norm_bias[1].astype(F32)
    db1 = jnp.sum(own_k * vec_k[0] + own_v * vec_k[1], -1)
    dg1 = (jnp.sum(own_k * k0 + own_v * v0, -1) - own_shift * db1) / own_gain
    lines = [vec_k[2], early[0], middle[0], last[0], vec_k[3], early[1], middle[1], last[1], early[2], last[2]]
    lines = jnp.stack(lines)
    cut = lax.dynamic_slice_in_dim(lines, fsdp * step, step, 1)
    wide_bias = jnp.stack([early[3:7].reshape(FF), last[3:7].reshape(FF)])
    return (
        out.reshape(shapes[0]),
        lat_grad.reshape(shapes[0]),
        token_grads.reshape(shapes[1]),
        *grads,
        jnp.stack([cut[0], dg1, cut[1], cut[2], cut[3]]),
        jnp.stack([cut[4], db1, cut[5], cut[6], cut[7]]),
        lax.dynamic_slice_in_dim(wide_bias, fsdp * bias_in.shape[1], bias_in.shape[1], 1),
        cut[8:10],
    )


def place_rows(pieces, s, seq):
    step = pieces[0].shape[0]
    whole = jnp.zeros((seq * step, *pieces[0].shape[1:]), F32)
    for k, piece in enumerate(pieces):
        at = ((s - k) % seq) * step
        whole = lax.dynamic_update_slice_in_dim(whole, piece.astype(F32), at, 0)
    return whole


def solution(mesh):
    in_specs = (
        P(None, "fsdp", None, None),
        P(None, "fsdp", "seq", None),
        P(None, "fsdp"),
        P(None, "fsdp", None),
        P(None, None, "fsdp", None),
        P(None, "fsdp", None),
        P(None, "fsdp", None),
        P(None, "fsdp", None),
        P(None, "fsdp"),
        P(None, "fsdp"),
        P(None, "fsdp"),
        P(None, "fsdp"),
        P(None, "fsdp", None, None),
    )
    out_specs = (
        P(None, "fsdp", None, None),
        P(None, "fsdp", None, None),
        P(None, "fsdp", "seq", None),
        P(None, None, "fsdp", None),
        P(None, "fsdp", None),
        P(None, "fsdp", None),
        P(None, "fsdp", None),
        P(None, "fsdp"),
        P(None, "fsdp"),
        P(None, "fsdp"),
        P(None, "fsdp"),
    )
    step = functools.partial(per_device, mesh.shape["fsdp"], mesh.shape["seq"])
    return jax.shard_map(step, mesh=mesh, in_specs=in_specs, out_specs=out_specs, check_vma=False)
```

```python
import functools

import jax
import jax.numpy as jnp
from jax import lax
from jax.experimental import pallas as pl
from jax.experimental.layout import Layout, with_layout_constraint
from jax.experimental.pallas import tpu as pltpu
from jax.sharding import PartitionSpec as P

D = 768
HEADS = 12
HEAD = 64
PAIRS = HEADS // 2
FF = 3072
NLAT = 128
PATCHES = 392
FRAMES = 16
OWNERS = 8
SHARE = D // OWNERS
CHUNKS = FF // D
HALF = D // 2
PAY = D + 128
KEYVAL_ROWS = 208
FORWARD_PAIRS = 3
BACK_PAIRS = 2
TOKEN_TILES = 2
GRAD_TILES = 1
TOKEN_ROWS = 416
VEC = 16
VEC_A = 48
VEC_B = 32
STEPS = 2
VEC_K = 32
SPAN = CHUNKS * SHARE
ROWS_F = 2 * SPAN + VEC
ROWS_A = ROWS_F + 4 * SHARE + VEC_A
ROWS_B = 2 * SPAN + SHARE + VEC_B
ROWS_K = 3 * SHARE + VEC_K
EPS = 1e-06
F32 = jnp.float32
BF = jnp.bfloat16
GELU_C = 0.7978845608028654
GELU_A = 0.044715
VMEM_CAP = 60 * 1024 * 1024


def nn(a, b):
    return lax.dot_general(a, b, (((1,), (0,)), ((), ())), preferred_element_type=F32)


def nt(a, b):
    return lax.dot_general(a, b, (((1,), (1,)), ((), ())), preferred_element_type=F32)


def tn(a, b):
    return lax.dot_general(a, b, (((0,), (0,)), ((), ())), preferred_element_type=F32)


def ln_parts(x):
    center = x - jnp.mean(x, -1, keepdims=True)
    rstd = lax.rsqrt(jnp.mean(center * center, -1, keepdims=True) + EPS)
    return center, rstd


def ln(x, gain, bias):
    center, rstd = ln_parts(x)
    return center * rstd * gain + bias


def ln_back(x, gain, grad):
    center, rstd = ln_parts(x)
    xhat = center * rstd
    dx = grad * gain
    back = rstd * (dx - jnp.mean(dx, -1, keepdims=True) - xhat * jnp.mean(dx * xhat, -1, keepdims=True))
    return back, grad * xhat


def gelu(h):
    return h * (0.5 * (1.0 + jnp.tanh(GELU_C * (h + GELU_A * h * h * h))))


def gelu_both(h):
    square = h * h
    t = jnp.tanh(GELU_C * (h + GELU_A * h * square))
    cdf = 0.5 * (1.0 + t)
    slope = cdf + 0.5 * h * (1.0 - t * t) * (GELU_C * (1.0 + 3.0 * GELU_A * square))
    return h * cdf, slope


def low_lanes(rows):
    return lax.broadcasted_iota(jnp.int32, (rows, 128), 1) < HEAD


def block_diag(pair):
    wide = pair.astype(F32)
    low = low_lanes(pair.shape[0])
    return jnp.concatenate([jnp.where(low, wide, 0.0), jnp.where(low, 0.0, wide)], 0).astype(BF)


def diag_of(both):
    rows = both.shape[0] // 2
    return jnp.where(low_lanes(rows), both[:rows], both[rows:])


class Pack:
    def __init__(self, arrays, where):
        self.arrays, self.where = arrays, where

    def start(self, refs, row, rows, place, f, sem, shares=range(OWNERS)):
        for m in shares:
            index, lead, first = self.where(m, row)
            src = refs[index] if lead is None else refs[index].at[lead]
            pltpu.make_async_copy(src.at[pl.ds(first, rows)], place(f ^ m), sem).start()


def wait_for(ref, sem):
    pltpu.make_async_copy(ref, ref, sem).wait()


def share_rows(ref, g, first=0, span=SHARE, step=SHARE):
    return ref.at[pl.ds(pl.multiple_of(g * step + first, SHARE), span)]


def start_square(pack, refs, row, dst, f, sem):
    pack.start(refs, row, SHARE, lambda g: share_rows(dst, g), f, sem)


def start_up(pack, refs, row, dst, f, sems):
    for t in range(CHUNKS):
        lanes = pl.ds(t * D, D)
        pack.start(
            refs,
            row + t * SHARE,
            SHARE,
            lambda g, lanes=lanes: dst.at[pl.ds(pl.multiple_of(g * SHARE, SHARE), SHARE), lanes],
            f,
            sems.at[t],
        )


def start_down(pack, refs, row, dst, f, sems):
    for i in range(CHUNKS):
        for t in range(CHUNKS):
            pack.start(
                refs,
                row + t * SHARE,
                SHARE,
                lambda g, t=t: share_rows(dst, g, t * SHARE, SHARE, SPAN),
                f,
                sems.at[i],
                (2 * i, 2 * i + 1),
            )


def chunk_at(f, i):
    return pl.ds(pl.multiple_of(((f >> 1) ^ i) * D, D), D)


ANY = pl.BlockSpec(memory_space=pl.ANY)
WHOLE = pl.BlockSpec(memory_space=pltpu.VMEM)


def sds(shape, dtype):
    return jax.ShapeDtypeStruct(shape, dtype)


def cost(flops, size, exps=0):
    return pl.CostEstimate(flops=1, bytes_accessed=1, transcendentals=0)


PARAMS = pltpu.CompilerParams(vmem_limit_bytes=VMEM_CAP)


def keyval_kernel(pack, local, tile, meta, x_ref, *refs):
    count = len(pack.arrays)
    wrefs, (xl_ref, k_ref, v_ref, gb_ref, bin_ref, wkv, small, sems) = refs[:count], refs[count:]
    f = meta[0]

    @pl.when((pl.program_id(0) == 0) & (pl.program_id(1) == 0))
    def _():
        for m in range(OWNERS):
            index, lead, first = pack.where(m, 3 * SHARE)
            src = wrefs[index] if lead is None else wrefs[index].at[lead]
            pltpu.make_async_copy(
                src.at[pl.ds(first, 16), pl.ds(0, 256)], small.at[m], sems.at[2]
            ).start()
        start_square(pack, wrefs, 0, wkv.at[0], f, sems.at[0])
        start_square(pack, wrefs, SHARE, wkv.at[1], f, sems.at[1])
        wait_for(small, sems.at[2])
        lane = lax.broadcasted_iota(jnp.int32, (128, D), 1)
        row = lax.broadcasted_iota(jnp.int32, (128, D), 0)
        total = jnp.zeros((16, D), F32)
        for m in range(OWNERS):
            g = f ^ m
            place = jnp.where((lane - g * SHARE == row) & (row < SHARE), 1.0, 0.0).astype(BF)
            total = total + nn(small[m, :, 0:128], place)
            wide = small[m].astype(F32)
            for u in range(6):
                i, part = u // 3, u % 3
                line = wide[12 + u : 13 + u, 0:128] if u < 4 else wide[u - 4 : u - 3, 128:256]
                at = pl.ds(pl.multiple_of((3 * g + part) * 128, 128), 128)
                bin_ref[i : i + 1, at] = line
        gb_ref[...] = total
        wait_for(wkv.at[0], sems.at[0])
        wait_for(wkv.at[1], sems.at[1])

    for first in range(0, tile, KEYVAL_ROWS):
        part = slice(first, first + KEYVAL_ROWS)
        normed = ln(x_ref[0, part, :].astype(F32), gb_ref[1:2], gb_ref[6:7])
        row = lax.broadcasted_iota(jnp.int32, (KEYVAL_ROWS, D), 0)
        row = row + (pl.program_id(1) * tile + first)
        xl = jnp.where(row < local, normed, 0.0).astype(BF)
        xl_ref[0, part, :] = xl
        k_ref[0, part, :] = nn(xl, wkv[0]).astype(BF)
        v_ref[0, part, :] = nn(xl, wkv[1]).astype(BF)


def keyval(pack, meta, tokens, local, padded):
    clips = tokens.shape[0]
    tile = padded // 2
    block = pl.BlockSpec((1, tile, D), lambda i, j, m: (i, j, 0))
    fixed = lambda shape: pl.BlockSpec(shape, lambda i, j, m: (0,) * len(shape))
    return pl.pallas_call(
        functools.partial(keyval_kernel, pack, local, tile),
        grid_spec=pltpu.PrefetchScalarGridSpec(
            num_scalar_prefetch=1,
            grid=(clips, padded // tile),
            in_specs=[block] + [ANY] * len(pack.arrays),
            out_specs=[block, block, block, fixed((16, D)), fixed((2, FF))],
            scratch_shapes=[
                pltpu.VMEM((2, D, D), BF),
                pltpu.VMEM((OWNERS, 16, 256), BF),
                pltpu.SemaphoreType.DMA((3,)),
            ],
        ),
        out_shape=[sds((clips, padded, D), BF)] * 3 + [sds((16, D), F32), sds((2, FF), F32)],
        compiler_params=PARAMS,
        cost_estimate=cost(4 * clips * padded * D * D, clips * padded * D * 8),
        name="keyval",
    )(meta, tokens, *pack.arrays)


def attend_kernel(pack, padded, meta, lat_ref, gb_ref, bias_ref, k_ref, v_ref, *refs):
    count = len(pack.arrays)
    wrefs, (pay_ref, q_ref, wq, qs, lv, sem) = refs[:count], refs[count:]
    f = meta[0]
    clip, group = pl.program_id(0), pl.program_id(1)

    @pl.when((clip == 0) & (group == 0))
    def _():
        start_square(pack, wrefs, 2 * SHARE, wq, f, sem.at[0])
        zl = ln(lat_ref[...].astype(F32), gb_ref[0:1], gb_ref[5:6]).astype(BF)
        wait_for(wq, sem.at[0])
        q = nn(zl, wq[...]).astype(BF).astype(F32) * 0.125
        qs[...] = q.astype(BF)
        q_ref[...] = qs[...]

    rows = pl.ds(pl.multiple_of(clip * NLAT, NLAT), NLAT)
    lane = lax.broadcasted_iota(jnp.int32, (NLAT, 128), 1)
    new = jnp.where(group == 0, 0.0, lv[...])
    for p in range(FORWARD_PAIRS):
        pair = group * FORWARD_PAIRS + p
        at = pl.ds(pl.multiple_of(pair * 128, 128), 128)
        mine = slice(p * 128, p * 128 + 128)
        e = jnp.exp(nt(block_diag(qs[rows, at]), k_ref[0, :, mine]) + bias_ref[0])
        pay_ref[0, :, at] = diag_of(nn(e.astype(BF), v_ref[0, :, mine])).astype(BF)
        l = jnp.sum(e, -1, keepdims=True)
        new = jnp.where(lane == 2 * pair, l[:NLAT], jnp.where(lane == 2 * pair + 1, l[NLAT:], new))
    lv[...] = new

    @pl.when(group == PAIRS // FORWARD_PAIRS - 1)
    def _():
        pay_ref[0, :, D:PAY] = split_pair(lv[...])


def split_pair(values):
    high = values.astype(BF).astype(F32)
    rest = values - high
    return jnp.where(low_lanes(values.shape[0]), high, pltpu.roll(rest, HEAD, 1)).astype(BF)


def join_pair(pay):
    wide = pay.astype(F32)
    return wide + pltpu.roll(wide, HEAD, 1)


def attend(pack, meta, lat, gb, bias, k, v):
    clips, padded = k.shape[0], k.shape[1]
    rows = lat.shape[0]
    fixed = lambda shape: pl.BlockSpec(shape, lambda i, j, m: (0,) * len(shape))
    lanes = pl.BlockSpec((1, padded, 128 * FORWARD_PAIRS), lambda i, j, m: (i, 0, j))
    return pl.pallas_call(
        functools.partial(attend_kernel, pack, padded),
        grid_spec=pltpu.PrefetchScalarGridSpec(
            num_scalar_prefetch=1,
            grid=(clips, PAIRS // FORWARD_PAIRS),
            in_specs=[
                fixed((rows, D)),
                fixed((16, D)),
                pl.BlockSpec((1, 1, padded), lambda i, j, m: (i, 0, 0)),
                lanes,
                lanes,
            ]
            + [ANY] * len(pack.arrays),
            out_specs=[
                pl.BlockSpec((1, NLAT, PAY), lambda i, j, m: (i, 0, 0)),
                fixed((rows, D)),
            ],
            scratch_shapes=[
                pltpu.VMEM((D, D), BF),
                pltpu.VMEM((rows, D), BF),
                pltpu.VMEM((NLAT, 128), F32),
                pltpu.SemaphoreType.DMA((1,)),
            ],
        ),
        out_shape=[sds((clips, NLAT, PAY), BF), sds((rows, D), BF)],
        compiler_params=PARAMS,
        cost_estimate=cost(
            8 * clips * padded * NLAT * D, clips * padded * D * 4, clips * padded * NLAT * HEADS
        ),
        name="attend",
    )(meta, lat, gb, bias, k, v, *pack.arrays)


def combine_kernel(*refs):
    parts, out_ref = refs[1:-1], refs[-1]
    total = parts[0][...].astype(F32)
    for part in parts[1:]:
        total = total + part[...].astype(F32)
    l = total[:, D:PAY]
    l = l + pltpu.roll(l, HEAD, 1)
    low = low_lanes(total.shape[0])
    for j in range(PAIRS):
        den = jnp.where(low, l[:, 2 * j : 2 * j + 1], l[:, 2 * j + 1 : 2 * j + 2])
        out_ref[:, 128 * j : 128 * j + 128] = (total[:, 128 * j : 128 * j + 128] / den).astype(BF)
    out_ref[:, D:PAY] = split_pair(l)


def combine(meta, pay, received):
    rows = received[0].shape[0] if received else pay.shape[0]
    fixed = pl.BlockSpec((rows, PAY), lambda i, m: (0, 0))
    return pl.pallas_call(
        combine_kernel,
        grid_spec=pltpu.PrefetchScalarGridSpec(
            num_scalar_prefetch=1,
            grid=(1,),
            in_specs=[pl.BlockSpec((rows, PAY), lambda i, m: (m[1], 0))] + [fixed] * len(received),
            out_specs=fixed,
        ),
        out_shape=sds((rows, PAY), BF),
        name="combine",
    )(meta, pay, *received)


def first_kernel(pack, count, meta, *refs):
    parts = refs[:count]
    lat_ref, gb_ref, bin_ref = refs[count : count + 3]
    refs = refs[count + 3 :]
    wrefs, refs = refs[: len(pack.arrays)], refs[len(pack.arrays) :]
    o_ref, l_ref, z1_ref, z2_ref, h_ref, wo, win, wout, hs, sems, hsems = refs
    f, s = meta[0], meta[1]
    start_square(pack, wrefs, 0, wo, f, sems.at[0])
    start_up(pack, wrefs, SHARE, win, f, sems.at[pl.ds(1, CHUNKS)])
    start_down(pack, wrefs, SHARE + SPAN, wout, f, sems.at[pl.ds(1 + CHUNKS, CHUNKS)])
    step = parts[0].shape[0]
    for k, part in enumerate(parts):
        rows = pl.ds(pl.multiple_of(lax.rem(s - k + count, count) * step, step), step)
        o_ref[rows, :] = part[:, :D]
        l_ref[rows, :] = join_pair(part[:, D:PAY])
    wait_for(wo, sems.at[0])
    z1 = lat_ref[...].astype(F32) + nn(o_ref[...], wo[...])
    z1_ref[...] = z1
    n = ln(z1, gb_ref[2:3], gb_ref[7:8]).astype(BF)
    y = jnp.zeros_like(z1)
    copies = []
    for i in range(CHUNKS):
        at = chunk_at(f, i)
        wait_for(win.at[:, at], sems.at[1 + ((f >> 1) ^ i)])
        h = nn(n, win[:, at]) + bin_ref[0:1, at]
        hs[:, at] = h
        copies.append(pltpu.make_async_copy(hs.at[:, at], h_ref.at[:, at], hsems.at[i]))
        copies[-1].start()
        a = gelu(h).astype(BF)
        wait_for(wout.at[at], sems.at[1 + CHUNKS + i])
        y = y + nn(a, wout[at, :])
    z2_ref[...] = z1 + (y + gb_ref[10:11])
    for copy in copies:
        copy.wait()


def first_block(pack, meta, parts, lat, gb, bins):
    rows = lat.shape[0]
    n_w = len(pack.arrays)
    return pl.pallas_call(
        functools.partial(first_kernel, pack, len(parts)),
        in_specs=[pl.BlockSpec(memory_space=pltpu.SMEM)] + [WHOLE] * (len(parts) + 3) + [ANY] * n_w,
        out_specs=[WHOLE] * 4 + [ANY],
        scratch_shapes=[
            pltpu.VMEM((D, D), BF),
            pltpu.VMEM((D, FF), BF),
            pltpu.VMEM((FF, D), BF),
            pltpu.VMEM((rows, FF), F32),
            pltpu.SemaphoreType.DMA((1 + 2 * CHUNKS,)),
            pltpu.SemaphoreType.DMA((CHUNKS,)),
        ],
        out_shape=[
            sds((rows, D), BF),
            sds((rows, 128), F32),
            sds((rows, D), F32),
            sds((rows, D), F32),
            sds((rows, FF), F32),
        ],
        compiler_params=PARAMS,
        cost_estimate=cost(18 * rows * D * D, 16 * D * D * 2),
        name="first_block",
    )(meta, *parts, lat, gb, bins, *pack.arrays)


def softmax_rows(scores):
    e = jnp.exp(scores - jnp.max(scores, -1, keepdims=True))
    return e / jnp.sum(e, -1, keepdims=True)


def put_vec(shares, rows, row, width):
    vec = jnp.concatenate(rows + [jnp.zeros((width - len(rows), HALF), F32)], 0).astype(BF)
    for which in range(2):
        for k in range(4):
            shares[which, k, row : row + width, :] = vec


def halves(line):
    return [line[:, i : i + HALF] for i in range(0, line.shape[1], HALF)]


def column_sum(values):
    return jnp.sum(values, 0, keepdims=True)


def put_rows(shares, f, row, grad, first=0):
    grad = grad.astype(BF)
    for g in range(OWNERS):
        rel = f ^ g
        shares[rel & 1, rel >> 1, row : row + SHARE, :] = grad[g * SHARE : g * SHARE + SHARE]


def put_down(shares, f, row, grad, u):
    grad = grad.astype(BF)
    span = CHUNKS * SHARE
    for i in range(D // span):
        rel = f ^ (u * (D // span) + i)
        shares[rel & 1, rel >> 1, row : row + span, :] = grad[i * span : i * span + span]


def ff_grads(shares, f, h, row, n, dh_ref, a_ref, dy_ref):
    for c in range(CHUNKS):
        at = pl.ds(pl.multiple_of(h * (FF // 2) + c * HALF, 128), HALF)
        put_rows(shares, f, row + c * SHARE, tn(n, dh_ref[:, at]))
    dyh = dy_ref[:, pl.ds(pl.multiple_of(h * HALF, 128), HALF)]
    for u in range(CHUNKS):
        put_down(shares, f, row + CHUNKS * SHARE, tn(a_ref[:, u * D : u * D + D], dyh), u)


def share_copies(shares, keep_ref, send_ref, first, rows, sems):
    at = pl.ds(first, rows)
    return [
        pltpu.make_async_copy(shares.at[which, k, at], ref.at[k, at], sems.at[which, k])
        for which, ref in ((0, keep_ref), (1, send_ref))
        for k in range(4)
    ]


def start_all(copies):
    for copy in copies:
        copy.start()


def wait_all(copies):
    for copy in copies:
        copy.wait()


def second_kernel(pack, meta, z2_ref, g4_ref, gb_ref, bin_ref, *refs):
    count = len(pack.arrays)
    wrefs, (out_ref, g2_ref, keep_ref, send_ref) = refs[:count], refs[count : count + 4]
    wqkv, wo, win, wout, qkv, o2, probs, hs, ac, dhs, dqkv, dab, dob, shares, sems, osems = refs[count + 4 :]
    f, h = meta[0], meta[2]
    for j in range(3):
        start_square(pack, wrefs, j * SHARE, wqkv.at[j], f, sems.at[j])
    start_square(pack, wrefs, 3 * SHARE, wo, f, sems.at[3])
    start_up(pack, wrefs, 4 * SHARE, win, f, sems.at[pl.ds(4, CHUNKS)])
    start_down(pack, wrefs, 4 * SHARE + SPAN, wout, f, sems.at[pl.ds(4 + CHUNKS, CHUNKS)])
    z2 = z2_ref[...]
    m = ln(z2, gb_ref[3:4], gb_ref[8:9]).astype(BF)
    for j in range(3):
        wait_for(wqkv.at[j], sems.at[j])
        qkv[j] = nn(m, wqkv[j]).astype(BF)
    tiles = []
    for clip in range(z2.shape[0] // NLAT):
        for pair in range(PAIRS):
            tiles.append((slice(clip * NLAT, clip * NLAT + NLAT), slice(pair * 128, pair * 128 + 128)))
    for i, (rows, at) in enumerate(tiles):
        p = softmax_rows(nt(block_diag(qkv[0, rows, at]), qkv[1, rows, at]) * 0.125)
        probs[i] = p
        o2[rows, at] = diag_of(nn(p.astype(BF), qkv[2, rows, at])).astype(BF)
    wait_for(wo, sems.at[3])
    z3 = z2 + nn(o2[...], wo[...])
    n = ln(z3, gb_ref[4:5], gb_ref[9:10]).astype(BF)
    y = jnp.zeros_like(z3)
    for c in range(CHUNKS):
        wait_for(win.at[:, c * D : c * D + D], sems.at[4 + c])
    for i in range(CHUNKS):
        wait_for(wout.at[chunk_at(f, i)], sems.at[4 + CHUNKS + i])
    for i in range(CHUNKS):
        at = slice(i * D, i * D + D)
        act, slope = gelu_both(nn(n, win[:, at]) + bin_ref[1:2, at])
        hs[:, at] = slope
        a = act.astype(BF)
        ac[:, at] = a
        y = y + nn(a, wout[at, :])
    out_ref[...] = z3 + (y + gb_ref[11:12])
    dy = g4_ref[...]
    dn = jnp.zeros_like(z3)
    dbin = []
    for c in range(CHUNKS):
        at = slice(c * D, c * D + D)
        dh = (nt(dy, wout[at, :]) * hs[:, at]).astype(BF)
        dhs[:, at] = dh
        dbin += halves(column_sum(dh.astype(F32)))
        dn = dn + nt(dh, win[:, at])
    back, dgain = ln_back(z3, gb_ref[4:5], dn)
    g4 = dy.astype(F32)
    g3 = g4 + back
    ff_grads(shares, f, h, 0, n, dhs, ac, g4_ref)
    vec = halves(column_sum(dgain)) + halves(column_sum(dn)) + halves(column_sum(g4)) + dbin
    put_vec(shares, vec, 2 * SPAN, VEC)
    early = share_copies(shares, keep_ref, send_ref, 0, ROWS_F, osems.at[0])
    start_all(early)

    half = pl.ds(pl.multiple_of(h * HALF, 128), HALF)
    dab[...] = g3.astype(BF)
    dob[...] = nt(dab[...], wo[...]).astype(BF)
    put_rows(shares, f, ROWS_F + 3 * SHARE, tn(o2[...], dab[:, half]))
    for i, (rows, at) in enumerate(tiles):
        q, k, v = qkv[0, rows, at], qkv[1, rows, at], qkv[2, rows, at]
        p = probs[i]
        dobd = block_diag(dob[rows, at])
        dp = nt(dobd, v)
        ds = (p * (dp - jnp.sum(p * dp, -1, keepdims=True))).astype(BF)
        dqkv[0, rows, at] = (diag_of(nn(ds, k)) * 0.125).astype(BF)
        dqkv[1, rows, at] = (tn(ds, block_diag(q)) * 0.125).astype(BF)
        dqkv[2, rows, at] = tn(p.astype(BF), dobd).astype(BF)
    dm = jnp.zeros_like(g3)
    for j in range(3):
        dm = dm + nt(dqkv[j], wqkv[j])
        put_rows(shares, f, ROWS_F + j * SHARE, tn(m, dqkv[j, :, half]))
    back, dgain = ln_back(z2, gb_ref[3:4], dm)
    g2_ref[...] = g3 + back
    put_vec(shares, halves(column_sum(dgain)) + halves(column_sum(dm)), ROWS_F + 4 * SHARE, VEC_A)
    late = share_copies(shares, keep_ref, send_ref, ROWS_F, ROWS_A - ROWS_F, osems.at[1])
    start_all(late)
    wait_all(early + late)


def second_block(pack, meta, z2, g4, gb, bins):
    rows = z2.shape[0]
    square = pltpu.VMEM((rows, D), BF)
    return pl.pallas_call(
        functools.partial(second_kernel, pack),
        in_specs=[pl.BlockSpec(memory_space=pltpu.SMEM)] + [WHOLE] * 4 + [ANY] * len(pack.arrays),
        out_specs=[WHOLE] * 2 + [ANY] * 2,
        scratch_shapes=[
            pltpu.VMEM((3, D, D), BF),
            pltpu.VMEM((D, D), BF),
            pltpu.VMEM((D, FF), BF),
            pltpu.VMEM((FF, D), BF),
            pltpu.VMEM((3, rows, D), BF),
            square,
            pltpu.VMEM((rows // NLAT * PAIRS, 2 * NLAT, NLAT), F32),
            pltpu.VMEM((rows, FF), F32),
            pltpu.VMEM((rows, FF), BF),
            pltpu.VMEM((rows, FF), BF),
            pltpu.VMEM((3, rows, D), BF),
            square,
            square,
            pltpu.VMEM((2, 4, ROWS_A, HALF), BF),
            pltpu.SemaphoreType.DMA((4 + 2 * CHUNKS,)),
            pltpu.SemaphoreType.DMA((2, 2, 4)),
        ],
        out_shape=[
            sds((rows, D), F32),
            sds((rows, D), F32),
            sds((4, ROWS_A, HALF), BF),
            sds((4, ROWS_A, HALF), BF),
        ],
        compiler_params=PARAMS,
        cost_estimate=cost(0, 0),
        name="second_block",
    )(meta, z2, g4, gb, bins, *pack.arrays)


def fourth_kernel(pack, meta, g2_ref, z1_ref, o_ref, l_ref, gb_ref, h_ref, *refs):
    wrefs, refs = refs[: len(pack.arrays)], refs[len(pack.arrays) :]
    g1_ref, du_ref, dl_ref, keep_ref, send_ref = refs[:5]
    wo, win, wout, hs, ac, dhs, dab, dyb, shares, sems, osems = refs[5:]
    f, h = meta[0], meta[2]
    hcopy = pltpu.make_async_copy(h_ref, hs, sems.at[1])
    hcopy.start()
    start_down(pack, wrefs, SHARE + SPAN, wout, f, sems.at[pl.ds(2, CHUNKS)])
    start_up(pack, wrefs, SHARE, win, f, sems.at[pl.ds(2 + CHUNKS, CHUNKS)])
    start_square(pack, wrefs, 0, wo, f, sems.at[0])
    half = pl.ds(pl.multiple_of(h * HALF, 128), HALF)
    z1 = z1_ref[...]
    n = ln(z1, gb_ref[2:3], gb_ref[7:8]).astype(BF)
    g2 = g2_ref[...]
    dyb[...] = g2.astype(BF)
    hcopy.wait()
    for c in range(CHUNKS):
        at = slice(c * D, c * D + D)
        act, slope = gelu_both(hs[:, at])
        ac[:, at] = act.astype(BF)
        hs[:, at] = slope
    for i in range(CHUNKS):
        wait_for(wout.at[chunk_at(f, i)], sems.at[2 + i])
    for c in range(CHUNKS):
        wait_for(win.at[:, c * D : c * D + D], sems.at[2 + CHUNKS + c])
    dn = jnp.zeros_like(g2)
    dbin = []
    for c in range(CHUNKS):
        at = slice(c * D, c * D + D)
        dh = (nt(dyb[...], wout[at, :]) * hs[:, at]).astype(BF)
        dhs[:, at] = dh
        dbin += halves(column_sum(dh.astype(F32)))
        dn = dn + nt(dh, win[:, at])
    back, dgain = ln_back(z1, gb_ref[2:3], dn)
    g1 = g2 + back
    g1_ref[...] = g1
    ff_grads(shares, f, h, 0, n, dhs, ac, dyb)
    vec = halves(column_sum(dgain)) + halves(column_sum(dn))
    vec += halves(column_sum(dyb[...].astype(F32))) + dbin
    put_vec(shares, vec, 2 * SPAN + SHARE, VEC_B)

    dab[...] = g1.astype(BF)
    wait_for(wo, sems.at[0])
    do = nt(dab[...], wo[...]).astype(BF).astype(F32)
    put_rows(shares, f, 2 * SPAN, tn(o_ref[...], dab[:, half]))
    low = low_lanes(g2.shape[0])
    lane = lax.broadcasted_iota(jnp.int32, low.shape, 1)
    l = l_ref[...]
    dl = jnp.zeros(low.shape, F32)
    for j in range(PAIRS):
        at = slice(128 * j, 128 * j + 128)
        first, later = l[:, 2 * j : 2 * j + 1], l[:, 2 * j + 1 : 2 * j + 2]
        du_ref[:, at] = (do[:, at] / jnp.where(low, first, later)).astype(BF)
        t = do[:, at] * o_ref[:, at].astype(F32)
        t_first = -jnp.sum(jnp.where(low, t, 0.0), -1, keepdims=True) / first
        t_later = -jnp.sum(jnp.where(low, 0.0, t), -1, keepdims=True) / later
        dl = jnp.where(lane == 2 * j, t_first, jnp.where(lane == 2 * j + 1, t_later, dl))
    dl_ref[...] = dl
    late = share_copies(shares, keep_ref, send_ref, 0, ROWS_B, osems)
    start_all(late)
    wait_all(late)


def fourth_block(pack, meta, g2, z1, o, l, gb, hidden):
    rows = z1.shape[0]
    arrays = pack.arrays
    return pl.pallas_call(
        functools.partial(fourth_kernel, pack),
        in_specs=[pl.BlockSpec(memory_space=pltpu.SMEM)] + [WHOLE] * 5 + [ANY] * (1 + len(arrays)),
        out_specs=[WHOLE] * 3 + [ANY] * 2,
        scratch_shapes=[
            pltpu.VMEM((D, D), BF),
            pltpu.VMEM((D, FF), BF),
            pltpu.VMEM((FF, D), BF),
            pltpu.VMEM((rows, FF), F32),
            pltpu.VMEM((rows, FF), BF),
            pltpu.VMEM((rows, FF), BF),
            pltpu.VMEM((rows, D), BF),
            pltpu.VMEM((rows, D), BF),
            pltpu.VMEM((2, 4, ROWS_B, HALF), BF),
            pltpu.SemaphoreType.DMA((2 + 2 * CHUNKS,)),
            pltpu.SemaphoreType.DMA((2, 4)),
        ],
        out_shape=[
            sds((rows, D), F32),
            sds((rows, D), BF),
            sds((rows, 128), F32),
            sds((4, ROWS_B, HALF), BF),
            sds((4, ROWS_B, HALF), BF),
        ],
        compiler_params=PARAMS,
        cost_estimate=cost(30 * rows * D * D, 12 * D * D * 4),
        name="fourth_block",
    )(meta, g2, z1, o, l, gb, hidden, *arrays)


def attend_back_kernel(q_ref, du_ref, dl_ref, mask_ref, k_ref, v_ref, dk_ref, dv_ref, dq_ref, dlt):
    group = pl.program_id(1)

    @pl.when(group == 0)
    def _():
        dlt[...] = dl_ref[0].T

    mask = mask_ref[0]
    mask = jnp.concatenate([mask, mask], 1)
    upper = lax.broadcasted_iota(jnp.int32, (128, NLAT), 0) < HEAD
    for p in range(BACK_PAIRS):
        pair = group * BACK_PAIRS + p
        mine = slice(p * 128, p * 128 + 128)
        qbd, dubd = block_diag(q_ref[0, :, mine]), block_diag(du_ref[0, :, mine])
        line = [dlt[pl.ds(2 * pair + i, 1), :] for i in range(2)]
        k, v = k_ref[0, :, mine], v_ref[0, :, mine]
        e = jnp.exp(nt(k, qbd) + mask)
        ds = (e * (nt(v, dubd) + jnp.concatenate(line, 1))).astype(BF)
        dv_ref[0, :, mine] = nn(e.astype(BF), dubd).astype(BF)
        dk_ref[0, :, mine] = nn(ds, qbd).astype(BF)
        dqt = tn(k, ds)
        dqt = jnp.where(upper, dqt[:, :NLAT], dqt[:, NLAT:])
        dq_ref[0, :, mine] = (dqt.T * 0.125).astype(BF)


def attend_back(q, du, dl, mask, k, v):
    clips, padded = k.shape[0], k.shape[1]
    wide = 128 * BACK_PAIRS
    small = pl.BlockSpec((1, NLAT, wide), lambda i, j: (i, 0, j))
    whole = pl.BlockSpec((1, NLAT, 128), lambda i, j: (i, 0, 0))
    column = pl.BlockSpec((1, padded, 128), lambda i, j: (i, 0, 0))
    lanes = pl.BlockSpec((1, padded, wide), lambda i, j: (i, 0, j))
    return pl.pallas_call(
        attend_back_kernel,
        grid=(clips, PAIRS // BACK_PAIRS),
        in_specs=[small, small, whole, column, lanes, lanes],
        out_specs=[lanes, lanes, small],
        scratch_shapes=[pltpu.VMEM((128, NLAT), F32)],
        out_shape=[sds((clips, padded, D), BF)] * 2 + [sds((clips, NLAT, D), BF)],
        compiler_params=PARAMS,
        cost_estimate=cost(0, 0),
        name="attend_back",
    )(q, du, dl, mask, k, v)


def keyval_grad_kernel(meta, xl_ref, dk_ref, dv_ref, keep_ref, send_ref, sum_ref, acc, shares, sems):
    f = meta[0]
    step = pl.program_id(0)
    first = step == 0
    xt = xl_ref[0].T
    for j, ref in enumerate((dk_ref, dv_ref)):
        grad = nn(xt, ref[0])
        acc[j] = grad + jnp.where(first, 0.0, acc[j])
        line = column_sum(ref[0].astype(F32))
        sum_ref[j : j + 1, :] = line + jnp.where(first, 0.0, sum_ref[j : j + 1, :])

    @pl.when(step == pl.num_programs(0) - 1)
    def _():
        for j in range(2):
            for g in range(OWNERS):
                rel = f ^ g
                grad = acc[j, g * SHARE : g * SHARE + SHARE, :].astype(BF)
                shares[rel & 1, rel >> 1, j * SHARE : j * SHARE + SHARE, :] = grad
        copies = share_copies(shares, keep_ref, send_ref, 0, 2 * SHARE, sems)
        start_all(copies)
        wait_all(copies)


def keyval_grad(meta, xl, dk, dv):
    clips, padded = xl.shape[0], xl.shape[1]
    tile = padded // GRAD_TILES
    at = lambda i, m: (i // GRAD_TILES, lax.rem(i, GRAD_TILES), 0)
    block = pl.BlockSpec((1, tile, D), at)
    return pl.pallas_call(
        keyval_grad_kernel,
        grid_spec=pltpu.PrefetchScalarGridSpec(
            num_scalar_prefetch=1,
            grid=(clips * GRAD_TILES,),
            in_specs=[block] * 3,
            out_specs=[ANY, ANY, pl.BlockSpec((8, D), lambda i, m: (0, 0))],
            scratch_shapes=[
                pltpu.VMEM((2, D, D), F32),
                pltpu.VMEM((2, 4, 2 * SHARE, D), BF),
                pltpu.SemaphoreType.DMA((2, 4)),
            ],
        ),
        out_shape=[sds((4, ROWS_K, D), BF), sds((4, ROWS_K, D), BF), sds((8, D), F32)],
        compiler_params=PARAMS,
        cost_estimate=cost(4 * clips * padded * D * D, clips * padded * D * 6),
        name="keyval_grad",
    )(meta, xl, dk, dv)


def query_grad_kernel(pack, count, meta, *refs):
    own_ref, parts, refs = refs[0], refs[1:count], refs[count:]
    lat_ref, gb_ref, sum_ref, keep_in, send_in = refs[:5]
    refs = refs[5:]
    n_w = len(pack.arrays)
    wrefs, (back_ref, keep_ref, send_ref, wq, shares, sem, osems) = refs[:n_w], refs[n_w:]
    f = meta[0]
    start_square(pack, wrefs, 2 * SHARE, wq, f, sem.at[0])
    total = own_ref[...].astype(F32)
    for part in parts:
        total = total + part[...].astype(F32)
    dq = total.astype(BF)
    lat = lat_ref[...].astype(F32)
    zl = ln(lat, gb_ref[0:1], gb_ref[5:6]).astype(BF)
    grad = tn(zl, dq).astype(BF)
    for g in range(OWNERS):
        rel = f ^ g
        shares[rel & 1, rel >> 1, 0:SHARE, :] = grad[g * SHARE : g * SHARE + SHARE]
    wait_for(wq, sem.at[0])
    dzl = nt(dq, wq[...])
    back, dgain = ln_back(lat, gb_ref[0:1], dzl)
    back_ref[...] = back.astype(BF)
    lines = [sum_ref[0:1], sum_ref[1:2], column_sum(dgain), column_sum(dzl)]
    vec = jnp.concatenate(lines + [jnp.zeros((VEC_K - 4, D), F32)], 0).astype(BF)
    copies = []
    for which, ref in ((0, keep_ref), (1, send_ref)):
        for k in range(4):
            shares[which, k, SHARE : SHARE + VEC_K, :] = vec
            copies.append(
                pltpu.make_async_copy(
                    shares.at[which, k],
                    ref.at[k, pl.ds(2 * SHARE, SHARE + VEC_K)],
                    osems.at[which, k],
                )
            )
    for copy in copies:
        copy.start()
    for copy in copies:
        copy.wait()


def query_grad(pack, meta, dq, parts, lat, gb, sums, keep, send):
    rows = parts[0].shape[0] if parts else dq.shape[0]
    count = 1 + len(parts)
    mine = pl.BlockSpec((rows, D), lambda i, m: (m[1], 0))
    fixed = lambda shape: pl.BlockSpec(shape, lambda i, m: (0,) * len(shape))
    return pl.pallas_call(
        functools.partial(query_grad_kernel, pack, count),
        grid_spec=pltpu.PrefetchScalarGridSpec(
            num_scalar_prefetch=1,
            grid=(1,),
            in_specs=[mine]
            + [fixed((rows, D))] * len(parts)
            + [mine, fixed((16, D)), fixed((8, D)), ANY, ANY]
            + [ANY] * len(pack.arrays),
            out_specs=[fixed((rows, D)), ANY, ANY],
            scratch_shapes=[
                pltpu.VMEM((D, D), BF),
                pltpu.VMEM((2, 4, SHARE + VEC_K, D), BF),
                pltpu.SemaphoreType.DMA((1,)),
                pltpu.SemaphoreType.DMA((2, 4)),
            ],
        ),
        out_shape=[sds((rows, D), BF), sds(keep.shape, BF), sds(send.shape, BF)],
        input_output_aliases={count + 4: 1, count + 5: 2},
        compiler_params=PARAMS,
        name="query_grad",
    )(meta, dq, *parts, lat, gb, sums, keep, send, *pack.arrays)


def token_grad_kernel(pack, local, meta, x_ref, gb_ref, dk_ref, dv_ref, *refs):
    count = len(pack.arrays)
    wrefs, (out_ref, wkv, lines, sems, osems) = refs[:count], refs[count:]
    clip, at = pl.program_id(0), pl.program_id(1)
    clips, tiles = pl.num_programs(0), pl.num_programs(1)
    tile = x_ref.shape[1]
    n_clips, n_tiles = out_ref.shape[0] // (local * PAIRS), -(-local // tile)

    @pl.when((clip == 0) & (at == 0))
    def _():
        f = meta[0]
        start_square(pack, wrefs, 0, wkv.at[0], f, sems.at[0])
        start_square(pack, wrefs, SHARE, wkv.at[1], f, sems.at[1])
        wait_for(wkv.at[0], sems.at[0])
        wait_for(wkv.at[1], sems.at[1])

    for first in range(0, tile, TOKEN_ROWS):
        rows = slice(first, first + TOKEN_ROWS)
        grad = nt(dk_ref[0, rows, :], wkv[0]) + nt(dv_ref[0, rows, :], wkv[1])
        back, unused = ln_back(x_ref[0, rows, :].astype(F32), gb_ref[1:2], grad)
        base = (clip * local + at * tile + first) * PAIRS
        for t in range(PAIRS):
            lines[pl.ds(base + t, TOKEN_ROWS, stride=PAIRS), :] = back[:, 128 * t : 128 * t + 128]

    def piece(c, i):
        first = (c * local + i * tile) * PAIRS // 8 * 8
        last = (c * local + min((i + 1) * tile, local)) * PAIRS
        last = last if c == n_clips - 1 and i == n_tiles - 1 else last // 8 * 8
        where = pl.ds(first, last - first)
        slot = c * n_tiles + i
        return pltpu.make_async_copy(lines.at[where], out_ref.at[where], osems.at[slot])

    for c in range(n_clips):
        for i in range(n_tiles):

            @pl.when((clip == c) & (at == i))
            def _(c=c, i=i):
                piece(c, i).start()

    @pl.when((clip == n_clips - 1) & (at == n_tiles - 1))
    def _():
        for c in range(n_clips):
            for i in range(n_tiles):
                piece(c, i).wait()


def token_grad(pack, meta, tokens, gb, dk, dv):
    clips, local = tokens.shape[0], tokens.shape[1]
    padded = dk.shape[1]
    tile = padded // TOKEN_TILES
    block = pl.BlockSpec((1, tile, D), lambda i, j, m: (i, j, 0))
    rows = clips * local * PAIRS
    return pl.pallas_call(
        functools.partial(token_grad_kernel, pack, local),
        grid_spec=pltpu.PrefetchScalarGridSpec(
            num_scalar_prefetch=1,
            grid=(clips, padded // tile),
            in_specs=[block, pl.BlockSpec((16, D), lambda i, j, m: (0, 0)), block, block]
            + [ANY] * len(pack.arrays),
            out_specs=ANY,
            scratch_shapes=[
                pltpu.VMEM((2, D, D), BF),
                pltpu.VMEM((rows + (padded - local) * PAIRS + 8, 128), F32),
                pltpu.SemaphoreType.DMA((2,)),
                pltpu.SemaphoreType.DMA((clips * TOKEN_TILES,)),
            ],
        ),
        out_shape=sds((rows, 128), F32),
        compiler_params=PARAMS,
        cost_estimate=cost(4 * clips * padded * D * D, clips * padded * D * 10),
        name="token_grad",
    )(meta, tokens, gb, dk, dv, *pack.arrays)


def fold_kernel(keep_ref, recv_ref, *out_refs):
    for k, ref in enumerate(out_refs):
        ref[...] = (keep_ref[k].astype(F32) + recv_ref[k].astype(F32)).astype(BF)


def row_block(rows):
    return rows // 2 if rows % 32 == 0 else rows


def fold(keep, recv):
    rows, lanes = keep.shape[1:]
    step = row_block(rows)
    block = pl.BlockSpec((4, step, lanes), lambda i: (0, i, 0))
    return pl.pallas_call(
        fold_kernel,
        grid=(rows // step,),
        in_specs=[block, block],
        out_specs=[pl.BlockSpec((step, lanes), lambda i: (i, 0))] * 4,
        out_shape=[sds((rows, lanes), BF)] * 4,
        compiler_params=PARAMS,
        name="fold",
    )(keep, recv)


def both(x, y):
    return (x.astype(F32) + y.astype(F32)).astype(BF)


def split_kernel(mine_p, recv_p, mine_q, recv_q, keep_p, keep_q, send_p, send_q):
    for at, k in enumerate((0, 2)):
        keep_p[at] = both(mine_p[k], recv_p[k])
        send_p[at] = both(mine_p[k + 1], recv_p[k + 1])
        keep_q[at] = both(mine_q[at], recv_q[at])
        send_q[at] = both(mine_q[at + 2], recv_q[at + 2])


def split(keep, recv):
    rows, lanes = keep.shape[1:]
    step = rows // 2 // STEPS
    first = pl.BlockSpec((4, step, lanes), lambda i: (0, i, 0))
    later = pl.BlockSpec((4, step, lanes), lambda i: (0, i + STEPS, 0))
    return pl.pallas_call(
        split_kernel,
        grid=(STEPS,),
        in_specs=[first, first, later, later],
        out_specs=[pl.BlockSpec((2, step, lanes), lambda i: (0, i, 0))] * 4,
        out_shape=[sds((2, rows // 2, lanes), BF)] * 4,
        compiler_params=PARAMS,
        name="split",
    )(keep, recv, keep, recv)


def turn_kernel(keep_p, keep_q, recv_p, recv_q, own_ref, send_p, send_q):
    for i, (keep, recv, send) in enumerate(((keep_p, recv_p, send_p), (keep_q, recv_q, send_q))):
        own_ref[i] = both(keep[0], recv[0])
        send[...] = both(keep[1], recv[1])


def turn(keep_p, keep_q, recv_p, recv_q):
    half, lanes = keep_p.shape[1:]
    step = half // STEPS
    pair = pl.BlockSpec((2, step, lanes), lambda i: (0, i, 0))
    one = pl.BlockSpec((step, lanes), lambda i: (i, 0))
    return pl.pallas_call(
        turn_kernel,
        grid=(STEPS,),
        in_specs=[pair] * 4,
        out_specs=[pair, one, one],
        out_shape=[sds((2, half, lanes), BF), sds((half, lanes), BF), sds((half, lanes), BF)],
        compiler_params=PARAMS,
        name="turn",
    )(keep_p, keep_q, recv_p, recv_q)


def join_kernel(own_ref, recv_p, recv_q, out_ref):
    out_ref[0] = both(own_ref[0], recv_p[...])
    out_ref[1] = both(own_ref[1], recv_q[...])


def join(own, recv_p, recv_q):
    half, lanes = recv_p.shape
    step = half // STEPS
    pair = pl.BlockSpec((2, step, lanes), lambda i: (0, i, 0))
    one = pl.BlockSpec((step, lanes), lambda i: (i, 0))
    return pl.pallas_call(
        join_kernel,
        grid=(STEPS,),
        in_specs=[pair, one, one],
        out_specs=pair,
        out_shape=sds((2, half, lanes), BF),
        compiler_params=PARAMS,
        cost_estimate=pl.CostEstimate(flops=0, bytes_accessed=20 * half * lanes, transcendentals=0),
        name="join",
    )(own, recv_p, recv_q).reshape(2 * half, lanes)


def sum_kernel(*refs):
    total = refs[0][...].astype(F32)
    for ref in refs[1:-1]:
        total = total + ref[...].astype(F32)
    refs[-1][...] = total.astype(BF)


def sum_of(parts):
    rows, lanes = parts[0].shape
    step = row_block(rows)
    block = pl.BlockSpec((step, lanes), lambda i: (i, 0))
    return pl.pallas_call(
        sum_kernel,
        grid=(rows // step,),
        in_specs=[block] * len(parts),
        out_specs=block,
        out_shape=sds((rows, lanes), BF),
        compiler_params=PARAMS,
        name="sum_parts",
    )(*parts)


def chunk_sums_kernel(meta, *refs):
    parts, outs = refs[:4], refs[4:]
    count = len(outs)
    step = outs[0].shape[0]
    for k, out in enumerate(outs):
        rows = pl.ds(pl.multiple_of(lax.rem(meta[1] + k, count) * step, step), step)
        total = parts[0][rows, :].astype(F32)
        for part in parts[1:]:
            total = total + part[rows, :].astype(F32)
        out[...] = total.astype(BF)


def chunk_sums(meta, parts, count=4):
    rows, lanes = parts[0].shape
    return pl.pallas_call(
        chunk_sums_kernel,
        in_specs=[pl.BlockSpec(memory_space=pltpu.SMEM)] + [WHOLE] * len(parts),
        out_specs=[WHOLE] * count,
        out_shape=[sds((rows // count, lanes), BF)] * count,
        compiler_params=PARAMS,
        name="chunk_sums",
    )(meta, *parts)


def after(x, *others):
    return lax.optimization_barrier((x, others))[0]


def exchange(x, bit):
    return lax.ppermute(x, "fsdp", [(i, i ^ bit) for i in range(OWNERS)])


def sum_over_fsdp(keep, send):
    full = jnp.stack([keep, send], 1).reshape(OWNERS, *keep.shape[1:])
    return lax.psum(full.astype(F32), "fsdp").astype(BF)


def finish_latent_kernel(count, meta, ma_ref, oa_ref, mb_ref, ob_ref, g1_ref, *refs):
    pieces, refs = refs[:count], refs[count:]
    lat_ref, qkv_ref, outw_ref, up_ref, down_ref, line_ref = refs
    s, h = meta[1], meta[2]
    step = pieces[0].shape[0]
    for k, piece in enumerate(pieces):
        rows = pl.ds(pl.multiple_of(lax.rem(s - k + count, count) * step, step), step)
        lat_ref[rows, :] = g1_ref[rows, :] + piece[...].astype(F32)
    for a_ref, b_ref, side in ((ma_ref, mb_ref, h), (oa_ref, ob_ref, 1 - h)):
        half = pl.ds(pl.multiple_of(side * HALF, 128), HALF)
        for layer, ref in ((1, a_ref), (0, b_ref)):
            for c in range(CHUNKS):
                at = pl.ds(pl.multiple_of(side * (FF // 2) + c * HALF, 128), HALF)
                up_ref[layer, :, at] = ref[c * SHARE : c * SHARE + SHARE, :].astype(F32)
            down_ref[layer, :, half] = ref[SPAN : 2 * SPAN, :].astype(F32)
        for i in range(4):
            first = ROWS_F + i * SHARE
            value = a_ref[first : first + SHARE, :].astype(F32)
            if i < 3:
                qkv_ref[0, i, :, half] = value
            else:
                outw_ref[1, :, half] = value
        outw_ref[0, :, half] = b_ref[2 * SPAN : 2 * SPAN + SHARE, :].astype(F32)
    last = ma_ref[2 * SPAN : ROWS_F, :].astype(F32)
    middle = ma_ref[ROWS_A - VEC_A : ROWS_A, :].astype(F32)
    first = mb_ref[ROWS_B - VEC_B : ROWS_B, :].astype(F32)
    line_ref[...] = jnp.zeros_like(line_ref)
    picks = [(first, 0), (middle, 0), (last, 0), (first, 1), (middle, 1), (last, 1), (first, 2), (last, 2)]
    picks += [(first, 3 + c) for c in range(CHUNKS)] + [(last, 3 + c) for c in range(CHUNKS)]
    for i, (vec, row) in enumerate(picks):
        for part in range(2):
            at = slice(part * HALF, part * HALF + HALF)
            line_ref[i : i + 1, at] = vec[2 * row + part : 2 * row + part + 1, :]


def finish_latent(meta, mine_f, other_f, mine_s, other_s, g1, pieces):
    rows = g1.shape[0]
    whole = lambda shape: pl.BlockSpec(shape, lambda i: (0,) * len(shape))
    return pl.pallas_call(
        functools.partial(finish_latent_kernel, len(pieces)),
        grid=(1,),
        in_specs=[pl.BlockSpec(memory_space=pltpu.SMEM)] + [WHOLE] * (5 + len(pieces)),
        out_specs=[
            whole((rows, D)),
            pl.BlockSpec((1, 3, SHARE, D), lambda i: (1, 0, 0, 0)),
            whole((2, SHARE, D)),
            whole((2, SHARE, FF)),
            whole((2, CHUNKS * SHARE, D)),
            whole((16, D)),
        ],
        out_shape=[
            sds((rows, D), F32),
            sds((2, 3, SHARE, D), F32),
            sds((2, SHARE, D), F32),
            sds((2, SHARE, FF), F32),
            sds((2, CHUNKS * SHARE, D), F32),
            sds((16, D), F32),
        ],
        compiler_params=PARAMS,
        name="finish_latent",
    )(meta, mine_f, other_f, mine_s, other_s, g1, *pieces)


def finish_token_kernel(count, meta, *refs):
    pieces, refs = refs[:count], refs[count:]
    w_ref, gain_ref, shift_ref, line_ref, qkv_in, qkv_ref, gain_out, shift_out, bin_out, bout_out, whole = refs
    f, s = meta[0], meta[1]
    step = pieces[0].shape[0]
    for k, piece in enumerate(pieces):
        rows = pl.ds(pl.multiple_of(lax.rem(s - k + count, count) * step, step), step)
        whole[rows, :] = piece[...].astype(F32)
    dk, dv, dq = (whole[i * SHARE : i * SHARE + SHARE, :] for i in range(3))
    qkv_ref[0, 0], qkv_ref[0, 1], qkv_ref[0, 2] = dq, dk, dv
    vec = whole[3 * SHARE : 3 * SHARE + 8, :]
    wk, wv = w_ref[0].astype(F32), w_ref[1].astype(F32)
    shift_sum = jnp.sum(wk * vec[0:1] + wv * vec[1:2], -1, keepdims=True)
    gain_sum = jnp.sum(wk * dk + wv * dv, -1, keepdims=True)
    lane = lax.broadcasted_iota(jnp.int32, (SHARE, 128), 1)
    turned = jnp.where(lane == 0, shift_sum, jnp.where(lane == 1, gain_sum, 0.0)).T
    db, total = turned[0:1, :SHARE], turned[1:2, :SHARE]
    dg = (total - shift_ref[1:2, :].astype(F32) * db) / gain_ref[1:2, :].astype(F32)
    lines = jnp.concatenate([line_ref[...], vec], 0)
    cut = pltpu.roll(lines, lax.rem(D - f * SHARE, D), 1)[:, :SHARE]
    gain_out[0:1, :], gain_out[1:2, :], gain_out[2:5, :] = cut[18:19], dg, cut[0:3]
    shift_out[0:1, :], shift_out[1:2, :], shift_out[2:5, :] = cut[19:20], db, cut[3:6]
    bout_out[...] = cut[6:8]
    wide = jnp.concatenate([line_ref[8 + c : 9 + c, :] for c in range(CHUNKS)], 1)
    other = jnp.concatenate([line_ref[12 + c : 13 + c, :] for c in range(CHUNKS)], 1)
    both = jnp.concatenate([wide, other], 0)
    span = CHUNKS * SHARE
    total = jnp.zeros((2, span), F32)
    for g in range(OWNERS):
        total = jnp.where(f == g, both[:, g * span : g * span + span], total)
    bin_out[...] = total


def finish_token(meta, pieces, weights, gain, shift, lines, qkv):
    whole = lambda shape: pl.BlockSpec(shape, lambda i: (0,) * len(shape))
    count = len(pieces)
    return pl.pallas_call(
        functools.partial(finish_token_kernel, count),
        grid=(1,),
        in_specs=[pl.BlockSpec(memory_space=pltpu.SMEM)] + [WHOLE] * (count + 4) + [ANY],
        out_specs=[
            pl.BlockSpec((1, 3, SHARE, D), lambda i: (0, 0, 0, 0)),
            whole((5, SHARE)),
            whole((5, SHARE)),
            whole((2, CHUNKS * SHARE)),
            whole((2, SHARE)),
        ],
        out_shape=[
            sds(qkv.shape, F32),
            sds((5, SHARE), F32),
            sds((5, SHARE), F32),
            sds((2, CHUNKS * SHARE), F32),
            sds((2, SHARE), F32),
        ],
        scratch_shapes=[pltpu.VMEM((ROWS_K, D), F32)],
        input_output_aliases={count + 5: 0},
        compiler_params=PARAMS,
        name="finish_token",
    )(meta, *pieces, weights, gain, shift, lines, qkv)


def unpack(left_a, right_a, left_b, right_b, whole_k):
    sides_a, sides_b = (left_a, right_a), (left_b, right_b)

    def up(sides):
        return jnp.concatenate(
            [x[c * SHARE : c * SHARE + SHARE] for x in sides for c in range(CHUNKS)], 1
        )

    def rows(sides, at, span=SHARE):
        return jnp.concatenate([x[at : at + span] for x in sides], 1)

    q1, k1, v1, out1 = (rows(sides_a, ROWS_F + i * SHARE) for i in range(4))
    out0 = rows(sides_b, 2 * SPAN)
    k0, v0, q0 = (whole_k[i * SHARE : i * SHARE + SHARE] for i in range(3))
    return (
        jnp.stack([jnp.stack([q0, k0, v0]), jnp.stack([q1, k1, v1])]).astype(F32),
        jnp.stack([out0, out1]).astype(F32),
        jnp.stack([up(sides_b), up(sides_a)]).astype(F32),
        jnp.stack([rows(sides_b, SPAN, SPAN), rows(sides_a, SPAN, SPAN)]).astype(F32),
    )


def per_device(size, seq, *args):
    (
        latents_in,
        inputs,
        clip_frames,
        text_mask,
        qkv_weight,
        out_weight,
        mlp_in,
        mlp_out,
        norm_gain,
        norm_bias,
        bias_in,
        bias_out,
        out_cotangent,
    ) = args
    micro, clips, nlat, _ = latents_in.shape
    count = micro * clips
    local = inputs.shape[2]
    padded = -(-local // 128) * 128
    rows = count * nlat
    s = lax.axis_index("seq")
    fsdp = lax.axis_index("fsdp")
    special = size == OWNERS
    meta = jnp.stack([fsdp if special else jnp.int32(0), s, s % 2]).astype(jnp.int32)
    lat = latents_in.reshape(rows, D)
    tokens = inputs.reshape(count, local, D)
    g4 = out_cotangent.reshape(rows, D)

    place = s * local + jnp.arange(padded, dtype=jnp.int32)
    frames = clip_frames.reshape(count, 1) * PATCHES
    text = text_mask.reshape(count, -1) > 0
    text_len = text.shape[1]
    slots = FRAMES * PATCHES
    wide = jnp.pad(text, ((0, 0), (slots, padded)))
    text_here = lax.dynamic_slice_in_dim(wide, s * local, padded, 1)
    valid = jnp.where(place[None] < slots, place[None] < frames, text_here)
    valid = valid & (jnp.arange(padded)[None] < local)
    bias = jnp.where(valid, 0.0, -1e30).astype(F32)
    mask = jnp.broadcast_to(bias[:, :, None], (count, padded, 128))

    def slabs(up):
        return up.reshape(SHARE, CHUNKS, D).transpose(1, 0, 2).reshape(SPAN, D)

    def pack_keyval(qkv, out, up, down, gain, shift, up_b, down_b):
        small = jnp.concatenate(
            [
                jnp.pad(jnp.concatenate([gain, shift, down_b], 0), ((0, 0), (0, 128 - SHARE))),
                up_b.reshape(6, 128),
                jnp.zeros((14, 128), BF),
            ],
            0,
        )
        small = jnp.concatenate([small[:16], small[16:]], 1)
        small = jnp.pad(small, ((0, 0), (0, D - 256)))
        return jnp.concatenate([qkv[0, 1], qkv[0, 2], qkv[0, 0], small], 0)

    def pack_first(qkv, out, up, down, *rest):
        return jnp.concatenate([out[0], slabs(up[0]), down[0]], 0)

    def pack_last(qkv, out, up, down, *rest):
        return jnp.concatenate([qkv[1].reshape(3 * SHARE, D), out[1], slabs(up[1]), down[1]], 0)

    packers = (pack_keyval, pack_first, pack_last)
    weights = (qkv_weight, out_weight, mlp_in, mlp_out, norm_gain, norm_bias, bias_in, bias_out)
    axes = (2, 1, 1, 1, 1, 1, 1, 1)
    def shift_to(x, k):
        return lax.ppermute(x, "seq", [(i, (i + k) % seq) for i in range(seq)])

    def scatter_rows(x):
        step = x.shape[0] // seq
        out = []
        for k in range(1, seq):
            piece = lax.dynamic_slice_in_dim(x, ((s + k) % seq) * step, step, 0)
            out.append(shift_to(piece, k))
        return out

    def gather_rows(x):
        return [x] + [shift_to(x, k) for k in range(1, seq)]

    pair = [(i, i ^ 1) for i in range(seq)]

    if special:
        def direct(x):
            return {0: x, 2: exchange(x, 2), 4: exchange(x, 4), 6: exchange(x, 6)}

        def direct_pack(p, later):
            arrays = [p[m] if m % 2 == 0 else exchange(later(p[m - 1]), 1) for m in range(OWNERS)]
            return Pack(arrays, lambda m, row: (m, None, row))

        def relay_pack(parts):
            half = parts[3].shape[0]
            arrays = []
            for x in parts:
                arrays += [x, exchange(x, 1)]

            def where(m, row):
                if m < 6:
                    return (m, None, row)
                return (m, None, row) if row < half else (m + 2, None, row - half)

            return Pack(arrays, where)

        x1 = pack_keyval(*weights)
        p1 = direct(x1)
        x3 = pack_last(*after(weights, x1))
        x3_2, x3_4 = exchange(x3, 2), exchange(x3, 4)
        tokens = with_layout_constraint(tokens, Layout(major_to_minor=(0, 1, 2)))
        bias, tokens = after((bias, tokens), x3)
        g1 = direct_pack(p1, lambda x: after(x, p1[2], tokens))
        xl, k, v, gb, bins = keyval(g1, meta, tokens, local, padded)
        mask = after(bias, k)
        mask = jnp.broadcast_to(mask[:, :, None], (count, padded, 128))
        pay, q = attend(g1, meta, lat, gb, bias[:, None, :], k, v)
        pay = pay.reshape(rows, PAY)
        arrived = scatter_rows(pay)
        x2 = pack_first(*after(weights, k))
        x3_2, x3_4, x2 = after((x3_2, x3_4, x2), pay)
        half = x3.shape[0] // 2
        turn_2, turn_4 = x3_2[:half], x3_4[half:]
        x2_2, x2_4 = exchange(x2, 2), exchange(x2, 4)
        share = combine(meta, after(pay, mask), arrived)
        parts = gather_rows(share)
        turn_2, turn_4, x2_2, x2_4 = after((turn_2, turn_4, x2_2, x2_4), parts)
        half = SHARE + SPAN
        x2_6a, x2_6b = exchange(x2_2[:half], 4), exchange(x2_4[half:], 2)
        x3_6a, x3_6b = exchange(turn_2, 4), exchange(turn_4, 2)
        g2 = relay_pack([x2, *after((x2_2, x2_4), x2_6a, x2_6b), x2_6a, x2_6b])
        o, l, z1, z2, hidden = first_block(g2, meta, parts, lat, gb, bins)
        x3_6a, x3_6b = after((x3_6a, x3_6b), z2)
        g34 = relay_pack([x3, x3_2, x3_4, x3_6a, x3_6b])
    else:
        full = []
        for w, axis in zip(weights, axes):
            whole = lax.all_gather(w, "fsdp", axis=axis, tiled=True)
            shape = whole.shape
            parts = whole.reshape(*shape[:axis], OWNERS, shape[axis] // OWNERS, *shape[axis + 1 :])
            full.append(jnp.moveaxis(parts, axis, 0))
        raw = [jax.vmap(packer)(*full) for packer in packers]
        g1, g2, g34 = [Pack([x], lambda m, row: (0, m, row)) for x in raw]
        xl, k, v, gb, bins = keyval(g1, meta, tokens, local, padded)
        pay, q = attend(g1, meta, lat, gb, bias[:, None, :], k, v)
        pay = pay.reshape(rows, PAY)
        share = combine(meta, pay, scatter_rows(pay))
        o, l, z1, z2, hidden = first_block(g2, meta, gather_rows(share), lat, gb, bins)
    out, g2_lat, keep_a, send_a = second_block(g34, meta, z2, g4, gb, bins)

    grad_one, du, dl, keep_b, send_b = fourth_block(g2, meta, g2_lat, z1, o, l, gb, hidden)
    cube = lambda x: x.reshape(count, nlat, x.shape[-1])
    shapes = (latents_in.shape, inputs.shape)
    if special:
        recv_a, recv_b = exchange(send_a, 1), exchange(send_b, 1)
        split_a = split(*after((keep_a, recv_a), du))
        split_b = split(*after((keep_b, recv_b), *split_a))
        du, dl = after((du, dl), *split_a, *split_b)
        dk, dv, dq = attend_back(cube(q), cube(du), cube(dl), mask, k, v)
        dq = dq.reshape(rows, D)
        first_a = (*split_a[:2], exchange(split_a[2], 2), exchange(split_a[3], 4))
        first_b = (*split_b[:2], exchange(split_b[2], 2), exchange(split_b[3], 4))
        turn_a = turn(*after(first_a, dq))
        second_a = (turn_a[0], exchange(turn_a[1], 4), exchange(turn_a[2], 2))
        keep_k, send_k, sums = keyval_grad(meta, *after((xl, dk, dv), *turn_a))
        dq = after(dq, sums)
        dq_parts = scatter_rows(dq)
        turn_b = turn(*after(first_b, sums))
        second_b = (turn_b[0], exchange(turn_b[1], 4), exchange(turn_b[2], 2))
        mine_a = join(*after(second_a, *turn_b))
        mine_b = join(*after(second_b, mine_a))
        dq, dq_parts = after((dq, dq_parts), mine_b)
        back, keep_k, send_k = query_grad(g1, meta, dq, dq_parts, lat, gb, sums, keep_k, send_k)
        recv_k = exchange(send_k, 1)
        fold_k = fold(keep_k, recv_k)
        other_a = lax.ppermute(mine_a, "seq", pair)
        other_b = lax.ppermute(mine_b, "seq", pair)
        hop_k = [exchange(x, 2 * i) for i, x in enumerate(fold_k) if i]
        token_grads = token_grad(g1, meta, tokens, gb, *after((dk, dv), mine_a, mine_b, *fold_k))
        mine_k = chunk_sums(meta, after([fold_k[0]] + hop_k, token_grads), seq)
        back_rows = gather_rows(after(back, *mine_k))
        sent = [shift_to(x, i) for i, x in enumerate(mine_k) if i]
        pieces = gather_rows(sum_of([mine_k[0]] + sent))
        lat_grad, qkv_grad, outw_grad, up_grad, down_grad, lines = finish_latent(
            meta, mine_a, other_a, mine_b, other_b, grad_one, back_rows
        )
        qkv_grad, gain_grad, shift_grad, bin_grad, bout_grad = finish_token(
            meta, pieces, qkv_weight[0, 1:3], norm_gain, norm_bias, lines, qkv_grad
        )
        return (
            out.reshape(shapes[0]),
            lat_grad.reshape(shapes[0]),
            token_grads.reshape(shapes[1]),
            qkv_grad,
            outw_grad,
            up_grad,
            down_grad,
            gain_grad,
            shift_grad,
            bin_grad,
            bout_grad,
        )

    dk, dv, dq = attend_back(cube(q), cube(du), cube(dl), mask, k, v)
    dq = dq.reshape(rows, D)
    keep_k, send_k, sums = keyval_grad(meta, xl, dk, dv)
    back, keep_k, send_k = query_grad(g1, meta, dq, scatter_rows(dq), lat, gb, sums, keep_k, send_k)
    token_grads = token_grad(g1, meta, tokens, gb, dk, dv)
    lat_grad = grad_one + place_rows(gather_rows(back), s, seq)
    mine_a, mine_b, mine_k = (
        sum_over_fsdp(*x) for x in ((keep_a, send_a), (keep_b, send_b), (keep_k, send_k))
    )

    def sides(mine):
        other = lax.ppermute(mine, "seq", pair)
        return jnp.where(s % 2 == 0, mine, other), jnp.where(s % 2 == 0, other, mine)

    whole_k = lax.psum(mine_k.astype(F32), "seq")
    shares = (*sides(mine_a), *sides(mine_b), whole_k)
    wide = jax.vmap(unpack)(*shares)
    grads = []
    for x, w, axis in zip(wide, weights, axes):
        x = jnp.moveaxis(x, 0, axis)
        x = x.reshape(*x.shape[:axis], -1, *x.shape[axis + 2 :])
        grads.append(lax.dynamic_slice_in_dim(x, fsdp * w.shape[axis], w.shape[axis], axis))
    last = shares[0][0, 2 * SPAN : ROWS_F].astype(F32).reshape(-1, D)
    middle = shares[0][0, -VEC_A:].astype(F32).reshape(-1, D)
    early = shares[2][0, -VEC_B:].astype(F32).reshape(-1, D)
    vec_k = whole_k[0][-VEC_K:]
    step = norm_gain.shape[1]
    k0, v0 = grads[0][0, 1], grads[0][0, 2]
    own_k, own_v = qkv_weight[0, 1].astype(F32), qkv_weight[0, 2].astype(F32)
    own_gain, own_shift = norm_gain[1].astype(F32), norm_bias[1].astype(F32)
    db1 = jnp.sum(own_k * vec_k[0] + own_v * vec_k[1], -1)
    dg1 = (jnp.sum(own_k * k0 + own_v * v0, -1) - own_shift * db1) / own_gain
    lines = [vec_k[2], early[0], middle[0], last[0], vec_k[3], early[1], middle[1], last[1], early[2], last[2]]
    lines = jnp.stack(lines)
    cut = lax.dynamic_slice_in_dim(lines, fsdp * step, step, 1)
    wide_bias = jnp.stack([early[3:7].reshape(FF), last[3:7].reshape(FF)])
    return (
        out.reshape(shapes[0]),
        lat_grad.reshape(shapes[0]),
        token_grads.reshape(shapes[1]),
        *grads,
        jnp.stack([cut[0], dg1, cut[1], cut[2], cut[3]]),
        jnp.stack([cut[4], db1, cut[5], cut[6], cut[7]]),
        lax.dynamic_slice_in_dim(wide_bias, fsdp * bias_in.shape[1], bias_in.shape[1], 1),
        cut[8:10],
    )


def place_rows(pieces, s, seq):
    step = pieces[0].shape[0]
    whole = jnp.zeros((seq * step, *pieces[0].shape[1:]), F32)
    for k, piece in enumerate(pieces):
        at = ((s - k) % seq) * step
        whole = lax.dynamic_update_slice_in_dim(whole, piece.astype(F32), at, 0)
    return whole


def solution(mesh):
    in_specs = (
        P(None, "fsdp", None, None),
        P(None, "fsdp", "seq", None),
        P(None, "fsdp"),
        P(None, "fsdp", None),
        P(None, None, "fsdp", None),
        P(None, "fsdp", None),
        P(None, "fsdp", None),
        P(None, "fsdp", None),
        P(None, "fsdp"),
        P(None, "fsdp"),
        P(None, "fsdp"),
        P(None, "fsdp"),
        P(None, "fsdp", None, None),
    )
    out_specs = (
        P(None, "fsdp", None, None),
        P(None, "fsdp", None, None),
        P(None, "fsdp", "seq", None),
        P(None, None, "fsdp", None),
        P(None, "fsdp", None),
        P(None, "fsdp", None),
        P(None, "fsdp", None),
        P(None, "fsdp"),
        P(None, "fsdp"),
        P(None, "fsdp"),
        P(None, "fsdp"),
    )
    step = functools.partial(per_device, mesh.shape["fsdp"], mesh.shape["seq"])
    return jax.shard_map(step, mesh=mesh, in_specs=in_specs, out_specs=out_specs, check_vma=False)
```

```python
import functools

import jax
import jax.numpy as jnp
from jax import lax
from jax.experimental import pallas as pl
from jax.experimental.layout import Layout, with_layout_constraint
from jax.experimental.pallas import tpu as pltpu
from jax.sharding import PartitionSpec as P

D = 768
HEADS = 12
HEAD = 64
PAIRS = HEADS // 2
FF = 3072
NLAT = 128
PATCHES = 392
FRAMES = 16
OWNERS = 8
SHARE = D // OWNERS
CHUNKS = FF // D
HALF = D // 2
PAY = D + 128
KEYVAL_ROWS = 208
FORWARD_PAIRS = 3
BACK_PAIRS = 2
TOKEN_TILES = 2
GRAD_TILES = 1
TOKEN_ROWS = 416
VEC = 16
VEC_A = 48
VEC_B = 32
STEPS = 2
VEC_K = 32
SPAN = CHUNKS * SHARE
ROWS_F = 2 * SPAN + VEC
ROWS_A = ROWS_F + 4 * SHARE + VEC_A
ROWS_B = 2 * SPAN + SHARE + VEC_B
ROWS_K = 3 * SHARE + VEC_K
EPS = 1e-06
F32 = jnp.float32
BF = jnp.bfloat16
GELU_C = 0.7978845608028654
GELU_A = 0.044715
VMEM_CAP = 60 * 1024 * 1024


def nn(a, b):
    return lax.dot_general(a, b, (((1,), (0,)), ((), ())), preferred_element_type=F32)


def nt(a, b):
    return lax.dot_general(a, b, (((1,), (1,)), ((), ())), preferred_element_type=F32)


def tn(a, b):
    return lax.dot_general(a, b, (((0,), (0,)), ((), ())), preferred_element_type=F32)


def ln_parts(x):
    center = x - jnp.mean(x, -1, keepdims=True)
    rstd = lax.rsqrt(jnp.mean(center * center, -1, keepdims=True) + EPS)
    return center, rstd


def ln(x, gain, bias):
    center, rstd = ln_parts(x)
    return center * rstd * gain + bias


def ln_back(x, gain, grad):
    center, rstd = ln_parts(x)
    xhat = center * rstd
    dx = grad * gain
    back = rstd * (dx - jnp.mean(dx, -1, keepdims=True) - xhat * jnp.mean(dx * xhat, -1, keepdims=True))
    return back, grad * xhat


def gelu(h):
    return h * (0.5 * (1.0 + jnp.tanh(GELU_C * (h + GELU_A * h * h * h))))


def gelu_both(h):
    square = h * h
    t = jnp.tanh(GELU_C * (h + GELU_A * h * square))
    cdf = 0.5 * (1.0 + t)
    slope = cdf + 0.5 * h * (1.0 - t * t) * (GELU_C * (1.0 + 3.0 * GELU_A * square))
    return h * cdf, slope


def low_lanes(rows):
    return lax.broadcasted_iota(jnp.int32, (rows, 128), 1) < HEAD


def block_diag(pair):
    wide = pair.astype(F32)
    low = low_lanes(pair.shape[0])
    return jnp.concatenate([jnp.where(low, wide, 0.0), jnp.where(low, 0.0, wide)], 0).astype(BF)


def diag_of(both):
    rows = both.shape[0] // 2
    return jnp.where(low_lanes(rows), both[:rows], both[rows:])


class Pack:
    def __init__(self, arrays, where):
        self.arrays, self.where = arrays, where

    def start(self, refs, row, rows, place, f, sem, shares=range(OWNERS)):
        for m in shares:
            index, lead, first = self.where(m, row)
            src = refs[index] if lead is None else refs[index].at[lead]
            pltpu.make_async_copy(src.at[pl.ds(first, rows)], place(f ^ m), sem).start()


def wait_for(ref, sem):
    pltpu.make_async_copy(ref, ref, sem).wait()


def share_rows(ref, g, first=0, span=SHARE, step=SHARE):
    return ref.at[pl.ds(pl.multiple_of(g * step + first, SHARE), span)]


def start_square(pack, refs, row, dst, f, sem):
    pack.start(refs, row, SHARE, lambda g: share_rows(dst, g), f, sem)


def start_up(pack, refs, row, dst, f, sems):
    for t in range(CHUNKS):
        lanes = pl.ds(t * D, D)
        pack.start(
            refs,
            row + t * SHARE,
            SHARE,
            lambda g, lanes=lanes: dst.at[pl.ds(pl.multiple_of(g * SHARE, SHARE), SHARE), lanes],
            f,
            sems.at[t],
        )


def start_down(pack, refs, row, dst, f, sems):
    for i in range(CHUNKS):
        for t in range(CHUNKS):
            pack.start(
                refs,
                row + t * SHARE,
                SHARE,
                lambda g, t=t: share_rows(dst, g, t * SHARE, SHARE, SPAN),
                f,
                sems.at[i],
                (2 * i, 2 * i + 1),
            )


def chunk_at(f, i):
    return pl.ds(pl.multiple_of(((f >> 1) ^ i) * D, D), D)


ANY = pl.BlockSpec(memory_space=pl.ANY)
WHOLE = pl.BlockSpec(memory_space=pltpu.VMEM)


def sds(shape, dtype):
    return jax.ShapeDtypeStruct(shape, dtype)


def cost(flops, size, exps=0):
    return pl.CostEstimate(flops=1, bytes_accessed=1, transcendentals=0)


PARAMS = pltpu.CompilerParams(vmem_limit_bytes=VMEM_CAP)


def keyval_kernel(pack, local, tile, meta, x_ref, *refs):
    count = len(pack.arrays)
    wrefs, (xl_ref, k_ref, v_ref, gb_ref, bin_ref, wkv, small, sems) = refs[:count], refs[count:]
    f = meta[0]

    @pl.when((pl.program_id(0) == 0) & (pl.program_id(1) == 0))
    def _():
        for m in range(OWNERS):
            index, lead, first = pack.where(m, 3 * SHARE)
            src = wrefs[index] if lead is None else wrefs[index].at[lead]
            pltpu.make_async_copy(
                src.at[pl.ds(first, 16), pl.ds(0, 256)], small.at[m], sems.at[2]
            ).start()
        start_square(pack, wrefs, SHARE, wkv.at[0], f, sems.at[0])
        start_square(pack, wrefs, 2 * SHARE, wkv.at[1], f, sems.at[1])
        wait_for(small, sems.at[2])
        lane = lax.broadcasted_iota(jnp.int32, (128, D), 1)
        row = lax.broadcasted_iota(jnp.int32, (128, D), 0)
        total = jnp.zeros((16, D), F32)
        for m in range(OWNERS):
            g = f ^ m
            place = jnp.where((lane - g * SHARE == row) & (row < SHARE), 1.0, 0.0).astype(BF)
            total = total + nn(small[m, :, 0:128], place)
            wide = small[m].astype(F32)
            for u in range(6):
                i, part = u // 3, u % 3
                line = wide[12 + u : 13 + u, 0:128] if u < 4 else wide[u - 4 : u - 3, 128:256]
                at = pl.ds(pl.multiple_of((3 * g + part) * 128, 128), 128)
                bin_ref[i : i + 1, at] = line
        gb_ref[...] = total
        wait_for(wkv.at[0], sems.at[0])
        wait_for(wkv.at[1], sems.at[1])

    for first in range(0, tile, KEYVAL_ROWS):
        part = slice(first, first + KEYVAL_ROWS)
        normed = ln(x_ref[0, part, :].astype(F32), gb_ref[1:2], gb_ref[6:7])
        row = lax.broadcasted_iota(jnp.int32, (KEYVAL_ROWS, D), 0)
        row = row + (pl.program_id(1) * tile + first)
        xl = jnp.where(row < local, normed, 0.0).astype(BF)
        xl_ref[0, part, :] = xl
        k_ref[0, part, :] = nn(xl, wkv[0]).astype(BF)
        v_ref[0, part, :] = nn(xl, wkv[1]).astype(BF)


def keyval(pack, meta, tokens, local, padded):
    clips = tokens.shape[0]
    tile = padded // 2
    block = pl.BlockSpec((1, tile, D), lambda i, j, m: (i, j, 0))
    fixed = lambda shape: pl.BlockSpec(shape, lambda i, j, m: (0,) * len(shape))
    return pl.pallas_call(
        functools.partial(keyval_kernel, pack, local, tile),
        grid_spec=pltpu.PrefetchScalarGridSpec(
            num_scalar_prefetch=1,
            grid=(clips, padded // tile),
            in_specs=[block] + [ANY] * len(pack.arrays),
            out_specs=[block, block, block, fixed((16, D)), fixed((2, FF))],
            scratch_shapes=[
                pltpu.VMEM((2, D, D), BF),
                pltpu.VMEM((OWNERS, 16, 256), BF),
                pltpu.SemaphoreType.DMA((3,)),
            ],
        ),
        out_shape=[sds((clips, padded, D), BF)] * 3 + [sds((16, D), F32), sds((2, FF), F32)],
        compiler_params=PARAMS,
        cost_estimate=cost(4 * clips * padded * D * D, clips * padded * D * 8),
        name="keyval",
    )(meta, tokens, *pack.arrays)


def attend_kernel(pack, padded, meta, lat_ref, gb_ref, bias_ref, k_ref, v_ref, *refs):
    count = len(pack.arrays)
    wrefs, (pay_ref, q_ref, wq, qs, lv, sem) = refs[:count], refs[count:]
    f = meta[0]
    clip, group = pl.program_id(0), pl.program_id(1)

    @pl.when((clip == 0) & (group == 0))
    def _():
        start_square(pack, wrefs, 0, wq, f, sem.at[0])
        zl = ln(lat_ref[...].astype(F32), gb_ref[0:1], gb_ref[5:6]).astype(BF)
        wait_for(wq, sem.at[0])
        q = nn(zl, wq[...]).astype(BF).astype(F32) * 0.125
        qs[...] = q.astype(BF)
        q_ref[...] = qs[...]

    rows = pl.ds(pl.multiple_of(clip * NLAT, NLAT), NLAT)
    lane = lax.broadcasted_iota(jnp.int32, (NLAT, 128), 1)
    new = jnp.where(group == 0, 0.0, lv[...])
    for p in range(FORWARD_PAIRS):
        pair = group * FORWARD_PAIRS + p
        at = pl.ds(pl.multiple_of(pair * 128, 128), 128)
        mine = slice(p * 128, p * 128 + 128)
        e = jnp.exp(nt(block_diag(qs[rows, at]), k_ref[0, :, mine]) + bias_ref[0])
        pay_ref[0, :, at] = diag_of(nn(e.astype(BF), v_ref[0, :, mine])).astype(BF)
        l = jnp.sum(e, -1, keepdims=True)
        new = jnp.where(lane == 2 * pair, l[:NLAT], jnp.where(lane == 2 * pair + 1, l[NLAT:], new))
    lv[...] = new

    @pl.when(group == PAIRS // FORWARD_PAIRS - 1)
    def _():
        pay_ref[0, :, D:PAY] = split_pair(lv[...])


def split_pair(values):
    high = values.astype(BF).astype(F32)
    rest = values - high
    return jnp.where(low_lanes(values.shape[0]), high, pltpu.roll(rest, HEAD, 1)).astype(BF)


def join_pair(pay):
    wide = pay.astype(F32)
    return wide + pltpu.roll(wide, HEAD, 1)


def attend(pack, meta, lat, gb, bias, k, v):
    clips, padded = k.shape[0], k.shape[1]
    rows = lat.shape[0]
    fixed = lambda shape: pl.BlockSpec(shape, lambda i, j, m: (0,) * len(shape))
    lanes = pl.BlockSpec((1, padded, 128 * FORWARD_PAIRS), lambda i, j, m: (i, 0, j))
    return pl.pallas_call(
        functools.partial(attend_kernel, pack, padded),
        grid_spec=pltpu.PrefetchScalarGridSpec(
            num_scalar_prefetch=1,
            grid=(clips, PAIRS // FORWARD_PAIRS),
            in_specs=[
                fixed((rows, D)),
                fixed((16, D)),
                pl.BlockSpec((1, 1, padded), lambda i, j, m: (i, 0, 0)),
                lanes,
                lanes,
            ]
            + [ANY] * len(pack.arrays),
            out_specs=[
                pl.BlockSpec((1, NLAT, PAY), lambda i, j, m: (i, 0, 0)),
                fixed((rows, D)),
            ],
            scratch_shapes=[
                pltpu.VMEM((D, D), BF),
                pltpu.VMEM((rows, D), BF),
                pltpu.VMEM((NLAT, 128), F32),
                pltpu.SemaphoreType.DMA((1,)),
            ],
        ),
        out_shape=[sds((clips, NLAT, PAY), BF), sds((rows, D), BF)],
        compiler_params=PARAMS,
        cost_estimate=cost(
            8 * clips * padded * NLAT * D, clips * padded * D * 4, clips * padded * NLAT * HEADS
        ),
        name="attend",
    )(meta, lat, gb, bias, k, v, *pack.arrays)


def combine_kernel(*refs):
    parts, out_ref = refs[1:-1], refs[-1]
    total = parts[0][...].astype(F32)
    for part in parts[1:]:
        total = total + part[...].astype(F32)
    l = total[:, D:PAY]
    l = l + pltpu.roll(l, HEAD, 1)
    low = low_lanes(total.shape[0])
    for j in range(PAIRS):
        den = jnp.where(low, l[:, 2 * j : 2 * j + 1], l[:, 2 * j + 1 : 2 * j + 2])
        out_ref[:, 128 * j : 128 * j + 128] = (total[:, 128 * j : 128 * j + 128] / den).astype(BF)
    out_ref[:, D:PAY] = split_pair(l)


def combine(meta, pay, received):
    rows = received[0].shape[0] if received else pay.shape[0]
    fixed = pl.BlockSpec((rows, PAY), lambda i, m: (0, 0))
    return pl.pallas_call(
        combine_kernel,
        grid_spec=pltpu.PrefetchScalarGridSpec(
            num_scalar_prefetch=1,
            grid=(1,),
            in_specs=[pl.BlockSpec((rows, PAY), lambda i, m: (m[1], 0))] + [fixed] * len(received),
            out_specs=fixed,
        ),
        out_shape=sds((rows, PAY), BF),
        name="combine",
    )(meta, pay, *received)


def first_kernel(pack, count, meta, *refs):
    parts = refs[:count]
    lat_ref, gb_ref, bin_ref = refs[count : count + 3]
    refs = refs[count + 3 :]
    wrefs, refs = refs[: len(pack.arrays)], refs[len(pack.arrays) :]
    o_ref, l_ref, z1_ref, z2_ref, h_ref, wo, win, wout, hs, sems, hsems = refs
    f, s = meta[0], meta[1]
    start_square(pack, wrefs, 0, wo, f, sems.at[0])
    start_up(pack, wrefs, SHARE, win, f, sems.at[pl.ds(1, CHUNKS)])
    start_down(pack, wrefs, SHARE + SPAN, wout, f, sems.at[pl.ds(1 + CHUNKS, CHUNKS)])
    step = parts[0].shape[0]
    for k, part in enumerate(parts):
        rows = pl.ds(pl.multiple_of(lax.rem(s - k + count, count) * step, step), step)
        o_ref[rows, :] = part[:, :D]
        l_ref[rows, :] = join_pair(part[:, D:PAY])
    wait_for(wo, sems.at[0])
    z1 = lat_ref[...].astype(F32) + nn(o_ref[...], wo[...])
    z1_ref[...] = z1
    n = ln(z1, gb_ref[2:3], gb_ref[7:8]).astype(BF)
    y = jnp.zeros_like(z1)
    copies = []
    for i in range(CHUNKS):
        at = chunk_at(f, i)
        wait_for(win.at[:, at], sems.at[1 + ((f >> 1) ^ i)])
        h = nn(n, win[:, at]) + bin_ref[0:1, at]
        hs[:, at] = h
        copies.append(pltpu.make_async_copy(hs.at[:, at], h_ref.at[:, at], hsems.at[i]))
        copies[-1].start()
        a = gelu(h).astype(BF)
        wait_for(wout.at[at], sems.at[1 + CHUNKS + i])
        y = y + nn(a, wout[at, :])
    z2_ref[...] = z1 + (y + gb_ref[10:11])
    for copy in copies:
        copy.wait()


def first_block(pack, meta, parts, lat, gb, bins):
    rows = lat.shape[0]
    n_w = len(pack.arrays)
    return pl.pallas_call(
        functools.partial(first_kernel, pack, len(parts)),
        in_specs=[pl.BlockSpec(memory_space=pltpu.SMEM)] + [WHOLE] * (len(parts) + 3) + [ANY] * n_w,
        out_specs=[WHOLE] * 4 + [ANY],
        scratch_shapes=[
            pltpu.VMEM((D, D), BF),
            pltpu.VMEM((D, FF), BF),
            pltpu.VMEM((FF, D), BF),
            pltpu.VMEM((rows, FF), F32),
            pltpu.SemaphoreType.DMA((1 + 2 * CHUNKS,)),
            pltpu.SemaphoreType.DMA((CHUNKS,)),
        ],
        out_shape=[
            sds((rows, D), BF),
            sds((rows, 128), F32),
            sds((rows, D), F32),
            sds((rows, D), F32),
            sds((rows, FF), F32),
        ],
        compiler_params=PARAMS,
        cost_estimate=cost(18 * rows * D * D, 16 * D * D * 2),
        name="first_block",
    )(meta, *parts, lat, gb, bins, *pack.arrays)


def softmax_rows(scores):
    e = jnp.exp(scores - jnp.max(scores, -1, keepdims=True))
    return e / jnp.sum(e, -1, keepdims=True)


def put_vec(shares, rows, row, width):
    vec = jnp.concatenate(rows + [jnp.zeros((width - len(rows), HALF), F32)], 0).astype(BF)
    for which in range(2):
        for k in range(4):
            shares[which, k, row : row + width, :] = vec


def halves(line):
    return [line[:, i : i + HALF] for i in range(0, line.shape[1], HALF)]


def column_sum(values):
    return jnp.sum(values, 0, keepdims=True)


def put_rows(shares, f, row, grad, first=0):
    grad = grad.astype(BF)
    for g in range(OWNERS):
        rel = f ^ g
        shares[rel & 1, rel >> 1, row : row + SHARE, :] = grad[g * SHARE : g * SHARE + SHARE]


def put_down(shares, f, row, grad, u):
    grad = grad.astype(BF)
    span = CHUNKS * SHARE
    for i in range(D // span):
        rel = f ^ (u * (D // span) + i)
        shares[rel & 1, rel >> 1, row : row + span, :] = grad[i * span : i * span + span]


def ff_grads(shares, f, h, row, n, dh_ref, a_ref, dy_ref):
    for c in range(CHUNKS):
        at = pl.ds(pl.multiple_of(h * (FF // 2) + c * HALF, 128), HALF)
        put_rows(shares, f, row + c * SHARE, tn(n, dh_ref[:, at]))
    dyh = dy_ref[:, pl.ds(pl.multiple_of(h * HALF, 128), HALF)]
    for u in range(CHUNKS):
        put_down(shares, f, row + CHUNKS * SHARE, tn(a_ref[:, u * D : u * D + D], dyh), u)


def share_copies(shares, keep_ref, send_ref, first, rows, sems):
    at = pl.ds(first, rows)
    return [
        pltpu.make_async_copy(shares.at[which, k, at], ref.at[k, at], sems.at[which, k])
        for which, ref in ((0, keep_ref), (1, send_ref))
        for k in range(4)
    ]


def start_all(copies):
    for copy in copies:
        copy.start()


def wait_all(copies):
    for copy in copies:
        copy.wait()


def second_kernel(pack, meta, z2_ref, g4_ref, gb_ref, bin_ref, *refs):
    count = len(pack.arrays)
    wrefs, (out_ref, g2_ref, keep_ref, send_ref) = refs[:count], refs[count : count + 4]
    wqkv, wo, win, wout, qkv, o2, probs, hs, ac, dhs, dqkv, dab, dob, shares, sems, osems = refs[count + 4 :]
    f, h = meta[0], meta[2]
    for j in range(3):
        start_square(pack, wrefs, j * SHARE, wqkv.at[j], f, sems.at[j])
    start_square(pack, wrefs, 3 * SHARE, wo, f, sems.at[3])
    start_up(pack, wrefs, 4 * SHARE, win, f, sems.at[pl.ds(4, CHUNKS)])
    start_down(pack, wrefs, 4 * SHARE + SPAN, wout, f, sems.at[pl.ds(4 + CHUNKS, CHUNKS)])
    z2 = z2_ref[...]
    m = ln(z2, gb_ref[3:4], gb_ref[8:9]).astype(BF)
    for j in range(3):
        wait_for(wqkv.at[j], sems.at[j])
        qkv[j] = nn(m, wqkv[j]).astype(BF)
    tiles = []
    for clip in range(z2.shape[0] // NLAT):
        for pair in range(PAIRS):
            tiles.append((slice(clip * NLAT, clip * NLAT + NLAT), slice(pair * 128, pair * 128 + 128)))
    for i, (rows, at) in enumerate(tiles):
        p = softmax_rows(nt(block_diag(qkv[0, rows, at]), qkv[1, rows, at]) * 0.125)
        probs[i] = p
        o2[rows, at] = diag_of(nn(p.astype(BF), qkv[2, rows, at])).astype(BF)
    wait_for(wo, sems.at[3])
    z3 = z2 + nn(o2[...], wo[...])
    n = ln(z3, gb_ref[4:5], gb_ref[9:10]).astype(BF)
    y = jnp.zeros_like(z3)
    for c in range(CHUNKS):
        wait_for(win.at[:, c * D : c * D + D], sems.at[4 + c])
    for i in range(CHUNKS):
        wait_for(wout.at[chunk_at(f, i)], sems.at[4 + CHUNKS + i])
    for i in range(CHUNKS):
        at = slice(i * D, i * D + D)
        act, slope = gelu_both(nn(n, win[:, at]) + bin_ref[1:2, at])
        hs[:, at] = slope
        a = act.astype(BF)
        ac[:, at] = a
        y = y + nn(a, wout[at, :])
    out_ref[...] = z3 + (y + gb_ref[11:12])
    dy = g4_ref[...]
    dn = jnp.zeros_like(z3)
    dbin = []
    for c in range(CHUNKS):
        at = slice(c * D, c * D + D)
        dh = (nt(dy, wout[at, :]) * hs[:, at]).astype(BF)
        dhs[:, at] = dh
        dbin += halves(column_sum(dh.astype(F32)))
        dn = dn + nt(dh, win[:, at])
    back, dgain = ln_back(z3, gb_ref[4:5], dn)
    g4 = dy.astype(F32)
    g3 = g4 + back
    ff_grads(shares, f, h, 0, n, dhs, ac, g4_ref)
    vec = halves(column_sum(dgain)) + halves(column_sum(dn)) + halves(column_sum(g4)) + dbin
    put_vec(shares, vec, 2 * SPAN, VEC)
    early = share_copies(shares, keep_ref, send_ref, 0, ROWS_F, osems.at[0])
    start_all(early)

    half = pl.ds(pl.multiple_of(h * HALF, 128), HALF)
    dab[...] = g3.astype(BF)
    dob[...] = nt(dab[...], wo[...]).astype(BF)
    put_rows(shares, f, ROWS_F + 3 * SHARE, tn(o2[...], dab[:, half]))
    for i, (rows, at) in enumerate(tiles):
        q, k, v = qkv[0, rows, at], qkv[1, rows, at], qkv[2, rows, at]
        p = probs[i]
        dobd = block_diag(dob[rows, at])
        dp = nt(dobd, v)
        ds = (p * (dp - jnp.sum(p * dp, -1, keepdims=True))).astype(BF)
        dqkv[0, rows, at] = (diag_of(nn(ds, k)) * 0.125).astype(BF)
        dqkv[1, rows, at] = (tn(ds, block_diag(q)) * 0.125).astype(BF)
        dqkv[2, rows, at] = tn(p.astype(BF), dobd).astype(BF)
    dm = jnp.zeros_like(g3)
    for j in range(3):
        dm = dm + nt(dqkv[j], wqkv[j])
        put_rows(shares, f, ROWS_F + j * SHARE, tn(m, dqkv[j, :, half]))
    back, dgain = ln_back(z2, gb_ref[3:4], dm)
    g2_ref[...] = g3 + back
    put_vec(shares, halves(column_sum(dgain)) + halves(column_sum(dm)), ROWS_F + 4 * SHARE, VEC_A)
    late = share_copies(shares, keep_ref, send_ref, ROWS_F, ROWS_A - ROWS_F, osems.at[1])
    start_all(late)
    wait_all(early + late)


def second_block(pack, meta, z2, g4, gb, bins):
    rows = z2.shape[0]
    square = pltpu.VMEM((rows, D), BF)
    return pl.pallas_call(
        functools.partial(second_kernel, pack),
        in_specs=[pl.BlockSpec(memory_space=pltpu.SMEM)] + [WHOLE] * 4 + [ANY] * len(pack.arrays),
        out_specs=[WHOLE] * 2 + [ANY] * 2,
        scratch_shapes=[
            pltpu.VMEM((3, D, D), BF),
            pltpu.VMEM((D, D), BF),
            pltpu.VMEM((D, FF), BF),
            pltpu.VMEM((FF, D), BF),
            pltpu.VMEM((3, rows, D), BF),
            square,
            pltpu.VMEM((rows // NLAT * PAIRS, 2 * NLAT, NLAT), F32),
            pltpu.VMEM((rows, FF), F32),
            pltpu.VMEM((rows, FF), BF),
            pltpu.VMEM((rows, FF), BF),
            pltpu.VMEM((3, rows, D), BF),
            square,
            square,
            pltpu.VMEM((2, 4, ROWS_A, HALF), BF),
            pltpu.SemaphoreType.DMA((4 + 2 * CHUNKS,)),
            pltpu.SemaphoreType.DMA((2, 2, 4)),
        ],
        out_shape=[
            sds((rows, D), F32),
            sds((rows, D), F32),
            sds((4, ROWS_A, HALF), BF),
            sds((4, ROWS_A, HALF), BF),
        ],
        compiler_params=PARAMS,
        cost_estimate=cost(0, 0),
        name="second_block",
    )(meta, z2, g4, gb, bins, *pack.arrays)


def fourth_kernel(pack, meta, g2_ref, z1_ref, o_ref, l_ref, gb_ref, h_ref, *refs):
    wrefs, refs = refs[: len(pack.arrays)], refs[len(pack.arrays) :]
    g1_ref, du_ref, dl_ref, keep_ref, send_ref = refs[:5]
    wo, win, wout, hs, ac, dhs, dab, dyb, shares, sems, osems = refs[5:]
    f, h = meta[0], meta[2]
    hcopy = pltpu.make_async_copy(h_ref, hs, sems.at[1])
    hcopy.start()
    start_down(pack, wrefs, SHARE + SPAN, wout, f, sems.at[pl.ds(2, CHUNKS)])
    start_up(pack, wrefs, SHARE, win, f, sems.at[pl.ds(2 + CHUNKS, CHUNKS)])
    start_square(pack, wrefs, 0, wo, f, sems.at[0])
    half = pl.ds(pl.multiple_of(h * HALF, 128), HALF)
    z1 = z1_ref[...]
    n = ln(z1, gb_ref[2:3], gb_ref[7:8]).astype(BF)
    g2 = g2_ref[...]
    dyb[...] = g2.astype(BF)
    hcopy.wait()
    for c in range(CHUNKS):
        at = slice(c * D, c * D + D)
        act, slope = gelu_both(hs[:, at])
        ac[:, at] = act.astype(BF)
        hs[:, at] = slope
    for i in range(CHUNKS):
        wait_for(wout.at[chunk_at(f, i)], sems.at[2 + i])
    for c in range(CHUNKS):
        wait_for(win.at[:, c * D : c * D + D], sems.at[2 + CHUNKS + c])
    dn = jnp.zeros_like(g2)
    dbin = []
    for c in range(CHUNKS):
        at = slice(c * D, c * D + D)
        dh = (nt(dyb[...], wout[at, :]) * hs[:, at]).astype(BF)
        dhs[:, at] = dh
        dbin += halves(column_sum(dh.astype(F32)))
        dn = dn + nt(dh, win[:, at])
    back, dgain = ln_back(z1, gb_ref[2:3], dn)
    g1 = g2 + back
    g1_ref[...] = g1
    ff_grads(shares, f, h, 0, n, dhs, ac, dyb)
    vec = halves(column_sum(dgain)) + halves(column_sum(dn))
    vec += halves(column_sum(dyb[...].astype(F32))) + dbin
    put_vec(shares, vec, 2 * SPAN + SHARE, VEC_B)

    dab[...] = g1.astype(BF)
    wait_for(wo, sems.at[0])
    do = nt(dab[...], wo[...]).astype(BF).astype(F32)
    put_rows(shares, f, 2 * SPAN, tn(o_ref[...], dab[:, half]))
    low = low_lanes(g2.shape[0])
    lane = lax.broadcasted_iota(jnp.int32, low.shape, 1)
    l = l_ref[...]
    dl = jnp.zeros(low.shape, F32)
    for j in range(PAIRS):
        at = slice(128 * j, 128 * j + 128)
        first, later = l[:, 2 * j : 2 * j + 1], l[:, 2 * j + 1 : 2 * j + 2]
        du_ref[:, at] = (do[:, at] / jnp.where(low, first, later)).astype(BF)
        t = do[:, at] * o_ref[:, at].astype(F32)
        t_first = -jnp.sum(jnp.where(low, t, 0.0), -1, keepdims=True) / first
        t_later = -jnp.sum(jnp.where(low, 0.0, t), -1, keepdims=True) / later
        dl = jnp.where(lane == 2 * j, t_first, jnp.where(lane == 2 * j + 1, t_later, dl))
    dl_ref[...] = dl
    late = share_copies(shares, keep_ref, send_ref, 0, ROWS_B, osems)
    start_all(late)
    wait_all(late)


def fourth_block(pack, meta, g2, z1, o, l, gb, hidden):
    rows = z1.shape[0]
    arrays = pack.arrays
    return pl.pallas_call(
        functools.partial(fourth_kernel, pack),
        in_specs=[pl.BlockSpec(memory_space=pltpu.SMEM)] + [WHOLE] * 5 + [ANY] * (1 + len(arrays)),
        out_specs=[WHOLE] * 3 + [ANY] * 2,
        scratch_shapes=[
            pltpu.VMEM((D, D), BF),
            pltpu.VMEM((D, FF), BF),
            pltpu.VMEM((FF, D), BF),
            pltpu.VMEM((rows, FF), F32),
            pltpu.VMEM((rows, FF), BF),
            pltpu.VMEM((rows, FF), BF),
            pltpu.VMEM((rows, D), BF),
            pltpu.VMEM((rows, D), BF),
            pltpu.VMEM((2, 4, ROWS_B, HALF), BF),
            pltpu.SemaphoreType.DMA((2 + 2 * CHUNKS,)),
            pltpu.SemaphoreType.DMA((2, 4)),
        ],
        out_shape=[
            sds((rows, D), F32),
            sds((rows, D), BF),
            sds((rows, 128), F32),
            sds((4, ROWS_B, HALF), BF),
            sds((4, ROWS_B, HALF), BF),
        ],
        compiler_params=PARAMS,
        cost_estimate=cost(30 * rows * D * D, 12 * D * D * 4),
        name="fourth_block",
    )(meta, g2, z1, o, l, gb, hidden, *arrays)


def attend_back_kernel(q_ref, du_ref, dl_ref, mask_ref, k_ref, v_ref, dk_ref, dv_ref, dq_ref, dlt):
    group = pl.program_id(1)

    @pl.when(group == 0)
    def _():
        dlt[...] = dl_ref[0].T

    mask = mask_ref[0]
    mask = jnp.concatenate([mask, mask], 1)
    upper = lax.broadcasted_iota(jnp.int32, (128, NLAT), 0) < HEAD
    for p in range(BACK_PAIRS):
        pair = group * BACK_PAIRS + p
        mine = slice(p * 128, p * 128 + 128)
        qbd, dubd = block_diag(q_ref[0, :, mine]), block_diag(du_ref[0, :, mine])
        line = [dlt[pl.ds(2 * pair + i, 1), :] for i in range(2)]
        k, v = k_ref[0, :, mine], v_ref[0, :, mine]
        e = jnp.exp(nt(k, qbd) + mask)
        ds = (e * (nt(v, dubd) + jnp.concatenate(line, 1))).astype(BF)
        dv_ref[0, :, mine] = nn(e.astype(BF), dubd).astype(BF)
        dk_ref[0, :, mine] = nn(ds, qbd).astype(BF)
        dqt = tn(k, ds)
        dqt = jnp.where(upper, dqt[:, :NLAT], dqt[:, NLAT:])
        dq_ref[0, :, mine] = (dqt.T * 0.125).astype(BF)


def attend_back(q, du, dl, mask, k, v):
    clips, padded = k.shape[0], k.shape[1]
    wide = 128 * BACK_PAIRS
    small = pl.BlockSpec((1, NLAT, wide), lambda i, j: (i, 0, j))
    whole = pl.BlockSpec((1, NLAT, 128), lambda i, j: (i, 0, 0))
    column = pl.BlockSpec((1, padded, 128), lambda i, j: (i, 0, 0))
    lanes = pl.BlockSpec((1, padded, wide), lambda i, j: (i, 0, j))
    return pl.pallas_call(
        attend_back_kernel,
        grid=(clips, PAIRS // BACK_PAIRS),
        in_specs=[small, small, whole, column, lanes, lanes],
        out_specs=[lanes, lanes, small],
        scratch_shapes=[pltpu.VMEM((128, NLAT), F32)],
        out_shape=[sds((clips, padded, D), BF)] * 2 + [sds((clips, NLAT, D), BF)],
        compiler_params=PARAMS,
        cost_estimate=cost(0, 0),
        name="attend_back",
    )(q, du, dl, mask, k, v)


def keyval_grad_kernel(meta, xl_ref, dk_ref, dv_ref, keep_ref, send_ref, sum_ref, acc, shares, sems):
    f = meta[0]
    step = pl.program_id(0)
    first = step == 0
    xt = xl_ref[0].T
    for j, ref in enumerate((dk_ref, dv_ref)):
        grad = nn(xt, ref[0])
        acc[j] = grad + jnp.where(first, 0.0, acc[j])
        line = column_sum(ref[0].astype(F32))
        sum_ref[j : j + 1, :] = line + jnp.where(first, 0.0, sum_ref[j : j + 1, :])

    @pl.when(step == pl.num_programs(0) - 1)
    def _():
        for j in range(2):
            for g in range(OWNERS):
                rel = f ^ g
                grad = acc[j, g * SHARE : g * SHARE + SHARE, :].astype(BF)
                shares[rel & 1, rel >> 1, j * SHARE : j * SHARE + SHARE, :] = grad
        copies = share_copies(shares, keep_ref, send_ref, 0, 2 * SHARE, sems)
        start_all(copies)
        wait_all(copies)


def keyval_grad(meta, xl, dk, dv):
    clips, padded = xl.shape[0], xl.shape[1]
    tile = padded // GRAD_TILES
    at = lambda i, m: (i // GRAD_TILES, lax.rem(i, GRAD_TILES), 0)
    block = pl.BlockSpec((1, tile, D), at)
    return pl.pallas_call(
        keyval_grad_kernel,
        grid_spec=pltpu.PrefetchScalarGridSpec(
            num_scalar_prefetch=1,
            grid=(clips * GRAD_TILES,),
            in_specs=[block] * 3,
            out_specs=[ANY, ANY, pl.BlockSpec((8, D), lambda i, m: (0, 0))],
            scratch_shapes=[
                pltpu.VMEM((2, D, D), F32),
                pltpu.VMEM((2, 4, 2 * SHARE, D), BF),
                pltpu.SemaphoreType.DMA((2, 4)),
            ],
        ),
        out_shape=[sds((4, ROWS_K, D), BF), sds((4, ROWS_K, D), BF), sds((8, D), F32)],
        compiler_params=PARAMS,
        cost_estimate=cost(4 * clips * padded * D * D, clips * padded * D * 6),
        name="keyval_grad",
    )(meta, xl, dk, dv)


def query_grad_kernel(pack, count, meta, *refs):
    own_ref, parts, refs = refs[0], refs[1:count], refs[count:]
    lat_ref, gb_ref, sum_ref, keep_in, send_in = refs[:5]
    refs = refs[5:]
    n_w = len(pack.arrays)
    wrefs, (back_ref, keep_ref, send_ref, wq, shares, sem, osems) = refs[:n_w], refs[n_w:]
    f = meta[0]
    start_square(pack, wrefs, 0, wq, f, sem.at[0])
    total = own_ref[...].astype(F32)
    for part in parts:
        total = total + part[...].astype(F32)
    dq = total.astype(BF)
    lat = lat_ref[...].astype(F32)
    zl = ln(lat, gb_ref[0:1], gb_ref[5:6]).astype(BF)
    grad = tn(zl, dq).astype(BF)
    for g in range(OWNERS):
        rel = f ^ g
        shares[rel & 1, rel >> 1, 0:SHARE, :] = grad[g * SHARE : g * SHARE + SHARE]

    def leave(first, rows, sems):
        return [
            pltpu.make_async_copy(
                shares.at[which, k, pl.ds(first, rows)],
                ref.at[k, pl.ds(2 * SHARE + first, rows)],
                sems.at[which, k],
            )
            for which, ref in ((0, keep_ref), (1, send_ref))
            for k in range(4)
        ]

    early = leave(0, SHARE, osems.at[0])
    start_all(early)
    wait_for(wq, sem.at[0])
    dzl = nt(dq, wq[...])
    back, dgain = ln_back(lat, gb_ref[0:1], dzl)
    back_ref[...] = back.astype(BF)
    lines = [sum_ref[0:1], sum_ref[1:2], column_sum(dgain), column_sum(dzl)]
    vec = jnp.concatenate(lines + [jnp.zeros((VEC_K - 4, D), F32)], 0).astype(BF)
    for which in range(2):
        for k in range(4):
            shares[which, k, SHARE : SHARE + VEC_K, :] = vec
    late = leave(SHARE, VEC_K, osems.at[1])
    start_all(late)
    wait_all(early + late)


def query_grad(pack, meta, dq, parts, lat, gb, sums, keep, send):
    rows = parts[0].shape[0] if parts else dq.shape[0]
    count = 1 + len(parts)
    mine = pl.BlockSpec((rows, D), lambda i, m: (m[1], 0))
    fixed = lambda shape: pl.BlockSpec(shape, lambda i, m: (0,) * len(shape))
    return pl.pallas_call(
        functools.partial(query_grad_kernel, pack, count),
        grid_spec=pltpu.PrefetchScalarGridSpec(
            num_scalar_prefetch=1,
            grid=(1,),
            in_specs=[mine]
            + [fixed((rows, D))] * len(parts)
            + [mine, fixed((16, D)), fixed((8, D)), ANY, ANY]
            + [ANY] * len(pack.arrays),
            out_specs=[fixed((rows, D)), ANY, ANY],
            scratch_shapes=[
                pltpu.VMEM((D, D), BF),
                pltpu.VMEM((2, 4, SHARE + VEC_K, D), BF),
                pltpu.SemaphoreType.DMA((1,)),
                pltpu.SemaphoreType.DMA((2, 2, 4)),
            ],
        ),
        out_shape=[sds((rows, D), BF), sds(keep.shape, BF), sds(send.shape, BF)],
        input_output_aliases={count + 4: 1, count + 5: 2},
        compiler_params=PARAMS,
        name="query_grad",
    )(meta, dq, *parts, lat, gb, sums, keep, send, *pack.arrays)


def token_grad_kernel(pack, local, meta, x_ref, gb_ref, dk_ref, dv_ref, *refs):
    count = len(pack.arrays)
    wrefs, (out_ref, wkv, lines, sems, osems) = refs[:count], refs[count:]
    clip, at = pl.program_id(0), pl.program_id(1)
    clips, tiles = pl.num_programs(0), pl.num_programs(1)
    tile = x_ref.shape[1]
    n_clips, n_tiles = out_ref.shape[0] // (local * PAIRS), -(-local // tile)

    @pl.when((clip == 0) & (at == 0))
    def _():
        f = meta[0]
        start_square(pack, wrefs, SHARE, wkv.at[0], f, sems.at[0])
        start_square(pack, wrefs, 2 * SHARE, wkv.at[1], f, sems.at[1])
        wait_for(wkv.at[0], sems.at[0])
        wait_for(wkv.at[1], sems.at[1])

    for first in range(0, tile, TOKEN_ROWS):
        rows = slice(first, first + TOKEN_ROWS)
        grad = nt(dk_ref[0, rows, :], wkv[0]) + nt(dv_ref[0, rows, :], wkv[1])
        back, unused = ln_back(x_ref[0, rows, :].astype(F32), gb_ref[1:2], grad)
        base = (clip * local + at * tile + first) * PAIRS
        for t in range(PAIRS):
            lines[pl.ds(base + t, TOKEN_ROWS, stride=PAIRS), :] = back[:, 128 * t : 128 * t + 128]

    def piece(c, i):
        first = (c * local + i * tile) * PAIRS // 8 * 8
        last = (c * local + min((i + 1) * tile, local)) * PAIRS
        last = last if c == n_clips - 1 and i == n_tiles - 1 else last // 8 * 8
        where = pl.ds(first, last - first)
        slot = c * n_tiles + i
        return pltpu.make_async_copy(lines.at[where], out_ref.at[where], osems.at[slot])

    for c in range(n_clips):
        for i in range(n_tiles):

            @pl.when((clip == c) & (at == i))
            def _(c=c, i=i):
                piece(c, i).start()

    @pl.when((clip == n_clips - 1) & (at == n_tiles - 1))
    def _():
        for c in range(n_clips):
            for i in range(n_tiles):
                piece(c, i).wait()


def token_grad(pack, meta, tokens, gb, dk, dv):
    clips, local = tokens.shape[0], tokens.shape[1]
    padded = dk.shape[1]
    tile = padded // TOKEN_TILES
    block = pl.BlockSpec((1, tile, D), lambda i, j, m: (i, j, 0))
    rows = clips * local * PAIRS
    return pl.pallas_call(
        functools.partial(token_grad_kernel, pack, local),
        grid_spec=pltpu.PrefetchScalarGridSpec(
            num_scalar_prefetch=1,
            grid=(clips, padded // tile),
            in_specs=[block, pl.BlockSpec((16, D), lambda i, j, m: (0, 0)), block, block]
            + [ANY] * len(pack.arrays),
            out_specs=ANY,
            scratch_shapes=[
                pltpu.VMEM((2, D, D), BF),
                pltpu.VMEM((rows + (padded - local) * PAIRS + 8, 128), F32),
                pltpu.SemaphoreType.DMA((2,)),
                pltpu.SemaphoreType.DMA((clips * TOKEN_TILES,)),
            ],
        ),
        out_shape=sds((rows, 128), F32),
        compiler_params=PARAMS,
        cost_estimate=cost(4 * clips * padded * D * D, clips * padded * D * 10),
        name="token_grad",
    )(meta, tokens, gb, dk, dv, *pack.arrays)


def fold_kernel(keep_ref, recv_ref, *out_refs):
    for k, ref in enumerate(out_refs):
        ref[...] = (keep_ref[k].astype(F32) + recv_ref[k].astype(F32)).astype(BF)


def row_block(rows):
    return rows // 2 if rows % 32 == 0 else rows


def fold(keep, recv):
    rows, lanes = keep.shape[1:]
    step = row_block(rows)
    block = pl.BlockSpec((4, step, lanes), lambda i: (0, i, 0))
    return pl.pallas_call(
        fold_kernel,
        grid=(rows // step,),
        in_specs=[block, block],
        out_specs=[pl.BlockSpec((step, lanes), lambda i: (i, 0))] * 4,
        out_shape=[sds((rows, lanes), BF)] * 4,
        compiler_params=PARAMS,
        name="fold",
    )(keep, recv)


def both(x, y):
    return (x.astype(F32) + y.astype(F32)).astype(BF)


def split_kernel(mine_p, recv_p, mine_q, recv_q, keep_p, keep_q, send_p, send_q):
    for at, k in enumerate((0, 2)):
        keep_p[at] = both(mine_p[k], recv_p[k])
        send_p[at] = both(mine_p[k + 1], recv_p[k + 1])
        keep_q[at] = both(mine_q[at], recv_q[at])
        send_q[at] = both(mine_q[at + 2], recv_q[at + 2])


def split(keep, recv):
    rows, lanes = keep.shape[1:]
    step = rows // 2 // STEPS
    first = pl.BlockSpec((4, step, lanes), lambda i: (0, i, 0))
    later = pl.BlockSpec((4, step, lanes), lambda i: (0, i + STEPS, 0))
    return pl.pallas_call(
        split_kernel,
        grid=(STEPS,),
        in_specs=[first, first, later, later],
        out_specs=[pl.BlockSpec((2, step, lanes), lambda i: (0, i, 0))] * 4,
        out_shape=[sds((2, rows // 2, lanes), BF)] * 4,
        compiler_params=PARAMS,
        name="split",
    )(keep, recv, keep, recv)


def turn_kernel(keep_p, keep_q, recv_p, recv_q, own_ref, send_p, send_q):
    for i, (keep, recv, send) in enumerate(((keep_p, recv_p, send_p), (keep_q, recv_q, send_q))):
        own_ref[i] = both(keep[0], recv[0])
        send[...] = both(keep[1], recv[1])


def turn(keep_p, keep_q, recv_p, recv_q):
    half, lanes = keep_p.shape[1:]
    step = half // STEPS
    pair = pl.BlockSpec((2, step, lanes), lambda i: (0, i, 0))
    one = pl.BlockSpec((step, lanes), lambda i: (i, 0))
    return pl.pallas_call(
        turn_kernel,
        grid=(STEPS,),
        in_specs=[pair] * 4,
        out_specs=[pair, one, one],
        out_shape=[sds((2, half, lanes), BF), sds((half, lanes), BF), sds((half, lanes), BF)],
        compiler_params=PARAMS,
        name="turn",
    )(keep_p, keep_q, recv_p, recv_q)


def join_kernel(own_ref, recv_p, recv_q, out_ref):
    out_ref[0] = both(own_ref[0], recv_p[...])
    out_ref[1] = both(own_ref[1], recv_q[...])


def join(own, recv_p, recv_q):
    half, lanes = recv_p.shape
    step = half // STEPS
    pair = pl.BlockSpec((2, step, lanes), lambda i: (0, i, 0))
    one = pl.BlockSpec((step, lanes), lambda i: (i, 0))
    return pl.pallas_call(
        join_kernel,
        grid=(STEPS,),
        in_specs=[pair, one, one],
        out_specs=pair,
        out_shape=sds((2, half, lanes), BF),
        compiler_params=PARAMS,
        cost_estimate=pl.CostEstimate(flops=0, bytes_accessed=20 * half * lanes, transcendentals=0),
        name="join",
    )(own, recv_p, recv_q).reshape(2 * half, lanes)


def sum_kernel(*refs):
    total = refs[0][...].astype(F32)
    for ref in refs[1:-1]:
        total = total + ref[...].astype(F32)
    refs[-1][...] = total.astype(BF)


def sum_of(parts):
    rows, lanes = parts[0].shape
    step = row_block(rows)
    block = pl.BlockSpec((step, lanes), lambda i: (i, 0))
    return pl.pallas_call(
        sum_kernel,
        grid=(rows // step,),
        in_specs=[block] * len(parts),
        out_specs=block,
        out_shape=sds((rows, lanes), BF),
        compiler_params=PARAMS,
        name="sum_parts",
    )(*parts)


def chunk_sums_kernel(meta, *refs):
    parts, outs = refs[:4], refs[4:]
    count = len(outs)
    step = outs[0].shape[0]
    for k, out in enumerate(outs):
        rows = pl.ds(pl.multiple_of(lax.rem(meta[1] + k, count) * step, step), step)
        total = parts[0][rows, :].astype(F32)
        for part in parts[1:]:
            total = total + part[rows, :].astype(F32)
        out[...] = total.astype(BF)


def chunk_sums(meta, parts, count=4):
    rows, lanes = parts[0].shape
    return pl.pallas_call(
        chunk_sums_kernel,
        in_specs=[pl.BlockSpec(memory_space=pltpu.SMEM)] + [WHOLE] * len(parts),
        out_specs=[WHOLE] * count,
        out_shape=[sds((rows // count, lanes), BF)] * count,
        compiler_params=PARAMS,
        name="chunk_sums",
    )(meta, *parts)


def after(x, *others):
    return lax.optimization_barrier((x, others))[0]


def exchange(x, bit):
    return lax.ppermute(x, "fsdp", [(i, i ^ bit) for i in range(OWNERS)])


def sum_over_fsdp(keep, send):
    full = jnp.stack([keep, send], 1).reshape(OWNERS, *keep.shape[1:])
    return lax.psum(full.astype(F32), "fsdp").astype(BF)


def finish_latent_kernel(count, meta, ma_ref, oa_ref, mb_ref, ob_ref, g1_ref, *refs):
    pieces, refs = refs[:count], refs[count:]
    lat_ref, qkv_ref, outw_ref, up_ref, down_ref, line_ref = refs
    s, h = meta[1], meta[2]
    step = pieces[0].shape[0]
    for k, piece in enumerate(pieces):
        rows = pl.ds(pl.multiple_of(lax.rem(s - k + count, count) * step, step), step)
        lat_ref[rows, :] = g1_ref[rows, :] + piece[...].astype(F32)
    for a_ref, b_ref, side in ((ma_ref, mb_ref, h), (oa_ref, ob_ref, 1 - h)):
        half = pl.ds(pl.multiple_of(side * HALF, 128), HALF)
        for layer, ref in ((1, a_ref), (0, b_ref)):
            for c in range(CHUNKS):
                at = pl.ds(pl.multiple_of(side * (FF // 2) + c * HALF, 128), HALF)
                up_ref[layer, :, at] = ref[c * SHARE : c * SHARE + SHARE, :].astype(F32)
            down_ref[layer, :, half] = ref[SPAN : 2 * SPAN, :].astype(F32)
        for i in range(4):
            first = ROWS_F + i * SHARE
            value = a_ref[first : first + SHARE, :].astype(F32)
            if i < 3:
                qkv_ref[0, i, :, half] = value
            else:
                outw_ref[1, :, half] = value
        outw_ref[0, :, half] = b_ref[2 * SPAN : 2 * SPAN + SHARE, :].astype(F32)
    last = ma_ref[2 * SPAN : ROWS_F, :].astype(F32)
    middle = ma_ref[ROWS_A - VEC_A : ROWS_A, :].astype(F32)
    first = mb_ref[ROWS_B - VEC_B : ROWS_B, :].astype(F32)
    line_ref[...] = jnp.zeros_like(line_ref)
    picks = [(first, 0), (middle, 0), (last, 0), (first, 1), (middle, 1), (last, 1), (first, 2), (last, 2)]
    picks += [(first, 3 + c) for c in range(CHUNKS)] + [(last, 3 + c) for c in range(CHUNKS)]
    for i, (vec, row) in enumerate(picks):
        for part in range(2):
            at = slice(part * HALF, part * HALF + HALF)
            line_ref[i : i + 1, at] = vec[2 * row + part : 2 * row + part + 1, :]


def finish_latent(meta, mine_f, other_f, mine_s, other_s, g1, pieces):
    rows = g1.shape[0]
    whole = lambda shape: pl.BlockSpec(shape, lambda i: (0,) * len(shape))
    return pl.pallas_call(
        functools.partial(finish_latent_kernel, len(pieces)),
        grid=(1,),
        in_specs=[pl.BlockSpec(memory_space=pltpu.SMEM)] + [WHOLE] * (5 + len(pieces)),
        out_specs=[
            whole((rows, D)),
            pl.BlockSpec((1, 3, SHARE, D), lambda i: (1, 0, 0, 0)),
            whole((2, SHARE, D)),
            whole((2, SHARE, FF)),
            whole((2, CHUNKS * SHARE, D)),
            whole((16, D)),
        ],
        out_shape=[
            sds((rows, D), F32),
            sds((2, 3, SHARE, D), F32),
            sds((2, SHARE, D), F32),
            sds((2, SHARE, FF), F32),
            sds((2, CHUNKS * SHARE, D), F32),
            sds((16, D), F32),
        ],
        compiler_params=PARAMS,
        name="finish_latent",
    )(meta, mine_f, other_f, mine_s, other_s, g1, *pieces)


def finish_token_kernel(count, meta, *refs):
    pieces, refs = refs[:count], refs[count:]
    w_ref, gain_ref, shift_ref, line_ref, qkv_in, qkv_ref, gain_out, shift_out, bin_out, bout_out, whole = refs
    f, s = meta[0], meta[1]
    step = pieces[0].shape[0]
    for k, piece in enumerate(pieces):
        rows = pl.ds(pl.multiple_of(lax.rem(s - k + count, count) * step, step), step)
        whole[rows, :] = piece[...].astype(F32)
    dk, dv, dq = (whole[i * SHARE : i * SHARE + SHARE, :] for i in range(3))
    qkv_ref[0, 0], qkv_ref[0, 1], qkv_ref[0, 2] = dq, dk, dv
    vec = whole[3 * SHARE : 3 * SHARE + 8, :]
    wk, wv = w_ref[0].astype(F32), w_ref[1].astype(F32)
    shift_sum = jnp.sum(wk * vec[0:1] + wv * vec[1:2], -1, keepdims=True)
    gain_sum = jnp.sum(wk * dk + wv * dv, -1, keepdims=True)
    lane = lax.broadcasted_iota(jnp.int32, (SHARE, 128), 1)
    turned = jnp.where(lane == 0, shift_sum, jnp.where(lane == 1, gain_sum, 0.0)).T
    db, total = turned[0:1, :SHARE], turned[1:2, :SHARE]
    dg = (total - shift_ref[1:2, :].astype(F32) * db) / gain_ref[1:2, :].astype(F32)
    lines = jnp.concatenate([line_ref[...], vec], 0)
    cut = pltpu.roll(lines, lax.rem(D - f * SHARE, D), 1)[:, :SHARE]
    gain_out[0:1, :], gain_out[1:2, :], gain_out[2:5, :] = cut[18:19], dg, cut[0:3]
    shift_out[0:1, :], shift_out[1:2, :], shift_out[2:5, :] = cut[19:20], db, cut[3:6]
    bout_out[...] = cut[6:8]
    wide = jnp.concatenate([line_ref[8 + c : 9 + c, :] for c in range(CHUNKS)], 1)
    other = jnp.concatenate([line_ref[12 + c : 13 + c, :] for c in range(CHUNKS)], 1)
    both = jnp.concatenate([wide, other], 0)
    span = CHUNKS * SHARE
    total = jnp.zeros((2, span), F32)
    for g in range(OWNERS):
        total = jnp.where(f == g, both[:, g * span : g * span + span], total)
    bin_out[...] = total


def finish_token(meta, pieces, weights, gain, shift, lines, qkv):
    whole = lambda shape: pl.BlockSpec(shape, lambda i: (0,) * len(shape))
    count = len(pieces)
    return pl.pallas_call(
        functools.partial(finish_token_kernel, count),
        grid=(1,),
        in_specs=[pl.BlockSpec(memory_space=pltpu.SMEM)] + [WHOLE] * (count + 4) + [ANY],
        out_specs=[
            pl.BlockSpec((1, 3, SHARE, D), lambda i: (0, 0, 0, 0)),
            whole((5, SHARE)),
            whole((5, SHARE)),
            whole((2, CHUNKS * SHARE)),
            whole((2, SHARE)),
        ],
        out_shape=[
            sds(qkv.shape, F32),
            sds((5, SHARE), F32),
            sds((5, SHARE), F32),
            sds((2, CHUNKS * SHARE), F32),
            sds((2, SHARE), F32),
        ],
        scratch_shapes=[pltpu.VMEM((ROWS_K, D), F32)],
        input_output_aliases={count + 5: 0},
        compiler_params=PARAMS,
        name="finish_token",
    )(meta, *pieces, weights, gain, shift, lines, qkv)


def unpack(left_a, right_a, left_b, right_b, whole_k):
    sides_a, sides_b = (left_a, right_a), (left_b, right_b)

    def up(sides):
        return jnp.concatenate(
            [x[c * SHARE : c * SHARE + SHARE] for x in sides for c in range(CHUNKS)], 1
        )

    def rows(sides, at, span=SHARE):
        return jnp.concatenate([x[at : at + span] for x in sides], 1)

    q1, k1, v1, out1 = (rows(sides_a, ROWS_F + i * SHARE) for i in range(4))
    out0 = rows(sides_b, 2 * SPAN)
    k0, v0, q0 = (whole_k[i * SHARE : i * SHARE + SHARE] for i in range(3))
    return (
        jnp.stack([jnp.stack([q0, k0, v0]), jnp.stack([q1, k1, v1])]).astype(F32),
        jnp.stack([out0, out1]).astype(F32),
        jnp.stack([up(sides_b), up(sides_a)]).astype(F32),
        jnp.stack([rows(sides_b, SPAN, SPAN), rows(sides_a, SPAN, SPAN)]).astype(F32),
    )


def per_device(size, seq, *args):
    (
        latents_in,
        inputs,
        clip_frames,
        text_mask,
        qkv_weight,
        out_weight,
        mlp_in,
        mlp_out,
        norm_gain,
        norm_bias,
        bias_in,
        bias_out,
        out_cotangent,
    ) = args
    micro, clips, nlat, _ = latents_in.shape
    count = micro * clips
    local = inputs.shape[2]
    padded = -(-local // 128) * 128
    rows = count * nlat
    s = lax.axis_index("seq")
    fsdp = lax.axis_index("fsdp")
    special = size == OWNERS
    meta = jnp.stack([fsdp if special else jnp.int32(0), s, s % 2]).astype(jnp.int32)
    lat = latents_in.reshape(rows, D)
    tokens = inputs.reshape(count, local, D)
    g4 = out_cotangent.reshape(rows, D)

    place = s * local + jnp.arange(padded, dtype=jnp.int32)
    frames = clip_frames.reshape(count, 1) * PATCHES
    text = text_mask.reshape(count, -1) > 0
    text_len = text.shape[1]
    slots = FRAMES * PATCHES
    wide = jnp.pad(text, ((0, 0), (slots, padded)))
    text_here = lax.dynamic_slice_in_dim(wide, s * local, padded, 1)
    valid = jnp.where(place[None] < slots, place[None] < frames, text_here)
    valid = valid & (jnp.arange(padded)[None] < local)
    bias = jnp.where(valid, 0.0, -1e30).astype(F32)
    mask = jnp.broadcast_to(bias[:, :, None], (count, padded, 128))

    def slabs(up):
        return up.reshape(SHARE, CHUNKS, D).transpose(1, 0, 2).reshape(SPAN, D)

    def pack_keyval(qkv, out, up, down, gain, shift, up_b, down_b):
        small = jnp.concatenate(
            [
                jnp.pad(jnp.concatenate([gain, shift, down_b], 0), ((0, 0), (0, 128 - SHARE))),
                up_b.reshape(6, 128),
                jnp.zeros((14, 128), BF),
            ],
            0,
        )
        small = jnp.concatenate([small[:16], small[16:]], 1)
        small = jnp.pad(small, ((0, 0), (0, D - 256)))
        return jnp.concatenate([qkv[0].reshape(3 * SHARE, D), small], 0)

    def pack_first(qkv, out, up, down, *rest):
        return jnp.concatenate([out[0], slabs(up[0]), down[0]], 0)

    def pack_last(qkv, out, up, down, *rest):
        return jnp.concatenate([qkv[1].reshape(3 * SHARE, D), out[1], slabs(up[1]), down[1]], 0)

    packers = (pack_keyval, pack_first, pack_last)
    weights = (qkv_weight, out_weight, mlp_in, mlp_out, norm_gain, norm_bias, bias_in, bias_out)
    axes = (2, 1, 1, 1, 1, 1, 1, 1)
    def shift_to(x, k):
        return lax.ppermute(x, "seq", [(i, (i + k) % seq) for i in range(seq)])

    def scatter_rows(x):
        step = x.shape[0] // seq
        out = []
        for k in range(1, seq):
            piece = lax.dynamic_slice_in_dim(x, ((s + k) % seq) * step, step, 0)
            out.append(shift_to(piece, k))
        return out

    def gather_rows(x):
        return [x] + [shift_to(x, k) for k in range(1, seq)]

    pair = [(i, i ^ 1) for i in range(seq)]

    if special:
        def direct(x):
            return {0: x, 2: exchange(x, 2), 4: exchange(x, 4), 6: exchange(x, 6)}

        def direct_pack(p, later):
            arrays = [p[m] if m % 2 == 0 else exchange(later(p[m - 1]), 1) for m in range(OWNERS)]
            return Pack(arrays, lambda m, row: (m, None, row))

        def relay_pack(parts):
            half = parts[3].shape[0]
            arrays = []
            for x in parts:
                arrays += [x, exchange(x, 1)]

            def where(m, row):
                if m < 6:
                    return (m, None, row)
                return (m, None, row) if row < half else (m + 2, None, row - half)

            return Pack(arrays, where)

        x1 = pack_keyval(*weights)
        p1 = direct(x1)
        x3 = pack_last(*after(weights, x1))
        x3_2, x3_4 = exchange(x3, 2), exchange(x3, 4)
        tokens = with_layout_constraint(tokens, Layout(major_to_minor=(0, 1, 2)))
        bias, tokens = after((bias, tokens), x3)
        g1 = direct_pack(p1, lambda x: after(x, p1[2], tokens))
        xl, k, v, gb, bins = keyval(g1, meta, tokens, local, padded)
        mask = after(bias, k)
        mask = jnp.broadcast_to(mask[:, :, None], (count, padded, 128))
        pay, q = attend(g1, meta, lat, gb, bias[:, None, :], k, v)
        pay = pay.reshape(rows, PAY)
        arrived = scatter_rows(pay)
        x2 = pack_first(*after(weights, k))
        x3_2, x3_4, x2 = after((x3_2, x3_4, x2), pay)
        half = x3.shape[0] // 2
        turn_2, turn_4 = x3_2[:half], x3_4[half:]
        x2_2, x2_4 = exchange(x2, 2), exchange(x2, 4)
        share = combine(meta, after(pay, mask), arrived)
        parts = gather_rows(share)
        turn_2, turn_4, x2_2, x2_4 = after((turn_2, turn_4, x2_2, x2_4), parts)
        half = SHARE + SPAN
        x2_6a, x2_6b = exchange(x2_2[:half], 4), exchange(x2_4[half:], 2)
        x3_6a, x3_6b = exchange(turn_2, 4), exchange(turn_4, 2)
        g2 = relay_pack([x2, *after((x2_2, x2_4), x2_6a, x2_6b), x2_6a, x2_6b])
        o, l, z1, z2, hidden = first_block(g2, meta, parts, lat, gb, bins)
        x3_6a, x3_6b = after((x3_6a, x3_6b), z2)
        g34 = relay_pack([x3, x3_2, x3_4, x3_6a, x3_6b])
    else:
        full = []
        for w, axis in zip(weights, axes):
            whole = lax.all_gather(w, "fsdp", axis=axis, tiled=True)
            shape = whole.shape
            parts = whole.reshape(*shape[:axis], OWNERS, shape[axis] // OWNERS, *shape[axis + 1 :])
            full.append(jnp.moveaxis(parts, axis, 0))
        raw = [jax.vmap(packer)(*full) for packer in packers]
        g1, g2, g34 = [Pack([x], lambda m, row: (0, m, row)) for x in raw]
        xl, k, v, gb, bins = keyval(g1, meta, tokens, local, padded)
        pay, q = attend(g1, meta, lat, gb, bias[:, None, :], k, v)
        pay = pay.reshape(rows, PAY)
        share = combine(meta, pay, scatter_rows(pay))
        o, l, z1, z2, hidden = first_block(g2, meta, gather_rows(share), lat, gb, bins)
    out, g2_lat, keep_a, send_a = second_block(g34, meta, z2, g4, gb, bins)

    grad_one, du, dl, keep_b, send_b = fourth_block(g2, meta, g2_lat, z1, o, l, gb, hidden)
    cube = lambda x: x.reshape(count, nlat, x.shape[-1])
    shapes = (latents_in.shape, inputs.shape)
    if special:
        recv_a, recv_b = exchange(send_a, 1), exchange(send_b, 1)
        split_a = split(*after((keep_a, recv_a), du))
        split_b = split(*after((keep_b, recv_b), *split_a))
        du, dl = after((du, dl), *split_a, *split_b)
        dk, dv, dq = attend_back(cube(q), cube(du), cube(dl), mask, k, v)
        dq = dq.reshape(rows, D)
        first_a = (*split_a[:2], exchange(split_a[2], 2), exchange(split_a[3], 4))
        first_b = (*split_b[:2], exchange(split_b[2], 2), exchange(split_b[3], 4))
        turn_a = turn(*after(first_a, dq))
        second_a = (turn_a[0], exchange(turn_a[1], 4), exchange(turn_a[2], 2))
        keep_k, send_k, sums = keyval_grad(meta, *after((xl, dk, dv), *turn_a))
        dq = after(dq, sums)
        dq_parts = scatter_rows(dq)
        turn_b = turn(*after(first_b, sums))
        second_b = (turn_b[0], exchange(turn_b[1], 4), exchange(turn_b[2], 2))
        mine_a = join(*after(second_a, *turn_b))
        mine_b = join(*after(second_b, mine_a))
        dq, dq_parts = after((dq, dq_parts), mine_b)
        back, keep_k, send_k = query_grad(g1, meta, dq, dq_parts, lat, gb, sums, keep_k, send_k)
        recv_k = exchange(send_k, 1)
        fold_k = fold(keep_k, recv_k)
        other_a = lax.ppermute(mine_a, "seq", pair)
        other_b = lax.ppermute(mine_b, "seq", pair)
        hop_k = [exchange(x, 2 * i) for i, x in enumerate(fold_k) if i]
        token_grads = token_grad(g1, meta, tokens, gb, *after((dk, dv), mine_a, mine_b, *fold_k))
        mine_k = chunk_sums(meta, after([fold_k[0]] + hop_k, token_grads), seq)
        back_rows = gather_rows(after(back, *mine_k))
        sent = [shift_to(x, i) for i, x in enumerate(mine_k) if i]
        pieces = gather_rows(sum_of([mine_k[0]] + sent))
        lat_grad, qkv_grad, outw_grad, up_grad, down_grad, lines = finish_latent(
            meta, mine_a, other_a, mine_b, other_b, grad_one, back_rows
        )
        qkv_grad, gain_grad, shift_grad, bin_grad, bout_grad = finish_token(
            meta, pieces, qkv_weight[0, 1:3], norm_gain, norm_bias, lines, qkv_grad
        )
        return (
            out.reshape(shapes[0]),
            lat_grad.reshape(shapes[0]),
            token_grads.reshape(shapes[1]),
            qkv_grad,
            outw_grad,
            up_grad,
            down_grad,
            gain_grad,
            shift_grad,
            bin_grad,
            bout_grad,
        )

    dk, dv, dq = attend_back(cube(q), cube(du), cube(dl), mask, k, v)
    dq = dq.reshape(rows, D)
    keep_k, send_k, sums = keyval_grad(meta, xl, dk, dv)
    back, keep_k, send_k = query_grad(g1, meta, dq, scatter_rows(dq), lat, gb, sums, keep_k, send_k)
    token_grads = token_grad(g1, meta, tokens, gb, dk, dv)
    lat_grad = grad_one + place_rows(gather_rows(back), s, seq)
    mine_a, mine_b, mine_k = (
        sum_over_fsdp(*x) for x in ((keep_a, send_a), (keep_b, send_b), (keep_k, send_k))
    )

    def sides(mine):
        other = lax.ppermute(mine, "seq", pair)
        return jnp.where(s % 2 == 0, mine, other), jnp.where(s % 2 == 0, other, mine)

    whole_k = lax.psum(mine_k.astype(F32), "seq")
    shares = (*sides(mine_a), *sides(mine_b), whole_k)
    wide = jax.vmap(unpack)(*shares)
    grads = []
    for x, w, axis in zip(wide, weights, axes):
        x = jnp.moveaxis(x, 0, axis)
        x = x.reshape(*x.shape[:axis], -1, *x.shape[axis + 2 :])
        grads.append(lax.dynamic_slice_in_dim(x, fsdp * w.shape[axis], w.shape[axis], axis))
    last = shares[0][0, 2 * SPAN : ROWS_F].astype(F32).reshape(-1, D)
    middle = shares[0][0, -VEC_A:].astype(F32).reshape(-1, D)
    early = shares[2][0, -VEC_B:].astype(F32).reshape(-1, D)
    vec_k = whole_k[0][-VEC_K:]
    step = norm_gain.shape[1]
    k0, v0 = grads[0][0, 1], grads[0][0, 2]
    own_k, own_v = qkv_weight[0, 1].astype(F32), qkv_weight[0, 2].astype(F32)
    own_gain, own_shift = norm_gain[1].astype(F32), norm_bias[1].astype(F32)
    db1 = jnp.sum(own_k * vec_k[0] + own_v * vec_k[1], -1)
    dg1 = (jnp.sum(own_k * k0 + own_v * v0, -1) - own_shift * db1) / own_gain
    lines = [vec_k[2], early[0], middle[0], last[0], vec_k[3], early[1], middle[1], last[1], early[2], last[2]]
    lines = jnp.stack(lines)
    cut = lax.dynamic_slice_in_dim(lines, fsdp * step, step, 1)
    wide_bias = jnp.stack([early[3:7].reshape(FF), last[3:7].reshape(FF)])
    return (
        out.reshape(shapes[0]),
        lat_grad.reshape(shapes[0]),
        token_grads.reshape(shapes[1]),
        *grads,
        jnp.stack([cut[0], dg1, cut[1], cut[2], cut[3]]),
        jnp.stack([cut[4], db1, cut[5], cut[6], cut[7]]),
        lax.dynamic_slice_in_dim(wide_bias, fsdp * bias_in.shape[1], bias_in.shape[1], 1),
        cut[8:10],
    )


def place_rows(pieces, s, seq):
    step = pieces[0].shape[0]
    whole = jnp.zeros((seq * step, *pieces[0].shape[1:]), F32)
    for k, piece in enumerate(pieces):
        at = ((s - k) % seq) * step
        whole = lax.dynamic_update_slice_in_dim(whole, piece.astype(F32), at, 0)
    return whole


def solution(mesh):
    in_specs = (
        P(None, "fsdp", None, None),
        P(None, "fsdp", "seq", None),
        P(None, "fsdp"),
        P(None, "fsdp", None),
        P(None, None, "fsdp", None),
        P(None, "fsdp", None),
        P(None, "fsdp", None),
        P(None, "fsdp", None),
        P(None, "fsdp"),
        P(None, "fsdp"),
        P(None, "fsdp"),
        P(None, "fsdp"),
        P(None, "fsdp", None, None),
    )
    out_specs = (
        P(None, "fsdp", None, None),
        P(None, "fsdp", None, None),
        P(None, "fsdp", "seq", None),
        P(None, None, "fsdp", None),
        P(None, "fsdp", None),
        P(None, "fsdp", None),
        P(None, "fsdp", None),
        P(None, "fsdp"),
        P(None, "fsdp"),
        P(None, "fsdp"),
        P(None, "fsdp"),
    )
    step = functools.partial(per_device, mesh.shape["fsdp"], mesh.shape["seq"])
    return jax.shard_map(step, mesh=mesh, in_specs=in_specs, out_specs=out_specs, check_vma=False)
```
